128 devices in a mesh: lat: 8 (over z, core), lon: 16 (over x, y).
Axes of the slice: x: 4, y: 4, z: 4, core: 2. Of those that a mesh axis runs over, the one named last changes fastest.
Arguments:
- latents: bfloat16 [128, 256, 256], P('lat', 'lon'), may hold values from -6 to 6
- conv_weight: bfloat16 [9, 256, 256], replicated, may hold values from -0.125 to 0.125
- map_weight: bfloat16 [256, 1024], replicated, may hold values from -0.375 to 0.375
- map_bias: float32 [1024], replicated, may hold values from -6 to 6
- input_weight: float32 [3, 512], replicated, may hold values from -3.5 to 3.5
- hidden_weight: bfloat16 [1, 512, 512], replicated, may hold values from -0.25 to 0.25
- output_weight: float32 [512], replicated, may hold values from -0.25 to 0.25
- hit_owner: int32 [12288], P(('lat', 'lon')), may hold values from 0 to 127, as said below
- serve_block: int32 [128, 128], P(('lat', 'lon')), may hold values from -1 to 1, as said below
- query_grid: int32 [3, 786432], P(None, ('lat', 'lon')), may hold values from 0 to 127, as said below
- cotangent: float32 [786432], P(('lat', 'lon')), may hold values from -6 to 6
Outputs:
- latent_grad: float32 [128, 256, 256], P('lat', 'lon')
- conv_grad: float32 [9, 256, 256], replicated
- map_grad: float32 [256, 1024], replicated
- map_bias_grad: float32 [1024], replicated
- input_grad: float32 [3, 512], replicated
- hidden_grad: float32 [1, 512, 512], replicated
- output_grad: float32 [512], replicated
The draws below stay inside these ranges and needn't reach their ends.
Inputs may be any that keep to these rules, and one draw needn't show every extreme that they name: `hit_owner`: each device's 96 entries name distinct devices, numbered lat index times the size of lon plus lon index. `serve_block`: entry [o, r] is a block of device o, 0 to 1, when the list of device r names o, and -1 otherwise. `query_grid`: row 0 is the cell within the block (row-major over 8 rows of 16 cells), row 1 the sub-cell (0 to 35, row-major), row 2 the level (0 to 36).
All inputs are finite; a program needn't handle non-finite values.
Results may differ from the reference program's by a relative error of at most 0.0095.
Values may be sent and summed in bfloat16 or wider, within the bound.
A program may use at most 128 MiB of HBM per device.

```python
import math
import jax
import jax.numpy as jnp
from jax import lax

C = 256
WIDTH = 512
MODLAYERS = 2
BLOCK = 128
LEVELS = 37
SUB = 6
LAT_DEV = 16
LON_DEV = 16
GROUP = 64
BLK_DEV = 2
HITS = 96
NLAT = 128
NLON = 256
QUERIES = 786432
N_LAT = 8
N_LON = 16


def owner_table(key):
    device_total = N_LAT * N_LON
    base_score = jax.random.randint(jax.random.fold_in(key, 11), (device_total, device_total), 0, 2 ** 20)
    heat = jax.random.randint(jax.random.fold_in(key, 12), (device_total,), 0, 4) * 2 ** 19
    score = (base_score + heat[None, :]) * device_total + jnp.arange(device_total, dtype=jnp.int32)[None, :]
    _, owners = lax.top_k(score, HITS)
    return owners.astype(jnp.int32)


def draw_hit_owner(key, part):
    return owner_table(key).reshape(-1)


def draw_serve_block(key, part):
    device_total = N_LAT * N_LON
    owners = owner_table(key)
    member = jnp.zeros((device_total, device_total), jnp.int32).at[jnp.arange(device_total)[:, None], owners].set(1)
    picked = jax.random.randint(jax.random.fold_in(key, 13), (device_total, device_total), 0, BLK_DEV)
    return jnp.where(member.T == 1, picked, -1).astype(jnp.int32)


def draw_query_grid(key, part):
    total = N_LAT * N_LON * HITS * GROUP
    cell_index = jax.random.randint(jax.random.fold_in(key, 21), (total,), 0, BLOCK)
    sub_index = jax.random.randint(jax.random.fold_in(key, 22), (total,), 0, SUB * SUB)
    level_index = jax.random.randint(jax.random.fold_in(key, 23), (total,), 0, LEVELS)
    return jnp.stack([cell_index, sub_index, level_index]).astype(jnp.int32)


def block_levels(key, extent, cuts, smallest, top_value):
    def one(axis_at, blocks):
        steps = jax.random.uniform(jax.random.fold_in(jax.random.fold_in(key, 6), axis_at), (blocks,), jnp.float32, smallest / len(cuts), top_value / len(cuts))
        return jnp.repeat(jnp.exp(steps), extent[axis_at] // blocks).reshape((-1,) + (1,) * (len(extent) - axis_at - 1))

    loudness = one(*cuts[0])
    for cut in cuts[1:]:
        loudness = loudness * one(*cut)
    return loudness


def normal_values(stream_key, dims, spread, limit, shards=(), held_as=jnp.bfloat16):
    gain = block_levels(stream_key, dims, shards, -0.22, 0.18) if shards else 1.0
    drawn = jax.random.normal(stream_key, dims, jnp.float32) * spread * gain
    return jnp.minimum(jnp.maximum(drawn, -limit), limit).astype(held_as)


def setup_inputs(seed: int = 0) -> dict:
    keys = jax.random.split(jax.random.key(seed), 12)
    latents = normal_values(keys[0], (NLAT, NLON, C), 1.0, 6.0, ((0, 8), (1, 16)))
    conv_weight = normal_values(keys[1], (9, C, C), (9 * C) ** -0.5, 0.125)
    map_weight = normal_values(keys[2], (C, MODLAYERS * WIDTH), C ** -0.5, 0.375)
    map_bias = normal_values(keys[3], (MODLAYERS * WIDTH,), 1.0, 6.0, (), jnp.float32)
    input_weight = normal_values(keys[4], (3, WIDTH), 3 ** -0.5, 3.5, (), jnp.float32)
    hidden_weight = normal_values(keys[5], (MODLAYERS - 1, WIDTH, WIDTH), WIDTH ** -0.5, 0.25)
    output_weight = normal_values(keys[6], (WIDTH,), WIDTH ** -0.5, 0.25, (), jnp.float32)
    hit_owner = draw_hit_owner(jax.random.fold_in(keys[11], 71), 0)
    serve_block = draw_serve_block(jax.random.fold_in(keys[11], 71), 0)
    query_grid = draw_query_grid(jax.random.fold_in(keys[11], 71), 0)
    cotangent = normal_values(keys[10], (QUERIES,), 1.0, 6.0, ((0, 128),), jnp.float32)
    return dict(latents=latents, conv_weight=conv_weight, map_weight=map_weight, map_bias=map_bias, input_weight=input_weight, hidden_weight=hidden_weight, output_weight=output_weight, hit_owner=hit_owner, serve_block=serve_block, query_grid=query_grid, cotangent=cotangent)


OMEGA = 30.0

def conv_apply(padded, kernel, row_count, col_count, flipped):
    channels = padded.shape[-1]
    result = jnp.zeros((row_count * col_count, kernel.shape[-1]), jnp.float32)
    for shift_a in (-1, 0, 1):
        for shift_b in (-1, 0, 1):
            tap_index = (shift_a + 1) * 3 + shift_b + 1
            if flipped:
                window = padded[1 - shift_a:1 - shift_a + row_count, 1 - shift_b:1 - shift_b + col_count]
                matrix = kernel[tap_index].T
            else:
                window = padded[1 + shift_a:1 + shift_a + row_count, 1 + shift_b:1 + shift_b + col_count]
                matrix = kernel[tap_index]
            result = result + jnp.dot(window.reshape(row_count * col_count, channels), matrix, preferred_element_type=jnp.float32)
    return result

def conv_weight_grad(padded, grads, row_count, col_count):
    flat_grads = grads.reshape(row_count * col_count, -1)
    pieces = []
    for shift_a in (-1, 0, 1):
        for shift_b in (-1, 0, 1):
            window = padded[1 + shift_a:1 + shift_a + row_count, 1 + shift_b:1 + shift_b + col_count]
            window = window.reshape(row_count * col_count, -1)
            pieces.append(jnp.dot(window.T, flat_grads, preferred_element_type=jnp.float32))
    return jnp.stack(pieces)

def wrap_pad(source):
    extended = jnp.concatenate([source[:, -1:], source, source[:, :1]], axis=1)
    return jnp.pad(extended, ((1, 1), (0, 0), (0, 0)))

def query_coords(cell_index, sub_index, level_index, lat_base, lon_base, lon_tile, lat_cells, lon_cells):
    row_index = lat_base[:, None] + cell_index // lon_tile
    col_index = lon_base[:, None] + cell_index % lon_tile
    lat_coord = ((row_index * SUB + sub_index // SUB).astype(jnp.float32) + 0.5) / (lat_cells * SUB) * 2.0 - 1.0
    lon_coord = ((col_index * SUB + sub_index % SUB).astype(jnp.float32) + 0.5) / (lon_cells * SUB) * 2.0 - 1.0
    level_coord = (level_index.astype(jnp.float32) + 0.5) / LEVELS * 2.0 - 1.0
    return jnp.stack([lat_coord.reshape(-1), lon_coord.reshape(-1), level_coord.reshape(-1)])

def sine_grads(features, coords, cotan_rows, map_weight, map_bias, input_weight, hidden_weight, output_weight):
    hidden_size = input_weight.shape[1]
    depth_count = map_weight.shape[1] // hidden_size
    shifts = jnp.dot(features, map_weight, preferred_element_type=jnp.float32) + map_bias
    linear = coords[0][:, None] * input_weight[0] + coords[1][:, None] * input_weight[1] + coords[2][:, None] * input_weight[2]
    preacts = [OMEGA * linear + shifts[:, :hidden_size]]
    inputs_rounded = []
    for layer_index in range(1, depth_count):
        previous = jnp.sin(preacts[-1]).astype(jnp.bfloat16)
        inputs_rounded.append(previous)
        preacts.append(jnp.dot(previous, hidden_weight[layer_index - 1], preferred_element_type=jnp.float32) + shifts[:, layer_index * hidden_size:(layer_index + 1) * hidden_size])
    last_act = jnp.sin(preacts[-1])
    output_grad = jnp.dot(cotan_rows, last_act, precision=lax.Precision.HIGHEST)
    act_grad = cotan_rows[:, None] * output_weight[None, :]
    pre_grads = [None] * depth_count
    rounded_grads = [None] * depth_count
    hidden_grads = [None] * (depth_count - 1)
    for layer_index in range(depth_count - 1, -1, -1):
        pre_grads[layer_index] = act_grad * jnp.cos(preacts[layer_index])
        rounded_grads[layer_index] = pre_grads[layer_index].astype(jnp.bfloat16)
        if layer_index > 0:
            hidden_grads[layer_index - 1] = jnp.dot(inputs_rounded[layer_index - 1].T, rounded_grads[layer_index], preferred_element_type=jnp.float32)
            act_grad = jnp.dot(rounded_grads[layer_index], hidden_weight[layer_index - 1].T, preferred_element_type=jnp.float32)
    input_grad = OMEGA * jnp.dot(coords, pre_grads[0], precision=lax.Precision.HIGHEST)
    mod_grads = jnp.concatenate(rounded_grads, axis=1)
    bias_grad = lax.optimization_barrier(jnp.sum(jnp.concatenate(pre_grads, axis=1), axis=0))
    map_grad = jnp.dot(features.T, mod_grads, preferred_element_type=jnp.float32)
    feature_grads = jnp.dot(mod_grads, map_weight.T, preferred_element_type=jnp.float32)
    return (feature_grads, (map_grad, bias_grad, input_grad, jnp.stack(hidden_grads), output_grad))

def reference(latents, conv_weight, map_weight, map_bias, input_weight, hidden_weight, output_weight, hit_owner, serve_block, query_grid, cotangent):
    dev_count = N_LAT * N_LON
    padded = wrap_pad(latents)
    features = conv_apply(padded, conv_weight, NLAT, NLON, False).astype(jnp.bfloat16).reshape(NLAT, NLON, C)
    blocks = features.reshape(N_LAT, LAT_DEV, N_LON, LON_DEV, C).transpose(0, 2, 1, 3, 4).reshape(dev_count, BLK_DEV, BLOCK, C)
    owners = hit_owner.reshape(dev_count, HITS)
    query_rows = query_grid.reshape(3, dev_count, HITS, GROUP)
    cotan_all = cotangent.reshape(dev_count, HITS, GROUP)
    weights = (map_weight, map_bias, input_weight, hidden_weight, output_weight)
    zero_grads = (jnp.zeros((C, MODLAYERS * WIDTH), jnp.float32), jnp.zeros((MODLAYERS * WIDTH,), jnp.float32), jnp.zeros((3, WIDTH), jnp.float32), jnp.zeros((MODLAYERS - 1, WIDTH, WIDTH), jnp.float32), jnp.zeros((WIDTH,), jnp.float32))
    initial = (jnp.zeros((dev_count, BLK_DEV, BLOCK, C), jnp.float32), zero_grads)

    def visit(state_pair, device):
        block_sums, grad_totals = state_pair
        owner_row = owners[device]
        block_pick = serve_block[owner_row, device]
        hit_blocks = blocks[owner_row, block_pick]
        cell_index = query_rows[0, device]
        sub_index = query_rows[1, device]
        level_index = query_rows[2, device]
        features_q = jnp.take_along_axis(hit_blocks, cell_index[:, :, None], axis=1).reshape(HITS * GROUP, C)
        lat_base = owner_row // N_LON * LAT_DEV + block_pick * (BLOCK // LON_DEV)
        lon_base = owner_row % N_LON * LON_DEV
        coords = query_coords(cell_index, sub_index, level_index, lat_base, lon_base, LON_DEV, NLAT, NLON)
        feature_grads, grads = sine_grads(features_q, coords, cotan_all[device].reshape(-1), weights[0], weights[1], weights[2], weights[3], weights[4])
        hit_grads = jnp.zeros((HITS, BLOCK, C), jnp.float32).at[jnp.arange(HITS)[:, None], cell_index].add(feature_grads.reshape(HITS, GROUP, C))
        block_sums = block_sums.at[owner_row, block_pick].add(hit_grads)
        grad_totals = jax.tree.map(jnp.add, grad_totals, grads)
        return ((block_sums, grad_totals), None)
    (block_sums, grad_totals), _ = lax.scan(visit, initial, jnp.arange(dev_count, dtype=jnp.int32))
    feature_grad = block_sums.reshape(N_LAT, N_LON, LAT_DEV, LON_DEV, C).transpose(0, 2, 1, 3, 4).reshape(NLAT, NLON, C).astype(jnp.bfloat16)
    padded_grad = wrap_pad(feature_grad)
    latent_grad = conv_apply(padded_grad, conv_weight, NLAT, NLON, True).reshape(NLAT, NLON, C)
    conv_grad = conv_weight_grad(padded, feature_grad, NLAT, NLON)
    grad_scale = 1.0 / math.sqrt(QUERIES)
    return (latent_grad, conv_grad * grad_scale, grad_totals[0] * grad_scale, grad_totals[1] * grad_scale, grad_totals[2] * grad_scale, grad_totals[3] * grad_scale, grad_totals[4] * grad_scale)
```

```python
import functools
import math

import jax
import jax.numpy as jnp
import numpy as np
from jax import lax
from jax.experimental import pallas as pl
from jax.experimental.pallas import tpu as pltpu
from jax.sharding import PartitionSpec as P

BLOCK = 128
LEVELS = 37
SUB = 6
OMEGA = 30.0
INV_TURN = float(1.0 / (2.0 * math.pi))
TURN = float(2.0 * math.pi)
TILE = 512
ROWS = 32


def _fit():
    nodes = np.cos((2 * np.arange(400) + 1) * np.pi / 800)
    r = (nodes + 1) / 4
    z = r * r
    sine = np.sqrt(2.0) * np.sin(np.pi * r)
    cosine = np.sqrt(2.0) * np.cos(np.pi * r)
    sa = np.stack([r * z**k for k in range(4)], 1)
    ca = np.stack([z**k for k in range(5)], 1)
    return (
        [float(v) for v in np.linalg.lstsq(sa, sine, rcond=None)[0]],
        [float(v) for v in np.linalg.lstsq(ca, cosine, rcond=None)[0]],
    )


SIN_C, COS_C = _fit()


def sincos_turns(t):
    r = t - jnp.round(t)
    z = r * r
    s = r * (SIN_C[0] + z * (SIN_C[1] + z * (SIN_C[2] + z * SIN_C[3])))
    c = COS_C[0] + z * (COS_C[1] + z * (COS_C[2] + z * (COS_C[3] + z * COS_C[4])))
    return s * c, 1.0 - s * s


def dot(a, b):
    return jnp.dot(a, b, preferred_element_type=jnp.float32)


def dot_nt(a, b):
    return lax.dot_general(a, b, (((1,), (1,)), ((), ())), preferred_element_type=jnp.float32)


def dot_tn(a, b):
    return lax.dot_general(a, b, (((0,), (0,)), ((), ())), preferred_element_type=jnp.float32)


def split2(v):
    hi = v.astype(jnp.bfloat16)
    return hi, (v - hi.astype(jnp.float32)).astype(jnp.bfloat16)


def split3(v):
    hi = v.astype(jnp.bfloat16).astype(jnp.float32)
    mid = (v - hi).astype(jnp.bfloat16).astype(jnp.float32)
    return hi, mid, v - hi - mid


def shifted(center, top, bottom, left, right):
    rows, cols, ch = center.shape
    total = (rows + 2) * cols
    mid = jnp.concatenate([top, center.reshape(rows * cols, ch), bottom], axis=0)
    mid32 = mid.astype(jnp.float32)
    col = lax.broadcasted_iota(jnp.int32, (rows + 2, cols, ch), 1)
    low = pltpu.roll(mid32, 1, 0).reshape(rows + 2, cols, ch)
    high = pltpu.roll(mid32, total - 1, 0).reshape(rows + 2, cols, ch)
    low = jnp.where(col == 0, left.astype(jnp.float32)[:, None, :], low)
    high = jnp.where(col == cols - 1, right.astype(jnp.float32)[:, None, :], high)
    return (
        low.reshape(total, ch).astype(jnp.bfloat16),
        mid,
        high.reshape(total, ch).astype(jnp.bfloat16),
    )


def main_kernel(
    dims,
    base_ref,
    q_ref,
    center_ref,
    top_ref,
    bottom_ref,
    left_ref,
    right_ref,
    convw_ref,
    mapw_ref,
    mapb_ref,
    inw_ref,
    hid_ref,
    outw_ref,
    fg_ref,
    conv_ref,
    map_ref,
    hidg_ref,
    small_ref,
    x3_ref,
    feat_ref,
    tab0_ref,
    tab1_ref,
    wcol_ref,
    rhs_ref,
    t_ref,
    c0_ref,
    d_ref,
    g_ref,
    og_ref,
):
    lat_cells, lon_cells = dims
    rows, cols, ch = center_ref.shape
    cells = rows * cols
    width = inw_ref.shape[1]
    tile = rhs_ref.shape[1]
    tiles = q_ref.shape[1] // tile
    f32 = jnp.float32
    bf16 = jnp.bfloat16

    x3 = shifted(center_ref[...], top_ref[...], bottom_ref[...], left_ref[...], right_ref[...])
    for b in range(3):
        x3_ref[:, b * ch : (b + 1) * ch] = x3[b]
    acc = dot(x3_ref[0:cells, :], convw_ref[0])
    for a in (1, 2):
        acc += dot(x3_ref[a * cols : a * cols + cells, :], convw_ref[a])
    feat_ref[...] = acc.astype(bf16)

    shift = dot(feat_ref[...], mapw_ref[...]) + mapb_ref[...]
    cell = lax.broadcasted_iota(jnp.int32, (cells, width), 0)
    row_f = (cell // cols).astype(f32)
    col_f = (cell % cols).astype(f32)
    lat_c = ((base_ref[0] + row_f) * SUB + 0.5) * (2.0 / (lat_cells * SUB)) - 1.0
    lon_c = ((base_ref[1] + col_f) * SUB + 0.5) * (2.0 / (lon_cells * SUB)) - 1.0
    lev_c = 1.0 / LEVELS - 1.0
    linear = (
        lat_c * inw_ref[0:1, :] + lon_c * inw_ref[1:2, :] + lev_c * inw_ref[2:3, :]
    )
    turn0 = (OMEGA * linear + shift[:, :width]) * INV_TURN
    turn0 = turn0 - jnp.round(turn0)
    hi, lo = split2(turn0.T)
    tab0_ref[:, 0:cells] = hi
    tab0_ref[:, cells : 2 * cells] = lo
    turn1 = shift[:, width:] * INV_TURN
    turn1 = (turn1 - jnp.round(turn1)) * TURN
    hi, lo = split2(turn1.T)
    tab1_ref[:, width : width + cells] = hi
    tab1_ref[:, width + cells : width + 2 * cells] = lo
    tab1_ref[:, 0:width] = hid_ref[...].astype(f32).T.astype(bf16)
    steps = (
        2.0 * OMEGA * INV_TURN / (lat_cells * SUB),
        2.0 * OMEGA * INV_TURN / (lon_cells * SUB),
        2.0 * OMEGA * INV_TURN / LEVELS,
    )
    parts = [split3(inw_ref[c : c + 1, :] * steps[c]) for c in range(3)]
    ext_row = lax.broadcasted_iota(jnp.int32, (128, width), 0)
    ext = jnp.zeros((128, width), f32)
    for level in range(3):
        for c in range(3):
            ext = jnp.where(ext_row == level * 3 + c, parts[c][level], ext)
    tab0_ref[:, 2 * cells : 2 * cells + 128] = ext.T.astype(bf16)
    wcol_ref[...] = jnp.broadcast_to(outw_ref[...], (128, width)).T

    oh0 = width
    oh1 = width + cells
    ex0 = width + 2 * cells
    rhs_ref[ex0:, :] = jnp.zeros((128, tile), bf16)
    g_ref[...] = jnp.zeros_like(g_ref)
    hidg_ref[...] = jnp.zeros_like(hidg_ref)
    og_ref[...] = jnp.zeros_like(og_ref)

    def step(i, carry):
        at = pl.ds(pl.multiple_of(i * tile, tile), tile)
        cell_q = q_ref[0:1, at]
        sub_r = q_ref[1:2, at]
        sub_c = q_ref[2:3, at]
        level = q_ref[3:4, at]
        cot = q_ref[4:5, at]
        for m in range(0, cells, 64):
            iota = (lax.broadcasted_iota(jnp.int32, (64, tile), 0) + m).astype(f32)
            onehot = jnp.where(iota == cell_q, 1.0, 0.0).astype(bf16)
            rhs_ref[oh0 + m : oh0 + m + 64, :] = onehot
            rhs_ref[oh1 + m : oh1 + m + 64, :] = onehot
        r = lax.broadcasted_iota(jnp.int32, (16, tile), 0)
        ints = jnp.where(r % 3 == 0, sub_r, jnp.where(r % 3 == 1, sub_c, level))
        rhs_ref[ex0 : ex0 + 16, :] = jnp.where(r < 9, ints, 0.0).astype(bf16)
        t_ref[...] = dot(tab0_ref[...], rhs_ref[oh0:, :])
        for m in range(0, width, ROWS):
            s, c = sincos_turns(t_ref[m : m + ROWS, :])
            rhs_ref[m : m + ROWS, :] = s.astype(bf16)
            c0_ref[m : m + ROWS, :] = c
        t_ref[...] = dot(tab1_ref[...], rhs_ref[0:ex0, :])
        for m in range(0, width, ROWS):
            s, c = sincos_turns(t_ref[m : m + ROWS, :] * INV_TURN)
            sw = s * cot
            w = wcol_ref[m : m + ROWS, :]
            og = og_ref[m : m + ROWS, :]
            cc = c * cot
            for n in range(0, tile, 128):
                og = og + sw[:, n : n + 128]
                d_ref[width + m : width + m + ROWS, n : n + 128] = (
                    cc[:, n : n + 128] * w
                ).astype(bf16)
            og_ref[m : m + ROWS, :] = og
        t_ref[...] = dot(hid_ref[...], d_ref[width:, :])
        for m in range(0, width, ROWS):
            d_ref[m : m + ROWS, :] = (
                t_ref[m : m + ROWS, :] * c0_ref[m : m + ROWS, :]
            ).astype(bf16)
        hidg_ref[...] += dot_nt(rhs_ref[0:width, :], d_ref[width:, :])
        g_ref[...] += dot_nt(rhs_ref[oh1 : ex0 + 16, :], d_ref[...])
        return carry

    lax.fori_loop(0, tiles, step, 0)

    g = g_ref[0:cells, :]
    hi, lo = split2(g)
    fg = (dot_nt(hi, mapw_ref[...]) + dot_nt(lo, mapw_ref[...])).astype(bf16)
    fg_ref[...] = fg
    feat_t = feat_ref[...].astype(f32).T.astype(bf16)
    map_ref[...] = dot(feat_t, hi) + dot(feat_t, lo)
    for a in range(3):
        conv_ref[a] = dot_tn(x3_ref[a * cols : a * cols + cells, :], fg)
    bias = jnp.sum(g, axis=0, keepdims=True)
    g0 = g[:, :width]
    ig0 = jnp.sum(lat_c * g0, axis=0, keepdims=True) + (2.0 / (lat_cells * SUB)) * g_ref[
        cells : cells + 1, :width
    ]
    ig1 = jnp.sum(lon_c * g0, axis=0, keepdims=True) + (2.0 / (lon_cells * SUB)) * g_ref[
        cells + 1 : cells + 2, :width
    ]
    ig2 = lev_c * bias[:, :width] + (2.0 / LEVELS) * g_ref[cells + 2 : cells + 3, :width]
    og = jnp.sum(og_ref[...].T, axis=0, keepdims=True)
    small_ref[0:1, :] = bias
    small_ref[1:2, 0:width] = OMEGA * ig0
    small_ref[1:2, width:] = OMEGA * ig1
    small_ref[2:3, 0:width] = OMEGA * ig2
    small_ref[2:3, width:] = og


def run_main(base, queries, center, halo, weights, dims):
    conv_weight, map_weight, map_bias, input_weight, hidden_weight, output_weight = weights
    rows, cols, ch = center.shape
    cells = rows * cols
    width = input_weight.shape[1]
    f32 = jnp.float32
    bf16 = jnp.bfloat16
    vmem = pl.BlockSpec(memory_space=pltpu.VMEM)
    return pl.pallas_call(
        functools.partial(main_kernel, dims),
        out_shape=(
            jax.ShapeDtypeStruct((cells, ch), bf16),
            jax.ShapeDtypeStruct((3, 3 * ch, ch), f32),
            jax.ShapeDtypeStruct((ch, 2 * width), f32),
            jax.ShapeDtypeStruct((width, width), f32),
            jax.ShapeDtypeStruct((3, 2 * width), f32),
        ),
        in_specs=[pl.BlockSpec(memory_space=pltpu.SMEM)] + [vmem] * 12,
        out_specs=(vmem,) * 5,
        scratch_shapes=[
            pltpu.VMEM(((rows + 2) * cols, 3 * ch), bf16),
            pltpu.VMEM((cells, ch), bf16),
            pltpu.VMEM((width, 2 * cells + 128), bf16),
            pltpu.VMEM((width, width + 2 * cells), bf16),
            pltpu.VMEM((width, 128), f32),
            pltpu.VMEM((width + 2 * cells + 128, TILE), bf16),
            pltpu.VMEM((width, TILE), f32),
            pltpu.VMEM((width, TILE), f32),
            pltpu.VMEM((2 * width, TILE), bf16),
            pltpu.VMEM((cells + 16, 2 * width), f32),
            pltpu.VMEM((width, 128), f32),
        ],
        compiler_params=pltpu.CompilerParams(vmem_limit_bytes=48 << 20),
        name="queries",
    )(
        base,
        queries,
        center,
        *halo,
        conv_weight.reshape(3, 3 * ch, ch),
        map_weight,
        map_bias.reshape(1, -1),
        input_weight,
        hidden_weight[0],
        output_weight.reshape(1, -1),
    )


def latent_kernel(center_ref, top_ref, bottom_ref, left_ref, right_ref, convw_ref, out_ref):
    rows, cols, ch = center_ref.shape
    cells = rows * cols
    x3 = shifted(center_ref[...], top_ref[...], bottom_ref[...], left_ref[...], right_ref[...])
    acc = None
    for a in (-1, 0, 1):
        start = (1 - a) * cols
        for b in (-1, 0, 1):
            part = dot_nt(x3[1 - b][start : start + cells], convw_ref[3 * (a + 1) + b + 1])
            acc = part if acc is None else acc + part
    out_ref[...] = acc.reshape(rows, cols, ch)


def halo_of(tile):
    lat = lax.axis_size("lat")
    lon = lax.axis_size("lon")
    up = [(i, i + 1) for i in range(lat - 1)]
    down = [(i + 1, i) for i in range(lat - 1)]
    top = lax.ppermute(tile[-1:], "lat", up)
    bottom = lax.ppermute(tile[:1], "lat", down)
    east = [(i, (i + 1) % lon) for i in range(lon)]
    west = [((i + 1) % lon, i) for i in range(lon)]

    def column(j):
        return jnp.concatenate([top[0, j : j + 1], tile[:, j], bottom[0, j : j + 1]], axis=0)

    left = lax.ppermute(column(tile.shape[1] - 1), "lon", east)
    right = lax.ppermute(column(0), "lon", west)
    return top[0], bottom[0], left, right


def on_device(
    latents,
    conv_weight,
    map_weight,
    map_bias,
    input_weight,
    hidden_weight,
    output_weight,
    hit_owner,
    serve_block,
    query_grid,
    cotangent,
):
    rows, cols, ch = latents.shape
    lat_parts = lax.axis_size("lat")
    lon_parts = lax.axis_size("lon")
    dev_count = lat_parts * lon_parts
    dims = (rows * lat_parts, cols * lon_parts)
    hits = hit_owner.shape[0]
    group = cotangent.shape[0] // hits
    f32 = jnp.float32

    grid = query_grid.reshape(3, hits, group).astype(f32)
    data = jnp.concatenate(
        [grid[0], grid[1], grid[2], cotangent.reshape(hits, group)], axis=1
    )
    pick = (
        jnp.arange(dev_count, dtype=jnp.int32)[:, None] == hit_owner[None, :]
    ).astype(f32)
    outgoing = jnp.dot(pick, data, precision=lax.Precision.HIGHEST)
    arrived = lax.all_to_all(
        outgoing.reshape(dev_count, 1, 4 * group), ("lat", "lon"), split_axis=0, concat_axis=0, tiled=True
    ).reshape(dev_count, 4, group)
    block = jnp.maximum(serve_block[0], 0).astype(f32)[:, None]
    sub = arrived[:, 1]
    sub_r = jnp.floor((sub + 0.5) * (1.0 / SUB))
    zero = jnp.zeros_like(sub)
    queries = jnp.stack(
        [
            arrived[:, 0] + BLOCK * block,
            sub_r,
            sub - SUB * sub_r,
            arrived[:, 2],
            arrived[:, 3],
            zero,
            zero,
            zero,
        ]
    ).reshape(8, dev_count * group)

    base = jnp.stack(
        [lax.axis_index("lat") * rows, lax.axis_index("lon") * cols]
    ).astype(f32)
    weights = (conv_weight, map_weight, map_bias, input_weight, hidden_weight, output_weight)
    fg, conv_part, map_part, hid_part, small = run_main(
        base, queries, latents, halo_of(latents), weights, dims
    )
    fg3 = fg.reshape(rows, cols, ch)
    vmem = pl.BlockSpec(memory_space=pltpu.VMEM)
    latent_grad = pl.pallas_call(
        latent_kernel,
        out_shape=jax.ShapeDtypeStruct((rows, cols, ch), f32),
        in_specs=[vmem] * 6,
        out_specs=vmem,
        compiler_params=pltpu.CompilerParams(vmem_limit_bytes=32 << 20),
        name="latent",
    )(fg3, *halo_of(fg3), conv_weight)
    conv_part, map_part, hid_part, small = lax.psum(
        (conv_part, map_part, hid_part, small), ("lat", "lon")
    )
    scale = float(hits * group * dev_count) ** (-0.5)
    width = input_weight.shape[1]
    small = small * scale
    return (
        latent_grad,
        conv_part.reshape(9, ch, ch) * scale,
        map_part * scale,
        small[0],
        jnp.stack([small[1, :width], small[1, width:], small[2, :width]]),
        hid_part[None] * scale,
        small[2, width:],
    )


def solution(mesh):
    placed = (
        P("lat", "lon", None),
        P(),
        P(),
        P(),
        P(),
        P(),
        P(),
        P(("lat", "lon")),
        P(("lat", "lon"), None),
        P(None, ("lat", "lon")),
        P(("lat", "lon")),
    )
    return jax.shard_map(
        on_device,
        mesh=mesh,
        in_specs=placed,
        out_specs=(P("lat", "lon", None), P(), P(), P(), P(), P(), P()),
        check_vma=False,
    )
```

```python
import functools
import math

import jax
import jax.numpy as jnp
import numpy as np
from jax import lax
from jax.experimental import pallas as pl
from jax.experimental.pallas import tpu as pltpu
from jax.sharding import PartitionSpec as P

BLOCK = 128
LEVELS = 37
SUB = 6
OMEGA = 30.0
INV_TURN = float(1.0 / (2.0 * math.pi))
TURN = float(2.0 * math.pi)
TILE = 512
ROWS = 32


def _fit():
    nodes = np.cos((2 * np.arange(400) + 1) * np.pi / 800)
    r = (nodes + 1) / 4
    z = r * r
    sine = np.sqrt(2.0) * np.sin(np.pi * r)
    cosine = np.sqrt(2.0) * np.cos(np.pi * r)
    sa = np.stack([r * z**k for k in range(4)], 1)
    ca = np.stack([z**k for k in range(5)], 1)
    return (
        [float(v) for v in np.linalg.lstsq(sa, sine, rcond=None)[0]],
        [float(v) for v in np.linalg.lstsq(ca, cosine, rcond=None)[0]],
    )


SIN_C, COS_C = _fit()


def sincos_turns(t):
    r = t - jnp.round(t)
    z = r * r
    s = r * (SIN_C[0] + z * (SIN_C[1] + z * (SIN_C[2] + z * SIN_C[3])))
    c = COS_C[0] + z * (COS_C[1] + z * (COS_C[2] + z * (COS_C[3] + z * COS_C[4])))
    return s * c, 1.0 - s * s


def dot(a, b):
    return jnp.dot(a, b, preferred_element_type=jnp.float32)


def dot_nt(a, b):
    return lax.dot_general(a, b, (((1,), (1,)), ((), ())), preferred_element_type=jnp.float32)


def dot_tn(a, b):
    return lax.dot_general(a, b, (((0,), (0,)), ((), ())), preferred_element_type=jnp.float32)


def split2(v):
    hi = v.astype(jnp.bfloat16)
    return hi, (v - hi.astype(jnp.float32)).astype(jnp.bfloat16)


def split3(v):
    hi = v.astype(jnp.bfloat16).astype(jnp.float32)
    mid = (v - hi).astype(jnp.bfloat16).astype(jnp.float32)
    return hi, mid, v - hi - mid


def shifted(center, top, bottom, left, right):
    rows, cols, ch = center.shape
    total = (rows + 2) * cols
    mid = jnp.concatenate([top, center.reshape(rows * cols, ch), bottom], axis=0)
    mid32 = mid.astype(jnp.float32)
    col = lax.broadcasted_iota(jnp.int32, (rows + 2, cols, ch), 1)
    low = pltpu.roll(mid32, 1, 0).reshape(rows + 2, cols, ch)
    high = pltpu.roll(mid32, total - 1, 0).reshape(rows + 2, cols, ch)
    low = jnp.where(col == 0, left.astype(jnp.float32)[:, None, :], low)
    high = jnp.where(col == cols - 1, right.astype(jnp.float32)[:, None, :], high)
    return (
        low.reshape(total, ch).astype(jnp.bfloat16),
        mid,
        high.reshape(total, ch).astype(jnp.bfloat16),
    )


def main_kernel(
    dims,
    base_ref,
    q_ref,
    center_ref,
    top_ref,
    bottom_ref,
    left_ref,
    right_ref,
    convw_ref,
    mapw_ref,
    mapb_ref,
    inw_ref,
    hid_ref,
    outw_ref,
    fg_ref,
    grads_ref,
    small_ref,
    hidg_ref,
    x3_ref,
    feat_ref,
    tab0_ref,
    tab1_ref,
    wcol_ref,
    rhs_ref,
    t_ref,
    c0_ref,
    d_ref,
    g_ref,
    og_ref,
):
    lat_cells, lon_cells = dims
    rows, cols, ch = center_ref.shape
    cells = rows * cols
    width = inw_ref.shape[1]
    tile = rhs_ref.shape[1]
    tiles = q_ref.shape[1] // tile
    f32 = jnp.float32
    bf16 = jnp.bfloat16

    x3 = shifted(center_ref[...], top_ref[...], bottom_ref[...], left_ref[...], right_ref[...])
    for b in range(3):
        x3_ref[:, b * ch : (b + 1) * ch] = x3[b]
    acc = dot(x3_ref[0:cells, :], convw_ref[0])
    for a in (1, 2):
        acc += dot(x3_ref[a * cols : a * cols + cells, :], convw_ref[a])
    feat_ref[...] = acc.astype(bf16)

    shift = dot(feat_ref[...], mapw_ref[...]) + mapb_ref[...]
    cell = lax.broadcasted_iota(jnp.int32, (cells, width), 0)
    row_f = (cell // cols).astype(f32)
    col_f = (cell % cols).astype(f32)
    lat_c = ((base_ref[0] + row_f) * SUB + 0.5) * (2.0 / (lat_cells * SUB)) - 1.0
    lon_c = ((base_ref[1] + col_f) * SUB + 0.5) * (2.0 / (lon_cells * SUB)) - 1.0
    lev_c = 1.0 / LEVELS - 1.0
    linear = (
        lat_c * inw_ref[0:1, :] + lon_c * inw_ref[1:2, :] + lev_c * inw_ref[2:3, :]
    )
    turn0 = (OMEGA * linear + shift[:, :width]) * INV_TURN
    turn0 = turn0 - jnp.round(turn0)
    hi, lo = split2(turn0.T)
    tab0_ref[:, 0:cells] = hi
    tab0_ref[:, cells : 2 * cells] = lo
    turn1 = shift[:, width:] * INV_TURN
    turn1 = (turn1 - jnp.round(turn1)) * TURN
    hi, lo = split2(turn1.T)
    tab1_ref[:, width : width + cells] = hi
    tab1_ref[:, width + cells : width + 2 * cells] = lo
    tab1_ref[:, 0:width] = hid_ref[...].astype(f32).T.astype(bf16)
    steps = (
        2.0 * OMEGA * INV_TURN / (lat_cells * SUB),
        2.0 * OMEGA * INV_TURN / (lon_cells * SUB),
        2.0 * OMEGA * INV_TURN / LEVELS,
    )
    parts = [split3(inw_ref[c : c + 1, :] * steps[c]) for c in range(3)]
    ext_row = lax.broadcasted_iota(jnp.int32, (128, width), 0)
    ext = jnp.zeros((128, width), f32)
    for level in range(3):
        for c in range(3):
            ext = jnp.where(ext_row == level * 3 + c, parts[c][level], ext)
    tab0_ref[:, 2 * cells : 2 * cells + 128] = ext.T.astype(bf16)
    wcol_ref[...] = jnp.broadcast_to(outw_ref[...], (128, width)).T

    oh0 = width
    oh1 = width + cells
    ex0 = width + 2 * cells
    rhs_ref[ex0:, :] = jnp.zeros((128, tile), bf16)
    g_ref[...] = jnp.zeros_like(g_ref)
    hidg_ref[...] = jnp.zeros_like(hidg_ref)
    og_ref[...] = jnp.zeros_like(og_ref)

    def step(i, carry):
        at = pl.ds(pl.multiple_of(i * tile, tile), tile)
        cell_q = q_ref[0:1, at]
        sub_r = q_ref[1:2, at]
        sub_c = q_ref[2:3, at]
        level = q_ref[3:4, at]
        cot = q_ref[4:5, at]
        for m in range(0, cells, 64):
            iota = (lax.broadcasted_iota(jnp.int32, (64, tile), 0) + m).astype(f32)
            onehot = jnp.where(iota == cell_q, 1.0, 0.0).astype(bf16)
            rhs_ref[oh0 + m : oh0 + m + 64, :] = onehot
            rhs_ref[oh1 + m : oh1 + m + 64, :] = onehot
        r = lax.broadcasted_iota(jnp.int32, (16, tile), 0)
        ints = jnp.where(r % 3 == 0, sub_r, jnp.where(r % 3 == 1, sub_c, level))
        rhs_ref[ex0 : ex0 + 16, :] = jnp.where(r < 9, ints, 0.0).astype(bf16)
        t_ref[...] = dot(tab0_ref[...], rhs_ref[oh0:, :])
        for m in range(0, width, ROWS):
            s, c = sincos_turns(t_ref[m : m + ROWS, :])
            rhs_ref[m : m + ROWS, :] = s.astype(bf16)
            c0_ref[m : m + ROWS, :] = c
        t_ref[...] = dot(tab1_ref[...], rhs_ref[0:ex0, :])
        for m in range(0, width, ROWS):
            s, c = sincos_turns(t_ref[m : m + ROWS, :] * INV_TURN)
            sw = s * cot
            w = wcol_ref[m : m + ROWS, :]
            og = og_ref[m : m + ROWS, :]
            cc = c * cot
            for n in range(0, tile, 128):
                og = og + sw[:, n : n + 128]
                d_ref[width + m : width + m + ROWS, n : n + 128] = (
                    cc[:, n : n + 128] * w
                ).astype(bf16)
            og_ref[m : m + ROWS, :] = og
        t_ref[...] = dot(hid_ref[...], d_ref[width:, :])
        for m in range(0, width, ROWS):
            d_ref[m : m + ROWS, :] = (
                t_ref[m : m + ROWS, :] * c0_ref[m : m + ROWS, :]
            ).astype(bf16)
        hidg_ref[...] += dot_nt(rhs_ref[0:width, :], d_ref[width:, :])
        g_ref[...] += dot_nt(rhs_ref[oh1 : ex0 + 16, :], d_ref[...])
        return carry

    lax.fori_loop(0, tiles, step, 0)

    g = g_ref[0:cells, :]
    hi, lo = split2(g)
    fg = (dot_nt(hi, mapw_ref[...]) + dot_nt(lo, mapw_ref[...])).astype(bf16)
    fg_ref[...] = fg
    feat_t = feat_ref[...].astype(f32).T.astype(bf16)
    grad = dot(feat_t, hi) + dot(feat_t, lo)
    for k in range(4):
        grads_ref[9 + k] = grad[:, k * ch : (k + 1) * ch]
        r, c = k // 2 * ch, k % 2 * ch
        grads_ref[13 + k] = hidg_ref[r : r + ch, c : c + ch]
    for a in range(3):
        grad = dot_tn(x3_ref[a * cols : a * cols + cells, :], fg)
        for b in range(3):
            grads_ref[3 * a + b] = grad[b * ch : (b + 1) * ch, :]
    bias = jnp.sum(g, axis=0, keepdims=True)
    g0 = g[:, :width]
    ig0 = jnp.sum(lat_c * g0, axis=0, keepdims=True) + (2.0 / (lat_cells * SUB)) * g_ref[
        cells : cells + 1, :width
    ]
    ig1 = jnp.sum(lon_c * g0, axis=0, keepdims=True) + (2.0 / (lon_cells * SUB)) * g_ref[
        cells + 1 : cells + 2, :width
    ]
    ig2 = lev_c * bias[:, :width] + (2.0 / LEVELS) * g_ref[cells + 2 : cells + 3, :width]
    og = jnp.sum(og_ref[...].T, axis=0, keepdims=True)
    small_ref[...] = jnp.zeros_like(small_ref)
    small_ref[0:1, :] = bias
    small_ref[1:2, 0:width] = OMEGA * ig0
    small_ref[1:2, width:] = OMEGA * ig1
    small_ref[2:3, 0:width] = OMEGA * ig2
    small_ref[2:3, width:] = og


def run_main(base, queries, center, halo, weights, dims):
    conv_weight, map_weight, map_bias, input_weight, hidden_weight, output_weight = weights
    rows, cols, ch = center.shape
    cells = rows * cols
    width = input_weight.shape[1]
    f32 = jnp.float32
    bf16 = jnp.bfloat16
    vmem = pl.BlockSpec(memory_space=pltpu.VMEM)
    return pl.pallas_call(
        functools.partial(main_kernel, dims),
        out_shape=(
            jax.ShapeDtypeStruct((cells, ch), bf16),
            jax.ShapeDtypeStruct((17, ch, ch), f32),
            jax.ShapeDtypeStruct((8, 2 * width), f32),
        ),
        in_specs=[pl.BlockSpec(memory_space=pltpu.SMEM)] + [vmem] * 12,
        out_specs=(vmem,) * 3,
        scratch_shapes=[
            pltpu.VMEM((width, width), f32),
            pltpu.VMEM(((rows + 2) * cols, 3 * ch), bf16),
            pltpu.VMEM((cells, ch), bf16),
            pltpu.VMEM((width, 2 * cells + 128), bf16),
            pltpu.VMEM((width, width + 2 * cells), bf16),
            pltpu.VMEM((width, 128), f32),
            pltpu.VMEM((width + 2 * cells + 128, TILE), bf16),
            pltpu.VMEM((width, TILE), f32),
            pltpu.VMEM((width, TILE), f32),
            pltpu.VMEM((2 * width, TILE), bf16),
            pltpu.VMEM((cells + 16, 2 * width), f32),
            pltpu.VMEM((width, 128), f32),
        ],
        compiler_params=pltpu.CompilerParams(vmem_limit_bytes=48 << 20),
        name="queries",
    )(
        base,
        queries,
        center,
        *halo,
        conv_weight.reshape(3, 3 * ch, ch),
        map_weight,
        map_bias.reshape(1, -1),
        input_weight,
        hidden_weight[0],
        output_weight.reshape(1, -1),
    )


def finish_kernel(
    sizes,
    scale,
    fg_ref,
    convw_ref,
    wg_ref,
    small_ref,
    latent_ref,
    conv_ref,
    map_ref,
    hid_ref,
    total_ref,
    send1,
    recv1,
    acc1,
    send2,
    recv2,
    acc2,
    send3,
    recv3,
    slots4,
    half,
    other,
    pair_s,
    x_s,
    y_s,
    z_s,
    row_s,
    row_r,
    col_s,
    col_r,
    sem_s,
    sem_r,
    ssem_s,
    ssem_r,
    hsem_s,
    hsem_r,
):
    nx, ny, nz = sizes
    bf16 = jnp.bfloat16
    f32 = jnp.float32
    lat = lax.axis_index("lat")
    lon = lax.axis_index("lon")
    lat_n = lax.axis_size("lat")
    lon_n = lax.axis_size("lon")
    z, c = lax.div(lat, 2), lax.rem(lat, 2)
    x, y = lax.div(lon, ny), lax.rem(lon, ny)
    blocks, rows, lanes = half.shape
    quarter = rows // nx
    final = quarter // ny

    def at_pair():
        return (lat + 1 - 2 * c, lon)

    def at_x(d):
        return (lat, lax.rem(x + d, nx) * ny + y)

    def at_y(d):
        return (lat, x * ny + lax.rem(y + d, ny))

    def at_z(d):
        return (lax.rem(z + d, nz) * 2 + c, lon)

    def at_first(d):
        return (lat, (1 - c) * (lax.rem(x + d, nx) * ny + y) + c * (x * ny + lax.rem(y + d, ny)))

    def at_second(d):
        return (lat, c * (lax.rem(x + d, nx) * ny + y) + (1 - c) * (x * ny + lax.rem(y + d, ny)))

    first = (1 - c) * x + c * y
    second = c * x + (1 - c) * y

    def copy(src, dst, s, r, device):
        return pltpu.make_async_remote_copy(
            src_ref=src,
            dst_ref=dst,
            send_sem=s,
            recv_sem=r,
            device_id=device,
            device_id_type=pl.DeviceIdType.MESH,
        )

    around = [(-1, 0), (1, 0), (0, -1), (0, 1), (-1, -1), (-1, 1), (1, -1), (1, 1)]

    def at_rim(da, db):
        return (lax.rem(lat + da + lat_n, lat_n), lax.rem(lon + db + lon_n, lon_n))

    barrier = pltpu.get_barrier_semaphore()
    peers = [at_pair()]
    peers += [at_x(d) for d in range(1, nx)]
    peers += [at_y(d) for d in range(1, ny)]
    peers += [at_z(d) for d in range(1, nz)]
    peers += [at_rim(da, db) for da, db in around]
    for peer in peers:
        pl.semaphore_signal(barrier, inc=1, device_id=peer, device_id_type=pl.DeviceIdType.MESH)

    tile_rows, cols, ch = latent_ref.shape
    keep = pl.ds(pl.multiple_of(c * lanes, lanes), lanes)
    give = pl.ds(pl.multiple_of((1 - c) * lanes, lanes), lanes)

    def to_send1(b, carry):
        send1[b] = wg_ref[b, :, give].astype(bf16)
        return carry

    lax.fori_loop(0, blocks, to_send1, 0)
    fg = fg_ref[...]
    fg32 = fg.astype(f32).reshape(tile_rows, cols, ch)
    col_s[0] = fg32[:, cols - 1, :].astype(bf16)
    col_s[1] = fg32[:, 0, :].astype(bf16)
    pair_s[c] = small_ref[...]

    pl.semaphore_wait(barrier, len(peers))

    cells = tile_rows * cols
    rim = [
        copy(fg_ref.at[pl.ds(0, cols)], row_r.at[1], hsem_s.at[0], hsem_r.at[1], at_rim(-1, 0)),
        copy(fg_ref.at[pl.ds(cells - cols, cols)], row_r.at[0], hsem_s.at[1], hsem_r.at[0], at_rim(1, 0)),
        copy(col_s.at[0], col_r.at[0], hsem_s.at[2], hsem_r.at[2], at_rim(0, 1)),
        copy(col_s.at[1], col_r.at[1], hsem_s.at[3], hsem_r.at[3], at_rim(0, -1)),
        copy(fg_ref.at[pl.ds(cells - cols, cols)], row_r.at[2], hsem_s.at[4], hsem_r.at[4], at_rim(1, 1)),
        copy(fg_ref.at[pl.ds(cells - cols, cols)], row_r.at[3], hsem_s.at[5], hsem_r.at[5], at_rim(1, -1)),
        copy(fg_ref.at[pl.ds(0, cols)], row_r.at[4], hsem_s.at[6], hsem_r.at[6], at_rim(-1, 1)),
        copy(fg_ref.at[pl.ds(0, cols)], row_r.at[5], hsem_s.at[7], hsem_r.at[7], at_rim(-1, -1)),
    ]
    p1 = copy(send1, recv1, sem_s.at[0], sem_r.at[0], at_pair())
    p1.start()
    q1 = copy(pair_s.at[c], pair_s.at[c], ssem_s.at[0], ssem_r.at[0], at_pair())
    q1.start()
    for item in rim:
        item.start()

    q1.wait()
    x_s[x] = pair_s[0] + pair_s[1]
    q2 = [
        copy(x_s.at[x], x_s.at[x], ssem_s.at[d], ssem_r.at[d], at_x(d)) for d in range(1, nx)
    ]
    for item in q2:
        item.start()

    p1.wait()

    def add1(b, carry):
        v = wg_ref[b, :, keep] + recv1[b].astype(f32)
        acc1[b] = v
        send2[b] = v.astype(bf16)
        return carry

    lax.fori_loop(0, blocks, add1, 0)
    p2 = []
    for d in range(1, nx):
        target = lax.rem(first + d, nx)
        p2.append(
            copy(
                send2.at[:, pl.ds(pl.multiple_of(target * quarter, quarter), quarter), :],
                recv2.at[d - 1],
                sem_s.at[d],
                sem_r.at[d],
                at_first(d),
            )
        )
        p2[-1].start()
    for item in q2:
        item.wait()
    y_s[y] = (x_s[0] + x_s[1]) + (x_s[2] + x_s[3])
    q3 = [
        copy(y_s.at[y], y_s.at[y], ssem_s.at[3 + d], ssem_r.at[3 + d], at_y(d))
        for d in range(1, ny)
    ]
    for item in q3:
        item.start()

    for item in rim:
        item.wait()
    up_ok = jnp.where(lat > 0, 1.0, 0.0).astype(f32)
    down_ok = jnp.where(lat < lat_n - 1, 1.0, 0.0).astype(f32)
    top = (row_r[0].astype(f32) * up_ok).astype(bf16)
    bottom = (row_r[1].astype(f32) * down_ok).astype(bf16)
    nw = row_r[2].astype(f32)[cols - 1 : cols] * up_ok
    ne = row_r[3].astype(f32)[0:1] * up_ok
    sw = row_r[4].astype(f32)[cols - 1 : cols] * down_ok
    se = row_r[5].astype(f32)[0:1] * down_ok
    left = jnp.concatenate([nw, col_r[0].astype(f32), sw], axis=0)
    right = jnp.concatenate([ne, col_r[1].astype(f32), se], axis=0)
    x3 = shifted(fg.reshape(tile_rows, cols, ch), top, bottom, left, right)
    acc = None
    for a in (-1, 0, 1):
        start = (1 - a) * cols
        for b in (-1, 0, 1):
            part = dot_nt(x3[1 - b][start : start + cells], convw_ref[3 * (a + 1) + b + 1])
            acc = part if acc is None else acc + part
    latent_ref[...] = acc.reshape(tile_rows, cols, ch)

    for item in p2:
        item.wait()
    mine = pl.ds(pl.multiple_of(first * quarter, quarter), quarter)

    def add2(b, carry):
        v = acc1[b, mine, :]
        for d in range(nx - 1):
            v += recv2[d, b].astype(f32)
        acc2[b] = v
        send3[b] = v.astype(bf16)
        return carry

    lax.fori_loop(0, blocks, add2, 0)
    p3 = []
    for d in range(1, ny):
        target = lax.rem(second + d, ny)
        p3.append(
            copy(
                send3.at[:, pl.ds(pl.multiple_of(target * final, final), final), :],
                recv3.at[d - 1],
                sem_s.at[3 + d],
                sem_r.at[3 + d],
                at_second(d),
            )
        )
        p3[-1].start()
    for item in q3:
        item.wait()
    z_s[z] = (y_s[0] + y_s[1]) + (y_s[2] + y_s[3])
    q4 = [
        copy(z_s.at[z], z_s.at[z], ssem_s.at[6 + d], ssem_r.at[6 + d], at_z(d))
        for d in range(1, nz)
    ]
    for item in q4:
        item.start()
    for item in p3:
        item.wait()
    ours = pl.ds(pl.multiple_of(second * final, final), final)

    def add3(b, carry):
        v = acc2[b, ours, :]
        for d in range(ny - 1):
            v += recv3[d, b].astype(f32)
        slots4[z, b] = v.astype(bf16)
        return carry

    lax.fori_loop(0, blocks, add3, 0)
    p4 = [
        copy(slots4.at[z], slots4.at[z], sem_s.at[6 + d], sem_r.at[6 + d], at_z(d))
        for d in range(1, nz)
    ]
    for item in p4:
        item.start()
    for item in q4:
        item.wait()
    total_ref[...] = ((z_s[0] + z_s[1]) + (z_s[2] + z_s[3])) * scale
    for item in p4:
        item.wait()
    place = pl.ds(pl.multiple_of(first * quarter + second * final, final), final)

    def add4(b, carry):
        v = (slots4[0, b].astype(f32) + slots4[1, b].astype(f32)) + (
            slots4[2, b].astype(f32) + slots4[3, b].astype(f32)
        )
        half[b, place, :] = v.astype(bf16)
        return carry

    lax.fori_loop(0, blocks, add4, 0)
    p5 = [
        copy(half.at[:, place, :], half.at[:, place, :], sem_s.at[9 + d], sem_r.at[9 + d], at_second(d))
        for d in range(1, ny)
    ]
    for item in p5:
        item.start()
    for item in p5:
        item.wait()
    p6 = [
        copy(half.at[:, mine, :], half.at[:, mine, :], sem_s.at[12 + d], sem_r.at[12 + d], at_first(d))
        for d in range(1, nx)
    ]
    for item in p6:
        item.start()
    for item in p6:
        item.wait()
    p7 = copy(half, other, sem_s.at[16], sem_r.at[16], at_pair())
    p7.start()

    def write(source, core):
        def conv_out(b, carry):
            lane = pl.ds(pl.multiple_of(core * lanes, lanes), lanes)
            conv_ref[b, :, lane] = source[b].astype(f32) * scale
            return carry

        lax.fori_loop(0, 9, conv_out, 0)
        for k in range(4):
            lane = pl.ds(pl.multiple_of(k * rows + core * lanes, lanes), lanes)
            map_ref[:, lane] = source[9 + k].astype(f32) * scale
            lane = pl.ds(pl.multiple_of(k % 2 * rows + core * lanes, lanes), lanes)
            hid_ref[k // 2 * rows : (k // 2 + 1) * rows, lane] = source[13 + k].astype(f32) * scale

    write(half, c)
    p7.wait()
    write(other, 1 - c)


def run_finish(fg, conv_weight, grads, small, tile_shape, scale, width):
    rows, cols, ch = tile_shape
    f32 = jnp.float32
    bf16 = jnp.bfloat16
    blocks, size, _ = grads.shape
    lanes = size // 2
    nx, ny, nz = 4, 4, 4
    dma = pltpu.SemaphoreType.DMA
    vmem = pl.BlockSpec(memory_space=pltpu.VMEM)
    return pl.pallas_call(
        functools.partial(finish_kernel, (nx, ny, nz), scale),
        out_shape=(
            jax.ShapeDtypeStruct((rows, cols, ch), f32),
            jax.ShapeDtypeStruct((9, ch, ch), f32),
            jax.ShapeDtypeStruct((ch, 2 * width), f32),
            jax.ShapeDtypeStruct((width, width), f32),
            jax.ShapeDtypeStruct(small.shape, f32),
        ),
        in_specs=[vmem] * 4,
        out_specs=(vmem,) * 5,
        scratch_shapes=[
            pltpu.VMEM((blocks, size, lanes), bf16),
            pltpu.VMEM((blocks, size, lanes), bf16),
            pltpu.VMEM((blocks, size, lanes), f32),
            pltpu.VMEM((blocks, size, lanes), bf16),
            pltpu.VMEM((nx - 1, blocks, size // nx, lanes), bf16),
            pltpu.VMEM((blocks, size // nx, lanes), f32),
            pltpu.VMEM((blocks, size // nx, lanes), bf16),
            pltpu.VMEM((ny - 1, blocks, size // nx // ny, lanes), bf16),
            pltpu.VMEM((nz, blocks, size // nx // ny, lanes), bf16),
            pltpu.VMEM((blocks, size, lanes), bf16),
            pltpu.VMEM((blocks, size, lanes), bf16),
            pltpu.VMEM((2,) + small.shape, f32),
            pltpu.VMEM((nx,) + small.shape, f32),
            pltpu.VMEM((ny,) + small.shape, f32),
            pltpu.VMEM((nz,) + small.shape, f32),
            pltpu.VMEM((1, cols, ch), bf16),
            pltpu.VMEM((6, cols, ch), bf16),
            pltpu.VMEM((2, rows, ch), bf16),
            pltpu.VMEM((2, rows, ch), bf16),
            dma((17,)),
            dma((17,)),
            dma((10,)),
            dma((10,)),
            dma((8,)),
            dma((8,)),
        ],
        compiler_params=pltpu.CompilerParams(
            vmem_limit_bytes=48 << 20, collective_id=1, has_side_effects=True
        ),
        name="finish",
    )(fg, conv_weight, grads, small)


def halo_of(tile):
    lat = lax.axis_size("lat")
    lon = lax.axis_size("lon")
    up = [(i, i + 1) for i in range(lat - 1)]
    down = [(i + 1, i) for i in range(lat - 1)]
    top = lax.ppermute(tile[-1:], "lat", up)
    bottom = lax.ppermute(tile[:1], "lat", down)
    east = [(i, (i + 1) % lon) for i in range(lon)]
    west = [((i + 1) % lon, i) for i in range(lon)]

    def column(j):
        return jnp.concatenate([top[0, j : j + 1], tile[:, j], bottom[0, j : j + 1]], axis=0)

    left = lax.ppermute(column(tile.shape[1] - 1), "lon", east)
    right = lax.ppermute(column(0), "lon", west)
    return top[0], bottom[0], left, right


def on_device(
    latents,
    conv_weight,
    map_weight,
    map_bias,
    input_weight,
    hidden_weight,
    output_weight,
    hit_owner,
    serve_block,
    query_grid,
    cotangent,
):
    rows, cols, ch = latents.shape
    lat_parts = lax.axis_size("lat")
    lon_parts = lax.axis_size("lon")
    dev_count = lat_parts * lon_parts
    dims = (rows * lat_parts, cols * lon_parts)
    hits = hit_owner.shape[0]
    group = cotangent.shape[0] // hits
    f32 = jnp.float32

    grid = query_grid.reshape(3, hits, group).astype(f32)
    data = jnp.concatenate(
        [grid[0], grid[1], grid[2], cotangent.reshape(hits, group)], axis=1
    )
    pick = (
        jnp.arange(dev_count, dtype=jnp.int32)[:, None] == hit_owner[None, :]
    ).astype(f32)
    outgoing = jnp.dot(pick, data, precision=lax.Precision.HIGHEST)
    arrived = lax.all_to_all(
        outgoing.reshape(dev_count, 1, 4 * group), ("lat", "lon"), split_axis=0, concat_axis=0, tiled=True
    ).reshape(dev_count, 4, group)
    block = jnp.maximum(serve_block[0], 0).astype(f32)[:, None]
    sub = arrived[:, 1]
    sub_r = jnp.floor((sub + 0.5) * (1.0 / SUB))
    zero = jnp.zeros_like(sub)
    queries = jnp.stack(
        [
            arrived[:, 0] + BLOCK * block,
            sub_r,
            sub - SUB * sub_r,
            arrived[:, 2],
            arrived[:, 3],
            zero,
            zero,
            zero,
        ]
    ).reshape(8, dev_count * group)

    base = jnp.stack(
        [lax.axis_index("lat") * rows, lax.axis_index("lon") * cols]
    ).astype(f32)
    weights = (conv_weight, map_weight, map_bias, input_weight, hidden_weight, output_weight)
    fg, grads, small = run_main(base, queries, latents, halo_of(latents), weights, dims)
    scale = float(hits * group * dev_count) ** (-0.5)
    width = input_weight.shape[1]
    latent_grad, conv_grad, map_grad, hidden_grad, small = run_finish(
        fg, conv_weight, grads, small, latents.shape, scale, width
    )
    return (
        latent_grad,
        conv_grad,
        map_grad,
        small[0],
        jnp.stack([small[1, :width], small[1, width:], small[2, :width]]),
        hidden_grad[None],
        small[2, width:],
    )


def solution(mesh):
    placed = (
        P("lat", "lon", None),
        P(),
        P(),
        P(),
        P(),
        P(),
        P(),
        P(("lat", "lon")),
        P(("lat", "lon"), None),
        P(None, ("lat", "lon")),
        P(("lat", "lon")),
    )
    return jax.shard_map(
        on_device,
        mesh=mesh,
        in_specs=placed,
        out_specs=(P("lat", "lon", None), P(), P(), P(), P(), P(), P()),
        check_vma=False,
    )
```

```python
import functools
import math

import jax
import jax.numpy as jnp
import numpy as np
from jax import lax
from jax.experimental import pallas as pl
from jax.experimental.pallas import tpu as pltpu
from jax.sharding import PartitionSpec as P

BLOCK = 128
LEVELS = 37
SUB = 6
OMEGA = 30.0
INV_TURN = float(1.0 / (2.0 * math.pi))
TURN = float(2.0 * math.pi)
TILE = 512
ROWS = 32
MCH = 512
NCH = 256
GM = 272
SPLIT = 10
CHUNKS = ((0, 6), (6, 12), (12, 17))


def _fit():
    nodes = np.cos((2 * np.arange(400) + 1) * np.pi / 800)
    r = (nodes + 1) / 4
    z = r * r
    sine = np.sqrt(2.0) * np.sin(np.pi * r)
    cosine = np.sqrt(2.0) * np.cos(np.pi * r)
    sa = np.stack([r * z**k for k in range(4)], 1)
    ca = np.stack([z**k for k in range(5)], 1)
    return (
        [float(v) for v in np.linalg.lstsq(sa, sine, rcond=None)[0]],
        [float(v) for v in np.linalg.lstsq(ca, cosine, rcond=None)[0]],
    )


SIN_C, COS_C = _fit()


def sincos_turns(t):
    r = t - jnp.round(t)
    z = r * r
    s = r * (SIN_C[0] + z * (SIN_C[1] + z * (SIN_C[2] + z * SIN_C[3])))
    c = COS_C[0] + z * (COS_C[1] + z * (COS_C[2] + z * (COS_C[3] + z * COS_C[4])))
    return s * c, 1.0 - s * s


def dot(a, b):
    return jnp.dot(a, b, preferred_element_type=jnp.float32)


def dot_nt(a, b):
    return lax.dot_general(a, b, (((1,), (1,)), ((), ())), preferred_element_type=jnp.float32)


def dot_tn(a, b):
    return lax.dot_general(a, b, (((0,), (0,)), ((), ())), preferred_element_type=jnp.float32)


def split2(v):
    hi = v.astype(jnp.bfloat16)
    return hi, (v - hi.astype(jnp.float32)).astype(jnp.bfloat16)


def split3(v):
    hi = v.astype(jnp.bfloat16).astype(jnp.float32)
    mid = (v - hi).astype(jnp.bfloat16).astype(jnp.float32)
    return hi, mid, v - hi - mid


def shifted(center, top, bottom, left, right):
    rows, cols, ch = center.shape
    total = (rows + 2) * cols
    mid = jnp.concatenate([top, center.reshape(rows * cols, ch), bottom], axis=0)
    mid32 = mid.astype(jnp.float32)
    col = lax.broadcasted_iota(jnp.int32, (rows + 2, cols, ch), 1)
    low = pltpu.roll(mid32, 1, 0).reshape(rows + 2, cols, ch)
    high = pltpu.roll(mid32, total - 1, 0).reshape(rows + 2, cols, ch)
    low = jnp.where(col == 0, left.astype(jnp.float32)[:, None, :], low)
    high = jnp.where(col == cols - 1, right.astype(jnp.float32)[:, None, :], high)
    return (
        low.reshape(total, ch).astype(jnp.bfloat16),
        mid,
        high.reshape(total, ch).astype(jnp.bfloat16),
    )


def main_kernel(
    dims,
    base_ref,
    q_ref,
    center_ref,
    top_ref,
    bottom_ref,
    left_ref,
    right_ref,
    convw_ref,
    mapw_ref,
    mapb_ref,
    inw_ref,
    hid_ref,
    outw_ref,
    fg_ref,
    grads_ref,
    small_ref,
    hidg_ref,
    x3_ref,
    feat_ref,
    tab0_ref,
    tab1_ref,
    wcol_ref,
    g_ref,
    og_ref,
    *pairs,
):
    lat_cells, lon_cells = dims
    rows, cols, ch = center_ref.shape
    cells = rows * cols
    width = inw_ref.shape[1]
    rhs_refs, c0_refs, d_refs = pairs[0:4], pairs[4:8], pairs[8:12]
    ta_ref, tc_ref, te_ref = pairs[12:]
    tile = rhs_refs[0].shape[1]
    tiles = q_ref.shape[1] // tile
    f32 = jnp.float32
    bf16 = jnp.bfloat16

    x3 = shifted(center_ref[...], top_ref[...], bottom_ref[...], left_ref[...], right_ref[...])
    for b in range(3):
        x3_ref[:, b * ch : (b + 1) * ch] = x3[b]
    acc = dot(x3_ref[0:cells, :], convw_ref[0])
    for a in (1, 2):
        acc += dot(x3_ref[a * cols : a * cols + cells, :], convw_ref[a])
    feat_ref[...] = acc.astype(bf16)

    shift = dot(feat_ref[...], mapw_ref[...]) + mapb_ref[...]
    cell = lax.broadcasted_iota(jnp.int32, (cells, width), 0)
    row_f = (cell // cols).astype(f32)
    col_f = (cell % cols).astype(f32)
    lat_c = ((base_ref[0] + row_f) * SUB + 0.5) * (2.0 / (lat_cells * SUB)) - 1.0
    lon_c = ((base_ref[1] + col_f) * SUB + 0.5) * (2.0 / (lon_cells * SUB)) - 1.0
    lev_c = 1.0 / LEVELS - 1.0
    linear = (
        lat_c * inw_ref[0:1, :] + lon_c * inw_ref[1:2, :] + lev_c * inw_ref[2:3, :]
    )
    turn0 = (OMEGA * linear + shift[:, :width]) * INV_TURN
    turn0 = turn0 - jnp.round(turn0)
    hi, lo = split2(turn0.T)
    tab0_ref[:, 0:cells] = hi
    tab0_ref[:, cells : 2 * cells] = lo
    turn1 = shift[:, width:] * INV_TURN
    turn1 = (turn1 - jnp.round(turn1)) * TURN
    hi, lo = split2(turn1.T)
    tab1_ref[:, width : width + cells] = hi
    tab1_ref[:, width + cells : width + 2 * cells] = lo
    tab1_ref[:, 0:width] = hid_ref[...].astype(f32).T.astype(bf16)
    steps = (
        2.0 * OMEGA * INV_TURN / (lat_cells * SUB),
        2.0 * OMEGA * INV_TURN / (lon_cells * SUB),
        2.0 * OMEGA * INV_TURN / LEVELS,
    )
    parts = [split3(inw_ref[c : c + 1, :] * steps[c]) for c in range(3)]
    ext_row = lax.broadcasted_iota(jnp.int32, (128, width), 0)
    ext = jnp.zeros((128, width), f32)
    for level in range(3):
        for c in range(3):
            ext = jnp.where(ext_row == level * 3 + c, parts[c][level], ext)
    tab0_ref[:, 2 * cells : 2 * cells + 128] = ext.T.astype(bf16)
    wcol_ref[...] = jnp.broadcast_to(outw_ref[...], (128, width)).T

    oh0 = width
    oh1 = width + cells
    ex0 = width + 2 * cells
    for rhs_ref in rhs_refs:
        rhs_ref[ex0:, :] = jnp.zeros((128, tile), bf16)
    g_ref[...] = jnp.zeros_like(g_ref)
    hidg_ref[...] = jnp.zeros_like(hidg_ref)
    og_ref[...] = jnp.zeros_like(og_ref)

    def encode(k, at):
        k = k % 4
        rhs_ref = rhs_refs[k]
        cell_q = q_ref[0:1, at]
        for m in range(0, cells, 64):
            iota = (lax.broadcasted_iota(jnp.int32, (64, tile), 0) + m).astype(f32)
            onehot = jnp.where(iota == cell_q, 1.0, 0.0).astype(bf16)
            rhs_ref[oh0 + m : oh0 + m + 64, :] = onehot
            rhs_ref[oh1 + m : oh1 + m + 64, :] = onehot
        r = lax.broadcasted_iota(jnp.int32, (16, tile), 0)
        ints = jnp.where(
            r % 3 == 0, q_ref[1:2, at], jnp.where(r % 3 == 1, q_ref[2:3, at], q_ref[3:4, at])
        )
        rhs_ref[ex0 : ex0 + 16, :] = jnp.where(r < 9, ints, 0.0).astype(bf16)

    def dots(out_ref, a_ref, b_ref, b_rows):
        def piece(m, n):
            def run():
                out_ref[m : m + MCH, n : n + NCH] = dot(
                    a_ref[m : m + MCH, :], b_ref[b_rows, n : n + NCH]
                )

            return run

        return [piece(m, n) for n in range(0, tile, NCH) for m in range(0, width, MCH)]

    def first_dot(k):
        k = k % 4

        return dots(ta_ref, tab0_ref, rhs_refs[k], slice(oh0, ex0 + 128))

    def second_dot(k):
        k = k % 4

        return dots(tc_ref, tab1_ref, rhs_refs[k], slice(0, ex0))

    def back_dot(k):
        k = k % 4

        return dots(te_ref, hid_ref, d_refs[k], slice(width, 2 * width))

    def first_sine(k):
        k = k % 4

        def piece(m):
            def run():
                s, c = sincos_turns(ta_ref[m : m + ROWS, :])
                rhs_refs[k][m : m + ROWS, :] = s.astype(bf16)
                c0_refs[k][m : m + ROWS, :] = c

            return run

        return [piece(m) for m in range(0, width, ROWS)]

    def second_sine(k, at):
        k = k % 4

        def piece(m):
            def run():
                cot = q_ref[4:5, at]
                s, c = sincos_turns(tc_ref[m : m + ROWS, :] * INV_TURN)
                sw = s * cot
                cc = c * cot
                w = wcol_ref[m : m + ROWS, :]
                og = og_ref[m : m + ROWS, :]
                for n in range(0, tile, 128):
                    og = og + sw[:, n : n + 128]
                    d_refs[k][width + m : width + m + ROWS, n : n + 128] = (
                        cc[:, n : n + 128] * w
                    ).astype(bf16)
                og_ref[m : m + ROWS, :] = og

            return run

        return [piece(m) for m in range(0, width, ROWS)]

    def back_cosine(k):
        k = k % 4

        def piece(m):
            def run():
                d_refs[k][m : m + ROWS, :] = (
                    te_ref[m : m + ROWS, :] * c0_refs[k][m : m + ROWS, :]
                ).astype(bf16)

            return run

        return [piece(m) for m in range(0, width, ROWS)]

    def hidden_sum(k):
        k = k % 4

        def piece(m, n):
            def run():
                hidg_ref[m : m + MCH, n : n + NCH] += dot_nt(
                    rhs_refs[k][m : m + MCH, :], d_refs[k][width + n : width + n + NCH, :]
                )

            return run

        return [piece(m, n) for n in range(0, width, NCH) for m in range(0, width, MCH)]

    def cell_sum(k):
        k = k % 4

        def piece(m, n):
            def run():
                e = min(m + GM, cells + 16)
                g_ref[m:e, n : n + NCH] += dot_nt(
                    rhs_refs[k][oh1 + m : oh1 + e, :], d_refs[k][n : n + NCH, :]
                )

            return run

        return [piece(m, n) for n in range(0, 2 * width, NCH) for m in range(0, cells + 16, GM)]

    def weave(first, second):
        i = j = 0
        while i < len(first) or j < len(second):
            if j >= len(second) or (i < len(first) and i * len(second) <= j * len(first)):
                first[i]()
                i += 1
            else:
                second[j]()
                j += 1

    def at_tile(i):
        return pl.ds(pl.multiple_of(i * tile, tile), tile)

    def stage(u, i, count):
        weave(
            back_dot(u) + (second_dot(u + 1) if count > 1 else []),
            first_sine(u + 2) if count > 2 else [],
        )
        ahead = []
        if count > 3:
            encode(u + 3, at_tile(i + 3))
            ahead = first_dot(u + 3)
        late = second_sine(u + 1, at_tile(i + 1)) if count > 1 else []
        weave(ahead + hidden_sum(u), back_cosine(u) + late[: len(late) * SPLIT // 16])
        weave(cell_sum(u), late[len(late) * SPLIT // 16 :])

    for i in range(3):
        encode(i, at_tile(i))
    weave(first_dot(0), [])
    weave([], first_sine(0))
    weave(first_dot(1) + second_dot(0), [])
    weave([], first_sine(1))
    weave(first_dot(2), second_sine(0, at_tile(0)))

    def step(i, carry):
        for u in range(4):
            stage(u, 4 * i + u, 4)
        return carry

    lax.fori_loop(0, tiles // 4 - 1, step, 0)
    for u in range(4):
        stage(u, tiles - 4 + u, 4 - u)

    g = g_ref[0:cells, :]
    hi, lo = split2(g)
    fg = (dot_nt(hi, mapw_ref[...]) + dot_nt(lo, mapw_ref[...])).astype(bf16)
    fg_ref[...] = fg
    feat_t = feat_ref[...].astype(f32).T.astype(bf16)
    grad = dot(feat_t, hi) + dot(feat_t, lo)
    for k in range(4):
        grads_ref[9 + k] = grad[:, k * ch : (k + 1) * ch]
        r, c = k // 2 * ch, k % 2 * ch
        grads_ref[13 + k] = hidg_ref[r : r + ch, c : c + ch]
    for a in range(3):
        grad = dot_tn(x3_ref[a * cols : a * cols + cells, :], fg)
        for b in range(3):
            grads_ref[3 * a + b] = grad[b * ch : (b + 1) * ch, :]
    bias = jnp.sum(g, axis=0, keepdims=True)
    g0 = g[:, :width]
    ig0 = jnp.sum(lat_c * g0, axis=0, keepdims=True) + (2.0 / (lat_cells * SUB)) * g_ref[
        cells : cells + 1, :width
    ]
    ig1 = jnp.sum(lon_c * g0, axis=0, keepdims=True) + (2.0 / (lon_cells * SUB)) * g_ref[
        cells + 1 : cells + 2, :width
    ]
    ig2 = lev_c * bias[:, :width] + (2.0 / LEVELS) * g_ref[cells + 2 : cells + 3, :width]
    og = jnp.sum(og_ref[...].T, axis=0, keepdims=True)
    small_ref[...] = jnp.zeros_like(small_ref)
    small_ref[0:1, :] = bias
    small_ref[1:2, 0:width] = OMEGA * ig0
    small_ref[1:2, width:] = OMEGA * ig1
    small_ref[2:3, 0:width] = OMEGA * ig2
    small_ref[2:3, width:] = og


def run_main(base, queries, center, halo, weights, dims):
    conv_weight, map_weight, map_bias, input_weight, hidden_weight, output_weight = weights
    rows, cols, ch = center.shape
    cells = rows * cols
    width = input_weight.shape[1]
    f32 = jnp.float32
    bf16 = jnp.bfloat16
    vmem = pl.BlockSpec(memory_space=pltpu.VMEM)
    return pl.pallas_call(
        functools.partial(main_kernel, dims),
        out_shape=(
            jax.ShapeDtypeStruct((cells, ch), bf16),
            jax.ShapeDtypeStruct((17, ch, ch), f32),
            jax.ShapeDtypeStruct((8, 2 * width), f32),
        ),
        in_specs=[pl.BlockSpec(memory_space=pltpu.SMEM)] + [vmem] * 12,
        out_specs=(vmem,) * 3,
        scratch_shapes=[
            pltpu.VMEM((width, width), f32),
            pltpu.VMEM(((rows + 2) * cols, 3 * ch), bf16),
            pltpu.VMEM((cells, ch), bf16),
            pltpu.VMEM((width, 2 * cells + 128), bf16),
            pltpu.VMEM((width, width + 2 * cells), bf16),
            pltpu.VMEM((width, 128), f32),
            pltpu.VMEM((cells + 16, 2 * width), f32),
            pltpu.VMEM((width, 128), f32),
        ]
        + [pltpu.VMEM((width + 2 * cells + 128, TILE), bf16)] * 4
        + [pltpu.VMEM((width, TILE), f32)] * 4
        + [pltpu.VMEM((2 * width, TILE), bf16)] * 4
        + [pltpu.VMEM((width, TILE), f32)] * 3,
        compiler_params=pltpu.CompilerParams(vmem_limit_bytes=48 << 20),
        name="queries",
    )(
        base,
        queries,
        center,
        *halo,
        conv_weight.reshape(3, 3 * ch, ch),
        map_weight,
        map_bias.reshape(1, -1),
        input_weight,
        hidden_weight[0],
        output_weight.reshape(1, -1),
    )


AROUND = ((-1, 0), (1, 0), (0, -1), (0, 1), (-1, -1), (-1, 1), (1, -1), (1, 1))


def remote(src, dst, send, recv, device):
    return pltpu.make_async_remote_copy(
        src_ref=src,
        dst_ref=dst,
        send_sem=send,
        recv_sem=recv,
        device_id=device,
        device_id_type=pl.DeviceIdType.MESH,
    )


def at_rim(da, db):
    lat_n = lax.axis_size("lat")
    lon_n = lax.axis_size("lon")
    lat = lax.rem(lax.axis_index("lat") + da + lat_n, lat_n)
    return (lat, lax.rem(lax.axis_index("lon") + db + lon_n, lon_n))


def meet(peers):
    barrier = pltpu.get_barrier_semaphore()
    for peer in peers:
        pl.semaphore_signal(barrier, inc=1, device_id=peer, device_id_type=pl.DeviceIdType.MESH)

    def wait():
        pl.semaphore_wait(barrier, len(peers))

    return wait


def rim_copies(flat_ref, cols, col_s, row_r, col_r, send, recv):
    cells = flat_ref.shape[0]
    first = flat_ref.at[pl.ds(0, cols)]
    last = flat_ref.at[pl.ds(cells - cols, cols)]
    return [
        remote(last, row_r.at[0], send.at[0], recv.at[0], at_rim(1, 0)),
        remote(first, row_r.at[1], send.at[1], recv.at[1], at_rim(-1, 0)),
        remote(col_s.at[0], col_r.at[0], send.at[2], recv.at[2], at_rim(0, 1)),
        remote(col_s.at[1], col_r.at[1], send.at[3], recv.at[3], at_rim(0, -1)),
        remote(last, row_r.at[2], send.at[4], recv.at[4], at_rim(1, 1)),
        remote(last, row_r.at[3], send.at[5], recv.at[5], at_rim(1, -1)),
        remote(first, row_r.at[4], send.at[6], recv.at[6], at_rim(-1, 1)),
        remote(first, row_r.at[5], send.at[7], recv.at[7], at_rim(-1, -1)),
    ]


def edge_columns(flat, rows, cols, col_s):
    tile = flat.astype(jnp.float32).reshape(rows, cols, flat.shape[1])
    col_s[0] = tile[:, cols - 1, :].astype(flat.dtype)
    col_s[1] = tile[:, 0, :].astype(flat.dtype)


def rim_values(cols, row_r, col_r):
    f32 = jnp.float32
    bf16 = jnp.bfloat16
    lat = lax.axis_index("lat")
    up = jnp.where(lat > 0, 1.0, 0.0).astype(f32)
    down = jnp.where(lat < lax.axis_size("lat") - 1, 1.0, 0.0).astype(f32)
    top = (row_r[0].astype(f32) * up).astype(bf16)
    bottom = (row_r[1].astype(f32) * down).astype(bf16)
    nw = row_r[2].astype(f32)[cols - 1 : cols] * up
    ne = row_r[3].astype(f32)[0:1] * up
    sw = row_r[4].astype(f32)[cols - 1 : cols] * down
    se = row_r[5].astype(f32)[0:1] * down
    left = jnp.concatenate([nw, col_r[0].astype(f32), sw], axis=0)
    right = jnp.concatenate([ne, col_r[1].astype(f32), se], axis=0)
    return top, bottom, left.astype(bf16), right.astype(bf16)


def front_kernel(
    data_ref,
    owner_ref,
    tile_ref,
    out_ref,
    top_ref,
    bottom_ref,
    left_ref,
    right_ref,
    go,
    mid,
    turned,
    row_r,
    col_s,
    col_r,
    send,
    recv,
    hsem_s,
    hsem_r,
):
    lat = lax.axis_index("lat")
    lon = lax.axis_index("lon")
    lat_n, lon_n, words = out_ref.shape
    hits = data_ref.shape[0]
    cols = top_ref.shape[0]
    rows = tile_ref.shape[0] // cols

    def at_lon(d):
        return (lat, lax.rem(lon + d, lon_n))

    def at_lat(d):
        return (lax.rem(lat + d, lat_n), lon)

    peers = [at_lon(d) for d in range(1, lon_n)] + [at_lat(d) for d in range(1, lat_n)]
    wait = meet(peers + [at_rim(da, db) for da, db in AROUND])

    at = lax.broadcasted_iota(jnp.int32, (lat_n * lon_n, hits), 0)
    device = lax.rem(at, lat_n) * lon_n + lax.div(at, lat_n)
    pick = jnp.where(device == owner_ref[...], 1.0, 0.0).astype(jnp.float32)
    picked = jnp.dot(
        pick, data_ref[...], precision=lax.Precision.HIGHEST, preferred_element_type=jnp.float32
    )
    go[...] = picked.reshape(lon_n, lat_n, words)
    mid[lon] = go[lon]
    edge_columns(tile_ref[...], rows, cols, col_s)
    wait()
    one = []
    for d in range(1, lon_n):
        peer = lax.rem(lon + d, lon_n)
        one.append(remote(go.at[peer], mid.at[lon], send.at[d], recv.at[d], at_lon(d)))
        one[-1].start()
    rim = rim_copies(tile_ref, cols, col_s, row_r, col_r, hsem_s, hsem_r)
    for item in rim:
        item.start()
    for item in one:
        item.wait()
    for k in range(lat_n):
        turned[k] = mid[:, k, :]
    out_ref[lat] = turned[lat]
    two = []
    for d in range(1, lat_n):
        peer = lax.rem(lat + d, lat_n)
        two.append(
            remote(
                turned.at[peer],
                out_ref.at[lat],
                send.at[lon_n + d],
                recv.at[lon_n + d],
                at_lat(d),
            )
        )
        two[-1].start()
    for item in rim:
        item.wait()
    top, bottom, left, right = rim_values(cols, row_r, col_r)
    top_ref[...] = top
    bottom_ref[...] = bottom
    left_ref[...] = left
    right_ref[...] = right
    for item in two:
        item.wait()


def run_front(data, owner, tile, lat_n, lon_n):
    rows, cols, ch = tile.shape
    hits, words = data.shape
    f32 = jnp.float32
    bf16 = jnp.bfloat16
    dma = pltpu.SemaphoreType.DMA
    vmem = pl.BlockSpec(memory_space=pltpu.VMEM)
    return pl.pallas_call(
        front_kernel,
        out_shape=(
            jax.ShapeDtypeStruct((lat_n, lon_n, words), f32),
            jax.ShapeDtypeStruct((cols, ch), bf16),
            jax.ShapeDtypeStruct((cols, ch), bf16),
            jax.ShapeDtypeStruct((rows + 2, ch), bf16),
            jax.ShapeDtypeStruct((rows + 2, ch), bf16),
        ),
        in_specs=[vmem] * 3,
        out_specs=(vmem,) * 5,
        scratch_shapes=[
            pltpu.VMEM((lon_n, lat_n, words), f32),
            pltpu.VMEM((lon_n, lat_n, words), f32),
            pltpu.VMEM((lat_n, lon_n, words), f32),
            pltpu.VMEM((6, cols, ch), bf16),
            pltpu.VMEM((2, rows, ch), bf16),
            pltpu.VMEM((2, rows, ch), bf16),
            dma((lon_n + lat_n,)),
            dma((lon_n + lat_n,)),
            dma((8,)),
            dma((8,)),
        ],
        compiler_params=pltpu.CompilerParams(
            vmem_limit_bytes=16 << 20, collective_id=2, has_side_effects=True
        ),
        name="front",
    )(data, owner.reshape(1, hits), tile.reshape(rows * cols, ch))


def finish_kernel(
    sizes,
    chunks,
    scale,
    fg_ref,
    convw_ref,
    wg_ref,
    small_ref,
    latent_ref,
    half,
    other,
    total_ref,
    send1,
    recv1,
    acc1,
    send2,
    recv2,
    acc2,
    send3,
    recv3,
    slots4,
    pair_s,
    x_s,
    y_s,
    z_s,
    row_r,
    col_s,
    col_r,
    sem_s,
    sem_r,
    ssem_s,
    ssem_r,
    hsem_s,
    hsem_r,
):
    nx, ny, nz = sizes
    bf16 = jnp.bfloat16
    f32 = jnp.float32
    lat = lax.axis_index("lat")
    lon = lax.axis_index("lon")
    z, c = lax.div(lat, 2), lax.rem(lat, 2)
    x, y = lax.div(lon, ny), lax.rem(lon, ny)
    blocks, rows, lanes = half.shape
    quarter = rows // nx
    final = quarter // ny

    def at_pair():
        return (lat + 1 - 2 * c, lon)

    def at_x(d):
        return (lat, lax.rem(x + d, nx) * ny + y)

    def at_y(d):
        return (lat, x * ny + lax.rem(y + d, ny))

    def at_z(d):
        return (lax.rem(z + d, nz) * 2 + c, lon)

    def at_first(d):
        return (lat, (1 - c) * at_x(d)[1] + c * at_y(d)[1])

    def at_second(d):
        return (lat, c * at_x(d)[1] + (1 - c) * at_y(d)[1])

    first = (1 - c) * x + c * y
    second = c * x + (1 - c) * y

    peers = [at_pair()]
    peers += [at_x(d) for d in range(1, nx)]
    peers += [at_y(d) for d in range(1, ny)]
    peers += [at_z(d) for d in range(1, nz)]
    peers += [at_rim(da, db) for da, db in AROUND]
    wait = meet(peers)

    tile_rows, cols, ch = latent_ref.shape
    cells = tile_rows * cols
    keep = pl.ds(pl.multiple_of(c * lanes, lanes), lanes)
    give = pl.ds(pl.multiple_of((1 - c) * lanes, lanes), lanes)
    mine = pl.ds(pl.multiple_of(first * quarter, quarter), quarter)
    ours = pl.ds(pl.multiple_of(second * final, final), final)
    place = pl.ds(pl.multiple_of(first * quarter + second * final, final), final)

    def each(chunk, body):
        def one(b, carry):
            body(b)
            return carry

        lax.fori_loop(chunk[0], chunk[1], one, 0)

    def to_send1(b):
        send1[b] = wg_ref[b, :, give].astype(bf16)

    edge_columns(fg_ref[...], tile_rows, cols, col_s)
    pair_s[c] = small_ref[...]
    each(chunks[0], to_send1)
    wait()
    rim = rim_copies(fg_ref, cols, col_s, row_r, col_r, hsem_s, hsem_r)
    for item in rim:
        item.start()
    q1 = remote(pair_s.at[c], pair_s.at[c], ssem_s.at[0], ssem_r.at[0], at_pair())
    q1.start()

    def part(k):
        return pl.ds(chunks[k][0], chunks[k][1] - chunks[k][0])

    p1 = []
    for k in range(len(chunks)):
        if k > 0:
            each(chunks[k], to_send1)
        p1.append(
            remote(
                send1.at[part(k)], recv1.at[part(k)], sem_s.at[k, 0], sem_r.at[k, 0], at_pair()
            )
        )
        p1[-1].start()

    q1.wait()
    x_s[x] = pair_s[0] + pair_s[1]
    q2 = [remote(x_s.at[x], x_s.at[x], ssem_s.at[d], ssem_r.at[d], at_x(d)) for d in range(1, nx)]
    for item in q2:
        item.start()

    def add1(b):
        v = wg_ref[b, :, keep] + recv1[b].astype(f32)
        acc1[b] = v
        send2[b] = v.astype(bf16)

    p2 = []
    for k in range(len(chunks)):
        p1[k].wait()
        each(chunks[k], add1)
        group = []
        for d in range(1, nx):
            target = lax.rem(first + d, nx)
            group.append(
                remote(
                    send2.at[part(k), pl.ds(pl.multiple_of(target * quarter, quarter), quarter), :],
                    recv2.at[d - 1, part(k)],
                    sem_s.at[k, d],
                    sem_r.at[k, d],
                    at_first(d),
                )
            )
            group[-1].start()
        p2.append(group)

    for item in q2:
        item.wait()
    y_s[y] = (x_s[0] + x_s[1]) + (x_s[2] + x_s[3])
    q3 = [
        remote(y_s.at[y], y_s.at[y], ssem_s.at[3 + d], ssem_r.at[3 + d], at_y(d))
        for d in range(1, ny)
    ]
    for item in q3:
        item.start()

    for item in rim:
        item.wait()
    top, bottom, left, right = rim_values(cols, row_r, col_r)
    x3 = shifted(fg_ref[...].reshape(tile_rows, cols, ch), top, bottom, left, right)
    acc = None
    for a in (-1, 0, 1):
        start = (1 - a) * cols
        for b in (-1, 0, 1):
            piece = dot_nt(x3[1 - b][start : start + cells], convw_ref[3 * (a + 1) + b + 1])
            acc = piece if acc is None else acc + piece
    latent_ref[...] = acc.reshape(tile_rows, cols, ch)

    def add2(b):
        v = acc1[b, mine, :]
        for d in range(nx - 1):
            v += recv2[d, b].astype(f32)
        acc2[b] = v
        send3[b] = v.astype(bf16)

    p3 = []
    for k in range(len(chunks)):
        for item in p2[k]:
            item.wait()
        each(chunks[k], add2)
        group = []
        for d in range(1, ny):
            target = lax.rem(second + d, ny)
            group.append(
                remote(
                    send3.at[part(k), pl.ds(pl.multiple_of(target * final, final), final), :],
                    recv3.at[d - 1, part(k)],
                    sem_s.at[k, 3 + d],
                    sem_r.at[k, 3 + d],
                    at_second(d),
                )
            )
            group[-1].start()
        p3.append(group)

    for item in q3:
        item.wait()
    z_s[z] = (y_s[0] + y_s[1]) + (y_s[2] + y_s[3])
    q4 = [
        remote(z_s.at[z], z_s.at[z], ssem_s.at[6 + d], ssem_r.at[6 + d], at_z(d))
        for d in range(1, nz)
    ]
    for item in q4:
        item.start()

    def add3(b):
        v = acc2[b, ours, :]
        for d in range(ny - 1):
            v += recv3[d, b].astype(f32)
        slots4[z, b] = v.astype(bf16)

    p4 = []
    for k in range(len(chunks)):
        for item in p3[k]:
            item.wait()
        each(chunks[k], add3)
        group = [
            remote(
                slots4.at[z, part(k)],
                slots4.at[z, part(k)],
                sem_s.at[k, 6 + d],
                sem_r.at[k, 6 + d],
                at_z(d),
            )
            for d in range(1, nz)
        ]
        for item in group:
            item.start()
        p4.append(group)

    def add4(b):
        v = (slots4[0, b].astype(f32) + slots4[1, b].astype(f32)) + (
            slots4[2, b].astype(f32) + slots4[3, b].astype(f32)
        )
        half[b, place, :] = v.astype(bf16)

    p5 = []
    for k in range(len(chunks)):
        for item in p4[k]:
            item.wait()
        each(chunks[k], add4)
        spot = half.at[part(k), place, :]
        group = [
            remote(spot, spot, sem_s.at[k, 9 + d], sem_r.at[k, 9 + d], at_second(d))
            for d in range(1, ny)
        ]
        for item in group:
            item.start()
        p5.append(group)

    for item in q4:
        item.wait()
    total_ref[...] = ((z_s[0] + z_s[1]) + (z_s[2] + z_s[3])) * scale

    p6 = []
    p7 = []
    for k in range(len(chunks)):
        for item in p5[k]:
            item.wait()
        spot = half.at[part(k), mine, :]
        group = [
            remote(spot, spot, sem_s.at[k, 12 + d], sem_r.at[k, 12 + d], at_first(d))
            for d in range(1, nx)
        ]
        for item in group:
            item.start()
        p6.append(group)
        p7.append(
            remote(
                half.at[part(k), mine, :],
                other.at[part(k), mine, :],
                sem_s.at[k, 16],
                sem_r.at[k, 16],
                at_pair(),
            )
        )
        p7[-1].start()
    for k in range(len(chunks)):
        for d in range(1, nx):
            p6[k][d - 1].wait()
            source = lax.rem(first + nx - d, nx)
            rows_d = pl.ds(pl.multiple_of(source * quarter, quarter), quarter)
            p7.append(
                remote(
                    half.at[part(k), rows_d, :],
                    other.at[part(k), rows_d, :],
                    sem_s.at[k, 16 + d],
                    sem_r.at[k, 16 + d],
                    at_pair(),
                )
            )
            p7[-1].start()
    for item in p7:
        item.wait()


def unpack_kernel(scale, core_ref, half_ref, other_ref, small_ref, conv_ref, map_ref, hid_ref, bias_ref, in_ref, out_ref):
    f32 = jnp.float32
    blocks, rows, lanes = half_ref.shape
    width = in_ref.shape[1]

    def write(ref, lane0):
        def conv_out(b, carry):
            lane = pl.ds(pl.multiple_of(lane0, lanes), lanes)
            conv_ref[b, :, lane] = ref[b].astype(f32) * scale
            return carry

        lax.fori_loop(0, 9, conv_out, 0)
        for k in range(4):
            lane = pl.ds(pl.multiple_of(k * rows + lane0, lanes), lanes)
            map_ref[:, lane] = ref[9 + k].astype(f32) * scale
            lane = pl.ds(pl.multiple_of(k % 2 * rows + lane0, lanes), lanes)
            hid_ref[k // 2 * rows : (k // 2 + 1) * rows, lane] = ref[13 + k].astype(f32) * scale

    core = core_ref[0]
    write(half_ref, core * lanes)
    write(other_ref, (1 - core) * lanes)
    bias_ref[...] = small_ref[0:1, :]
    in_ref[0:1, :] = small_ref[1:2, 0:width]
    in_ref[1:2, :] = small_ref[1:2, width:]
    in_ref[2:3, :] = small_ref[2:3, 0:width]
    out_ref[...] = small_ref[2:3, width:]


def run_unpack(half, other, small, scale, width):
    f32 = jnp.float32
    _, ch, _ = half.shape
    core = lax.rem(lax.axis_index("lat"), 2).astype(jnp.int32).reshape(1)
    vmem = pl.BlockSpec(memory_space=pltpu.VMEM)
    return pl.pallas_call(
        functools.partial(unpack_kernel, scale),
        out_shape=(
            jax.ShapeDtypeStruct((9, ch, ch), f32),
            jax.ShapeDtypeStruct((ch, 2 * width), f32),
            jax.ShapeDtypeStruct((width, width), f32),
            jax.ShapeDtypeStruct((1, 2 * width), f32),
            jax.ShapeDtypeStruct((3, width), f32),
            jax.ShapeDtypeStruct((1, width), f32),
        ),
        in_specs=[pl.BlockSpec(memory_space=pltpu.SMEM)] + [vmem] * 3,
        out_specs=(vmem,) * 6,
        compiler_params=pltpu.CompilerParams(vmem_limit_bytes=24 << 20),
        name="unpack",
    )(core, half, other, small)


def run_finish(fg, conv_weight, grads, small, tile_shape, scale, width):
    rows, cols, ch = tile_shape
    f32 = jnp.float32
    bf16 = jnp.bfloat16
    blocks, size, _ = grads.shape
    lanes = size // 2
    nx, ny, nz = 4, 4, 4
    dma = pltpu.SemaphoreType.DMA
    vmem = pl.BlockSpec(memory_space=pltpu.VMEM)
    return pl.pallas_call(
        functools.partial(finish_kernel, (nx, ny, nz), CHUNKS, scale),
        out_shape=(
            jax.ShapeDtypeStruct((rows, cols, ch), f32),
            jax.ShapeDtypeStruct((blocks, size, lanes), bf16),
            jax.ShapeDtypeStruct((blocks, size, lanes), bf16),
            jax.ShapeDtypeStruct(small.shape, f32),
        ),
        in_specs=[vmem] * 4,
        out_specs=(vmem,) * 4,
        scratch_shapes=[
            pltpu.VMEM((blocks, size, lanes), bf16),
            pltpu.VMEM((blocks, size, lanes), bf16),
            pltpu.VMEM((blocks, size, lanes), f32),
            pltpu.VMEM((blocks, size, lanes), bf16),
            pltpu.VMEM((nx - 1, blocks, size // nx, lanes), bf16),
            pltpu.VMEM((blocks, size // nx, lanes), f32),
            pltpu.VMEM((blocks, size // nx, lanes), bf16),
            pltpu.VMEM((ny - 1, blocks, size // nx // ny, lanes), bf16),
            pltpu.VMEM((nz, blocks, size // nx // ny, lanes), bf16),
            pltpu.VMEM((2,) + small.shape, f32),
            pltpu.VMEM((nx,) + small.shape, f32),
            pltpu.VMEM((ny,) + small.shape, f32),
            pltpu.VMEM((nz,) + small.shape, f32),
            pltpu.VMEM((6, cols, ch), bf16),
            pltpu.VMEM((2, rows, ch), bf16),
            pltpu.VMEM((2, rows, ch), bf16),
            dma((len(CHUNKS), 20)),
            dma((len(CHUNKS), 20)),
            dma((10,)),
            dma((10,)),
            dma((8,)),
            dma((8,)),
        ],
        compiler_params=pltpu.CompilerParams(
            vmem_limit_bytes=48 << 20, collective_id=1, has_side_effects=True
        ),
        name="finish",
    )(fg, conv_weight, grads, small)


def on_device(
    latents,
    conv_weight,
    map_weight,
    map_bias,
    input_weight,
    hidden_weight,
    output_weight,
    hit_owner,
    serve_block,
    query_grid,
    cotangent,
):
    rows, cols, ch = latents.shape
    lat_parts = lax.axis_size("lat")
    lon_parts = lax.axis_size("lon")
    dev_count = lat_parts * lon_parts
    dims = (rows * lat_parts, cols * lon_parts)
    hits = hit_owner.shape[0]
    group = cotangent.shape[0] // hits
    f32 = jnp.float32

    grid = query_grid.astype(f32).reshape(3, hits, group)
    data = jnp.concatenate(
        [grid[0], grid[1], grid[2], cotangent.reshape(hits, group)], axis=1
    )
    arrived, *halo = run_front(data, hit_owner, latents, lat_parts, lon_parts)
    arrived = arrived.reshape(dev_count, 4, group)
    block = jnp.maximum(serve_block[0], 0).astype(f32)[:, None]
    sub = arrived[:, 1]
    sub_r = jnp.floor((sub + 0.5) * (1.0 / SUB))
    zero = jnp.zeros_like(sub)
    queries = jnp.stack(
        [
            arrived[:, 0] + BLOCK * block,
            sub_r,
            sub - SUB * sub_r,
            arrived[:, 2],
            arrived[:, 3],
            zero,
            zero,
            zero,
        ]
    ).reshape(8, dev_count * group)

    base = jnp.stack(
        [lax.axis_index("lat") * rows, lax.axis_index("lon") * cols]
    ).astype(f32)
    weights = (conv_weight, map_weight, map_bias, input_weight, hidden_weight, output_weight)
    fg, grads, small = run_main(base, queries, latents, halo, weights, dims)
    scale = float(hits * group * dev_count) ** (-0.5)
    width = input_weight.shape[1]
    latent_grad, half, other, small = run_finish(
        fg, conv_weight, grads, small, latents.shape, scale, width
    )
    conv_grad, map_grad, hidden_grad, bias_grad, input_grad, output_grad = run_unpack(
        half, other, small, scale, width
    )
    return (
        latent_grad,
        conv_grad,
        map_grad,
        bias_grad[0],
        input_grad,
        hidden_grad[None],
        output_grad[0],
    )


def solution(mesh):
    placed = (
        P("lat", "lon", None),
        P(),
        P(),
        P(),
        P(),
        P(),
        P(),
        P(("lat", "lon")),
        P(("lat", "lon"), None),
        P(None, ("lat", "lon")),
        P(("lat", "lon")),
    )
    return jax.shard_map(
        on_device,
        mesh=mesh,
        in_specs=placed,
        out_specs=(P("lat", "lon", None), P(), P(), P(), P(), P(), P()),
        check_vma=False,
    )
```

```python
import functools
import math

import jax
import jax.numpy as jnp
import numpy as np
from jax import lax
from jax.experimental import pallas as pl
from jax.experimental.pallas import tpu as pltpu
from jax.sharding import PartitionSpec as P

BLOCK = 128
LEVELS = 37
SUB = 6
OMEGA = 30.0
INV_TURN = float(1.0 / (2.0 * math.pi))
TURN = float(2.0 * math.pi)
TILE = 512
ROWS = 32
MCH = 512
NCH = 256
GM = 272
SPLIT = 10
MAIN_MB = 36
FINISH_MB = 24
CHUNKS = ((0, 6), (6, 12), (12, 17))


def _fit():
    nodes = np.cos((2 * np.arange(400) + 1) * np.pi / 800)
    r = (nodes + 1) / 4
    found = []
    for odd, target in ((1, np.sin(np.pi * r)), (0, np.cos(np.pi * r))):
        basis = np.stack([r ** (2 * k + odd) for k in range(4)], 1)
        target = np.sqrt(2.0) * target
        weight = np.ones(len(r))
        for _ in range(60):
            root = np.sqrt(weight)
            c = np.linalg.lstsq(basis * root[:, None], target * root, rcond=None)[0]
            weight = weight * np.abs(basis @ c - target)
            weight = weight / weight.sum()
        found.append([float(np.float32(v)) for v in c])
    return found


SIN_C, COS_C = _fit()


def sincos_turns(t):
    r = t - jnp.round(t)
    z = r * r
    s = r * (SIN_C[0] + z * (SIN_C[1] + z * (SIN_C[2] + z * SIN_C[3])))
    c = COS_C[0] + z * (COS_C[1] + z * (COS_C[2] + z * COS_C[3]))
    return s * c, 1.0 - s * s


def dot(a, b):
    return jnp.dot(a, b, preferred_element_type=jnp.float32)


def dot_nt(a, b):
    return lax.dot_general(a, b, (((1,), (1,)), ((), ())), preferred_element_type=jnp.float32)


def dot_tn(a, b):
    return lax.dot_general(a, b, (((0,), (0,)), ((), ())), preferred_element_type=jnp.float32)


def split2(v):
    hi = v.astype(jnp.bfloat16)
    return hi, (v - hi.astype(jnp.float32)).astype(jnp.bfloat16)


def split3(v):
    hi = v.astype(jnp.bfloat16).astype(jnp.float32)
    mid = (v - hi).astype(jnp.bfloat16).astype(jnp.float32)
    return hi, mid, v - hi - mid


def shifted(center, top, bottom, left, right):
    rows, cols, ch = center.shape
    total = (rows + 2) * cols
    mid = jnp.concatenate([top, center.reshape(rows * cols, ch), bottom], axis=0)
    mid32 = mid.astype(jnp.float32)
    col = lax.broadcasted_iota(jnp.int32, (rows + 2, cols, ch), 1)
    low = pltpu.roll(mid32, 1, 0).reshape(rows + 2, cols, ch)
    high = pltpu.roll(mid32, total - 1, 0).reshape(rows + 2, cols, ch)
    low = jnp.where(col == 0, left.astype(jnp.float32)[:, None, :], low)
    high = jnp.where(col == cols - 1, right.astype(jnp.float32)[:, None, :], high)
    return (
        low.reshape(total, ch).astype(jnp.bfloat16),
        mid,
        high.reshape(total, ch).astype(jnp.bfloat16),
    )


def main_kernel(
    dims,
    base_ref,
    q_ref,
    center_ref,
    top_ref,
    bottom_ref,
    left_ref,
    right_ref,
    convw_ref,
    mapw_ref,
    mapb_ref,
    inw_ref,
    hid_ref,
    outw_ref,
    fg_ref,
    grads_ref,
    small_ref,
    hidg_ref,
    x3_ref,
    feat_ref,
    tab0_ref,
    tab1_ref,
    wcol_ref,
    g_ref,
    og_ref,
    *pairs,
):
    lat_cells, lon_cells = dims
    rows, cols, ch = center_ref.shape
    cells = rows * cols
    width = inw_ref.shape[1]
    rhs_refs, c0_refs, d_refs = pairs[0:4], pairs[4:8], pairs[8:12]
    ta_ref, tc_ref, te_ref = pairs[12:]
    tile = rhs_refs[0].shape[1]
    tiles = q_ref.shape[1] // tile
    f32 = jnp.float32
    bf16 = jnp.bfloat16

    x3 = shifted(center_ref[...], top_ref[...], bottom_ref[...], left_ref[...], right_ref[...])
    for b in range(3):
        x3_ref[:, b * ch : (b + 1) * ch] = x3[b]
    acc = dot(x3_ref[0:cells, :], convw_ref[0])
    for a in (1, 2):
        acc += dot(x3_ref[a * cols : a * cols + cells, :], convw_ref[a])
    feat_ref[...] = acc.astype(bf16)

    shift = dot(feat_ref[...], mapw_ref[...]) + mapb_ref[...]
    cell = lax.broadcasted_iota(jnp.int32, (cells, width), 0)
    row_f = (cell // cols).astype(f32)
    col_f = (cell % cols).astype(f32)
    lat_c = ((base_ref[0] + row_f) * SUB + 0.5) * (2.0 / (lat_cells * SUB)) - 1.0
    lon_c = ((base_ref[1] + col_f) * SUB + 0.5) * (2.0 / (lon_cells * SUB)) - 1.0
    lev_c = 1.0 / LEVELS - 1.0
    linear = (
        lat_c * inw_ref[0:1, :] + lon_c * inw_ref[1:2, :] + lev_c * inw_ref[2:3, :]
    )
    turn0 = (OMEGA * linear + shift[:, :width]) * INV_TURN
    turn0 = turn0 - jnp.round(turn0)
    hi, lo = split2(turn0.T)
    tab0_ref[:, 0:cells] = hi
    tab0_ref[:, cells : 2 * cells] = lo
    turn1 = shift[:, width:] * INV_TURN
    turn1 = (turn1 - jnp.round(turn1)) * TURN
    hi, lo = split2(turn1.T)
    tab1_ref[:, width : width + cells] = hi
    tab1_ref[:, width + cells : width + 2 * cells] = lo
    tab1_ref[:, 0:width] = hid_ref[...].astype(f32).T.astype(bf16)
    steps = (
        2.0 * OMEGA * INV_TURN / (lat_cells * SUB),
        2.0 * OMEGA * INV_TURN / (lon_cells * SUB),
        2.0 * OMEGA * INV_TURN / LEVELS,
    )
    parts = [split3(inw_ref[c : c + 1, :] * steps[c]) for c in range(3)]
    ext_row = lax.broadcasted_iota(jnp.int32, (128, width), 0)
    ext = jnp.zeros((128, width), f32)
    for level in range(3):
        for c in range(3):
            ext = jnp.where(ext_row == level * 3 + c, parts[c][level], ext)
    tab0_ref[:, 2 * cells : 2 * cells + 128] = ext.T.astype(bf16)
    wcol_ref[...] = jnp.broadcast_to(outw_ref[...], (128, width)).T

    oh0 = width
    oh1 = width + cells
    ex0 = width + 2 * cells
    for rhs_ref in rhs_refs:
        rhs_ref[ex0:, :] = jnp.zeros((128, tile), bf16)
    g_ref[...] = jnp.zeros_like(g_ref)
    hidg_ref[...] = jnp.zeros_like(hidg_ref)
    og_ref[...] = jnp.zeros_like(og_ref)

    def encode(k, at):
        k = k % 4
        rhs_ref = rhs_refs[k]
        cell_q = q_ref[0:1, at].astype(bf16)
        one = jnp.ones((64, tile), bf16)
        zero = jnp.zeros((64, tile), bf16)
        for m in range(0, cells, 64):
            iota = (lax.broadcasted_iota(jnp.int32, (64, tile), 0) + m).astype(f32).astype(bf16)
            onehot = jnp.where(iota == cell_q, one, zero)
            rhs_ref[oh0 + m : oh0 + m + 64, :] = onehot
            rhs_ref[oh1 + m : oh1 + m + 64, :] = onehot
        r = lax.broadcasted_iota(jnp.int32, (16, tile), 0)
        ints = jnp.where(
            r % 3 == 0, q_ref[1:2, at], jnp.where(r % 3 == 1, q_ref[2:3, at], q_ref[3:4, at])
        )
        rhs_ref[ex0 : ex0 + 16, :] = jnp.where(r < 9, ints, 0.0).astype(bf16)

    def dots(out_ref, a_ref, b_ref, b_rows):
        def piece(m, n):
            def run():
                out_ref[m : m + MCH, n : n + NCH] = dot(
                    a_ref[m : m + MCH, :], b_ref[b_rows, n : n + NCH]
                )

            return run

        return [piece(m, n) for n in range(0, tile, NCH) for m in range(0, width, MCH)]

    def first_dot(k):
        k = k % 4

        return dots(ta_ref, tab0_ref, rhs_refs[k], slice(oh0, ex0 + 128))

    def second_dot(k):
        k = k % 4

        return dots(tc_ref, tab1_ref, rhs_refs[k], slice(0, ex0))

    def back_dot(k):
        k = k % 4

        return dots(te_ref, hid_ref, d_refs[k], slice(width, 2 * width))

    def first_sine(k):
        k = k % 4

        def piece(m):
            def run():
                s, c = sincos_turns(ta_ref[m : m + ROWS, :])
                rhs_refs[k][m : m + ROWS, :] = s.astype(bf16)
                c0_refs[k][m : m + ROWS, :] = c

            return run

        return [piece(m) for m in range(0, width, ROWS)]

    def second_sine(k, at):
        k = k % 4

        def piece(m):
            def run():
                cot = q_ref[4:5, at]
                s, c = sincos_turns(tc_ref[m : m + ROWS, :] * INV_TURN)
                sw = s * cot
                cc = c * cot
                w = wcol_ref[m : m + ROWS, :]
                og = og_ref[m : m + ROWS, :]
                for n in range(0, tile, 128):
                    og = og + sw[:, n : n + 128]
                    d_refs[k][width + m : width + m + ROWS, n : n + 128] = (
                        cc[:, n : n + 128] * w
                    ).astype(bf16)
                og_ref[m : m + ROWS, :] = og

            return run

        return [piece(m) for m in range(0, width, ROWS)]

    def back_cosine(k):
        k = k % 4

        def piece(m):
            def run():
                d_refs[k][m : m + ROWS, :] = (
                    te_ref[m : m + ROWS, :] * c0_refs[k][m : m + ROWS, :]
                ).astype(bf16)

            return run

        return [piece(m) for m in range(0, width, ROWS)]

    def hidden_sum(k):
        k = k % 4

        def piece(m, n):
            def run():
                hidg_ref[m : m + MCH, n : n + NCH] += dot_nt(
                    rhs_refs[k][m : m + MCH, :], d_refs[k][width + n : width + n + NCH, :]
                )

            return run

        return [piece(m, n) for n in range(0, width, NCH) for m in range(0, width, MCH)]

    def cell_sum(k):
        k = k % 4

        def piece(m, n):
            def run():
                e = min(m + GM, cells + 16)
                g_ref[m:e, n : n + NCH] += dot_nt(
                    rhs_refs[k][oh1 + m : oh1 + e, :], d_refs[k][n : n + NCH, :]
                )

            return run

        return [piece(m, n) for n in range(0, 2 * width, NCH) for m in range(0, cells + 16, GM)]

    def weave(first, second):
        i = j = 0
        while i < len(first) or j < len(second):
            if j >= len(second) or (i < len(first) and i * len(second) <= j * len(first)):
                first[i]()
                i += 1
            else:
                second[j]()
                j += 1

    def at_tile(i):
        return pl.ds(pl.multiple_of(i * tile, tile), tile)

    def stage(u, i, count):
        weave(
            back_dot(u) + (second_dot(u + 1) if count > 1 else []),
            first_sine(u + 2) if count > 2 else [],
        )
        ahead = []
        if count > 3:
            encode(u + 3, at_tile(i + 3))
            ahead = first_dot(u + 3)
        late = second_sine(u + 1, at_tile(i + 1)) if count > 1 else []
        weave(ahead + hidden_sum(u), back_cosine(u) + late[: len(late) * SPLIT // 16])
        weave(cell_sum(u), late[len(late) * SPLIT // 16 :])

    for i in range(3):
        encode(i, at_tile(i))
    weave(first_dot(0), [])
    weave([], first_sine(0))
    weave(first_dot(1) + second_dot(0), [])
    weave([], first_sine(1))
    weave(first_dot(2), second_sine(0, at_tile(0)))

    def step(i, carry):
        for u in range(4):
            stage(u, 4 * i + u, 4)
        return carry

    lax.fori_loop(0, tiles // 4 - 1, step, 0)
    for u in range(4):
        stage(u, tiles - 4 + u, 4 - u)

    g = g_ref[0:cells, :]
    hi, lo = split2(g)
    fg = (dot_nt(hi, mapw_ref[...]) + dot_nt(lo, mapw_ref[...])).astype(bf16)
    fg_ref[...] = fg
    feat_t = feat_ref[...].astype(f32).T.astype(bf16)
    grad = dot(feat_t, hi) + dot(feat_t, lo)
    for k in range(4):
        grads_ref[9 + k] = grad[:, k * ch : (k + 1) * ch]
        r, c = k // 2 * ch, k % 2 * ch
        grads_ref[13 + k] = hidg_ref[r : r + ch, c : c + ch]
    for a in range(3):
        grad = dot_tn(x3_ref[a * cols : a * cols + cells, :], fg)
        for b in range(3):
            grads_ref[3 * a + b] = grad[b * ch : (b + 1) * ch, :]
    bias = jnp.sum(g, axis=0, keepdims=True)
    g0 = g[:, :width]
    ig0 = jnp.sum(lat_c * g0, axis=0, keepdims=True) + (2.0 / (lat_cells * SUB)) * g_ref[
        cells : cells + 1, :width
    ]
    ig1 = jnp.sum(lon_c * g0, axis=0, keepdims=True) + (2.0 / (lon_cells * SUB)) * g_ref[
        cells + 1 : cells + 2, :width
    ]
    ig2 = lev_c * bias[:, :width] + (2.0 / LEVELS) * g_ref[cells + 2 : cells + 3, :width]
    og = jnp.sum(og_ref[...].T, axis=0, keepdims=True)
    small_ref[...] = jnp.zeros_like(small_ref)
    small_ref[0:1, :] = bias
    small_ref[1:2, 0:width] = OMEGA * ig0
    small_ref[1:2, width:] = OMEGA * ig1
    small_ref[2:3, 0:width] = OMEGA * ig2
    small_ref[2:3, width:] = og


def run_main(base, queries, center, halo, weights, dims):
    conv_weight, map_weight, map_bias, input_weight, hidden_weight, output_weight = weights
    rows, cols, ch = center.shape
    cells = rows * cols
    width = input_weight.shape[1]
    f32 = jnp.float32
    bf16 = jnp.bfloat16
    vmem = pl.BlockSpec(memory_space=pltpu.VMEM)
    return pl.pallas_call(
        functools.partial(main_kernel, dims),
        out_shape=(
            jax.ShapeDtypeStruct((cells, ch), bf16),
            jax.ShapeDtypeStruct((17, ch, ch), f32),
            jax.ShapeDtypeStruct((8, 2 * width), f32),
        ),
        in_specs=[pl.BlockSpec(memory_space=pltpu.SMEM)] + [vmem] * 12,
        out_specs=(vmem,) * 3,
        scratch_shapes=[
            pltpu.VMEM((width, width), f32),
            pltpu.VMEM(((rows + 2) * cols, 3 * ch), bf16),
            pltpu.VMEM((cells, ch), bf16),
            pltpu.VMEM((width, 2 * cells + 128), bf16),
            pltpu.VMEM((width, width + 2 * cells), bf16),
            pltpu.VMEM((width, 128), f32),
            pltpu.VMEM((cells + 16, 2 * width), f32),
            pltpu.VMEM((width, 128), f32),
        ]
        + [pltpu.VMEM((width + 2 * cells + 128, TILE), bf16)] * 4
        + [pltpu.VMEM((width, TILE), f32)] * 4
        + [pltpu.VMEM((2 * width, TILE), bf16)] * 4
        + [pltpu.VMEM((width, TILE), f32)] * 3,
        compiler_params=pltpu.CompilerParams(vmem_limit_bytes=MAIN_MB << 20),
        name="queries",
    )(
        base,
        queries,
        center,
        *halo,
        conv_weight.reshape(3, 3 * ch, ch),
        map_weight,
        map_bias.reshape(1, -1),
        input_weight,
        hidden_weight[0],
        output_weight.reshape(1, -1),
    )


AROUND = ((-1, 0), (1, 0), (0, -1), (0, 1), (-1, -1), (-1, 1), (1, -1), (1, 1))


def remote(src, dst, send, recv, device):
    return pltpu.make_async_remote_copy(
        src_ref=src,
        dst_ref=dst,
        send_sem=send,
        recv_sem=recv,
        device_id=device,
        device_id_type=pl.DeviceIdType.MESH,
    )


def at_rim(da, db):
    lat_n = lax.axis_size("lat")
    lon_n = lax.axis_size("lon")
    lat = lax.rem(lax.axis_index("lat") + da + lat_n, lat_n)
    return (lat, lax.rem(lax.axis_index("lon") + db + lon_n, lon_n))


def meet(peers):
    barrier = pltpu.get_barrier_semaphore()
    for peer in peers:
        pl.semaphore_signal(barrier, inc=1, device_id=peer, device_id_type=pl.DeviceIdType.MESH)

    def wait():
        pl.semaphore_wait(barrier, len(peers))

    return wait


def rim_copies(flat_ref, cols, col_s, row_r, col_r, send, recv):
    cells = flat_ref.shape[0]
    first = flat_ref.at[pl.ds(0, cols)]
    last = flat_ref.at[pl.ds(cells - cols, cols)]
    return [
        remote(last, row_r.at[0], send.at[0], recv.at[0], at_rim(1, 0)),
        remote(first, row_r.at[1], send.at[1], recv.at[1], at_rim(-1, 0)),
        remote(col_s.at[0], col_r.at[0], send.at[2], recv.at[2], at_rim(0, 1)),
        remote(col_s.at[1], col_r.at[1], send.at[3], recv.at[3], at_rim(0, -1)),
        remote(last, row_r.at[2], send.at[4], recv.at[4], at_rim(1, 1)),
        remote(last, row_r.at[3], send.at[5], recv.at[5], at_rim(1, -1)),
        remote(first, row_r.at[4], send.at[6], recv.at[6], at_rim(-1, 1)),
        remote(first, row_r.at[5], send.at[7], recv.at[7], at_rim(-1, -1)),
    ]


def edge_columns(flat, rows, cols, col_s):
    tile = flat.astype(jnp.float32).reshape(rows, cols, flat.shape[1])
    col_s[0] = tile[:, cols - 1, :].astype(flat.dtype)
    col_s[1] = tile[:, 0, :].astype(flat.dtype)


def rim_values(cols, row_r, col_r):
    f32 = jnp.float32
    bf16 = jnp.bfloat16
    lat = lax.axis_index("lat")
    up = jnp.where(lat > 0, 1.0, 0.0).astype(f32)
    down = jnp.where(lat < lax.axis_size("lat") - 1, 1.0, 0.0).astype(f32)
    top = (row_r[0].astype(f32) * up).astype(bf16)
    bottom = (row_r[1].astype(f32) * down).astype(bf16)
    nw = row_r[2].astype(f32)[cols - 1 : cols] * up
    ne = row_r[3].astype(f32)[0:1] * up
    sw = row_r[4].astype(f32)[cols - 1 : cols] * down
    se = row_r[5].astype(f32)[0:1] * down
    left = jnp.concatenate([nw, col_r[0].astype(f32), sw], axis=0)
    right = jnp.concatenate([ne, col_r[1].astype(f32), se], axis=0)
    return top, bottom, left.astype(bf16), right.astype(bf16)


def front_kernel(
    grid_ref,
    cot_ref,
    owner_ref,
    tile_ref,
    out_ref,
    top_ref,
    bottom_ref,
    left_ref,
    right_ref,
    data,
    go,
    mid,
    turned,
    row_r,
    col_s,
    col_r,
    send,
    recv,
    hsem_s,
    hsem_r,
):
    lat = lax.axis_index("lat")
    lon = lax.axis_index("lon")
    lat_n, lon_n, words = out_ref.shape
    hits, group = cot_ref.shape
    cols = top_ref.shape[0]
    rows = tile_ref.shape[0] // cols

    def at_lon(d):
        return (lat, lax.rem(lon + d, lon_n))

    def at_lat(d):
        return (lax.rem(lat + d, lat_n), lon)

    peers = [at_lon(d) for d in range(1, lon_n)] + [at_lat(d) for d in range(1, lat_n)]
    wait = meet(peers + [at_rim(da, db) for da, db in AROUND])

    at = lax.broadcasted_iota(jnp.int32, (lat_n * lon_n, hits), 0)
    device = lax.rem(at, lat_n) * lon_n + lax.div(at, lat_n)
    pick = jnp.where(device == owner_ref[...], 1.0, 0.0).astype(jnp.float32)
    for k in range(3):
        data[:, k * group : (k + 1) * group] = grid_ref[k].astype(jnp.float32)
    data[:, 3 * group :] = cot_ref[...]
    picked = jnp.dot(
        pick, data[...], precision=lax.Precision.HIGHEST, preferred_element_type=jnp.float32
    )
    go[...] = picked.reshape(lon_n, lat_n, words)
    mid[lon] = go[lon]
    edge_columns(tile_ref[...], rows, cols, col_s)
    wait()
    one = []
    for d in range(1, lon_n):
        peer = lax.rem(lon + d, lon_n)
        one.append(remote(go.at[peer], mid.at[lon], send.at[d], recv.at[d], at_lon(d)))
        one[-1].start()
    rim = rim_copies(tile_ref, cols, col_s, row_r, col_r, hsem_s, hsem_r)
    for item in rim:
        item.start()
    for item in one:
        item.wait()
    for k in range(lat_n):
        turned[k] = mid[:, k, :]
    out_ref[lat] = turned[lat]
    two = []
    for d in range(1, lat_n):
        peer = lax.rem(lat + d, lat_n)
        two.append(
            remote(
                turned.at[peer],
                out_ref.at[lat],
                send.at[lon_n + d],
                recv.at[lon_n + d],
                at_lat(d),
            )
        )
        two[-1].start()
    for item in rim:
        item.wait()
    top, bottom, left, right = rim_values(cols, row_r, col_r)
    top_ref[...] = top
    bottom_ref[...] = bottom
    left_ref[...] = left
    right_ref[...] = right
    for item in two:
        item.wait()


def run_front(grid, cot, owner, tile, lat_n, lon_n):
    rows, cols, ch = tile.shape
    hits, group = cot.shape
    words = 4 * group
    f32 = jnp.float32
    bf16 = jnp.bfloat16
    dma = pltpu.SemaphoreType.DMA
    vmem = pl.BlockSpec(memory_space=pltpu.VMEM)
    return pl.pallas_call(
        front_kernel,
        out_shape=(
            jax.ShapeDtypeStruct((lat_n, lon_n, words), f32),
            jax.ShapeDtypeStruct((cols, ch), bf16),
            jax.ShapeDtypeStruct((cols, ch), bf16),
            jax.ShapeDtypeStruct((rows + 2, ch), bf16),
            jax.ShapeDtypeStruct((rows + 2, ch), bf16),
        ),
        in_specs=[vmem] * 4,
        out_specs=(vmem,) * 5,
        scratch_shapes=[
            pltpu.VMEM((hits, words), f32),
            pltpu.VMEM((lon_n, lat_n, words), f32),
            pltpu.VMEM((lon_n, lat_n, words), f32),
            pltpu.VMEM((lat_n, lon_n, words), f32),
            pltpu.VMEM((6, cols, ch), bf16),
            pltpu.VMEM((2, rows, ch), bf16),
            pltpu.VMEM((2, rows, ch), bf16),
            dma((lon_n + lat_n,)),
            dma((lon_n + lat_n,)),
            dma((8,)),
            dma((8,)),
        ],
        compiler_params=pltpu.CompilerParams(
            vmem_limit_bytes=16 << 20, collective_id=2, has_side_effects=True
        ),
        name="front",
    )(grid, cot, owner.reshape(1, hits), tile.reshape(rows * cols, ch))


def finish_kernel(
    sizes,
    chunks,
    scale,
    fg_ref,
    convw_ref,
    wg_ref,
    small_ref,
    latent_ref,
    half,
    other,
    total_ref,
    send1,
    recv1,
    acc1,
    send2,
    recv2,
    acc2,
    send3,
    recv3,
    slots4,
    pair_s,
    x_s,
    y_s,
    z_s,
    row_r,
    col_s,
    col_r,
    sem_s,
    sem_r,
    ssem_s,
    ssem_r,
    hsem_s,
    hsem_r,
):
    nx, ny, nz = sizes
    bf16 = jnp.bfloat16
    f32 = jnp.float32
    lat = lax.axis_index("lat")
    lon = lax.axis_index("lon")
    z, c = lax.div(lat, 2), lax.rem(lat, 2)
    x, y = lax.div(lon, ny), lax.rem(lon, ny)
    blocks, rows, lanes = half.shape
    quarter = rows // nx
    final = quarter // ny

    def at_pair():
        return (lat + 1 - 2 * c, lon)

    def at_x(d):
        return (lat, lax.rem(x + d, nx) * ny + y)

    def at_y(d):
        return (lat, x * ny + lax.rem(y + d, ny))

    def at_z(d):
        return (lax.rem(z + d, nz) * 2 + c, lon)

    axes = ((x, nx, at_x), (y, ny, at_y), (z, nz, at_z))
    orders = [[axes[(k + j) % 3] for j in range(3)] for k in range(len(chunks))]

    peers = [at_pair()]
    peers += [at_x(d) for d in range(1, nx)]
    peers += [at_y(d) for d in range(1, ny)]
    peers += [at_z(d) for d in range(1, nz)]
    peers += [at_rim(da, db) for da, db in AROUND]
    wait = meet(peers)

    tile_rows, cols, ch = latent_ref.shape
    cells = tile_rows * cols
    keep = pl.ds(pl.multiple_of(c * lanes, lanes), lanes)
    give = pl.ds(pl.multiple_of((1 - c) * lanes, lanes), lanes)

    def span(start, size):
        return pl.ds(pl.multiple_of(start, size), size)

    mine = [span(o[0][0] * quarter, quarter) for o in orders]
    ours = [span(o[1][0] * final, final) for o in orders]
    place = [span(o[0][0] * quarter + o[1][0] * final, final) for o in orders]

    def each(chunk, body):
        def one(b, carry):
            body(b)
            return carry

        lax.fori_loop(chunk[0], chunk[1], one, 0)

    def to_send1(b):
        send1[b] = wg_ref[b, :, give].astype(bf16)

    edge_columns(fg_ref[...], tile_rows, cols, col_s)
    pair_s[c] = small_ref[...]
    each(chunks[0], to_send1)
    wait()
    rim = rim_copies(fg_ref, cols, col_s, row_r, col_r, hsem_s, hsem_r)
    for item in rim:
        item.start()
    q1 = remote(pair_s.at[c], pair_s.at[c], ssem_s.at[0], ssem_r.at[0], at_pair())
    q1.start()

    def part(k):
        return pl.ds(chunks[k][0], chunks[k][1] - chunks[k][0])

    p1 = []
    for k in range(len(chunks)):
        if k > 0:
            each(chunks[k], to_send1)
        p1.append(
            remote(
                send1.at[part(k)], recv1.at[part(k)], sem_s.at[k, 0], sem_r.at[k, 0], at_pair()
            )
        )
        p1[-1].start()

    q1.wait()
    x_s[x] = pair_s[0] + pair_s[1]
    q2 = [remote(x_s.at[x], x_s.at[x], ssem_s.at[d], ssem_r.at[d], at_x(d)) for d in range(1, nx)]
    for item in q2:
        item.start()

    def add1(b):
        v = wg_ref[b, :, keep] + recv1[b].astype(f32)
        acc1[b] = v
        send2[b] = v.astype(bf16)

    p2 = []
    for k in range(len(chunks)):
        p1[k].wait()
        each(chunks[k], add1)
        group = []
        pos, count, at_first = orders[k][0]
        for d in range(1, count):
            target = lax.rem(pos + d, count)
            group.append(
                remote(
                    send2.at[part(k), pl.ds(pl.multiple_of(target * quarter, quarter), quarter), :],
                    recv2.at[d - 1, part(k)],
                    sem_s.at[k, d],
                    sem_r.at[k, d],
                    at_first(d),
                )
            )
            group[-1].start()
        p2.append(group)

    for item in q2:
        item.wait()
    y_s[y] = (x_s[0] + x_s[1]) + (x_s[2] + x_s[3])
    q3 = [
        remote(y_s.at[y], y_s.at[y], ssem_s.at[3 + d], ssem_r.at[3 + d], at_y(d))
        for d in range(1, ny)
    ]
    for item in q3:
        item.start()

    for item in rim:
        item.wait()
    top, bottom, left, right = rim_values(cols, row_r, col_r)
    x3 = shifted(fg_ref[...].reshape(tile_rows, cols, ch), top, bottom, left, right)
    acc = None
    for a in (-1, 0, 1):
        start = (1 - a) * cols
        for b in (-1, 0, 1):
            piece = dot_nt(x3[1 - b][start : start + cells], convw_ref[3 * (a + 1) + b + 1])
            acc = piece if acc is None else acc + piece
    latent_ref[...] = acc.reshape(tile_rows, cols, ch)

    def add2(k, b):
        v = acc1[b, mine[k], :]
        for d in range(nx - 1):
            v += recv2[d, b].astype(f32)
        acc2[b] = v
        send3[b] = v.astype(bf16)

    p3 = []
    for k in range(len(chunks)):
        for item in p2[k]:
            item.wait()
        each(chunks[k], functools.partial(add2, k))
        group = []
        pos, count, at_second = orders[k][1]
        for d in range(1, count):
            target = lax.rem(pos + d, count)
            group.append(
                remote(
                    send3.at[part(k), pl.ds(pl.multiple_of(target * final, final), final), :],
                    recv3.at[d - 1, part(k)],
                    sem_s.at[k, 3 + d],
                    sem_r.at[k, 3 + d],
                    at_second(d),
                )
            )
            group[-1].start()
        p3.append(group)

    for item in q3:
        item.wait()
    z_s[z] = (y_s[0] + y_s[1]) + (y_s[2] + y_s[3])
    q4 = [
        remote(z_s.at[z], z_s.at[z], ssem_s.at[6 + d], ssem_r.at[6 + d], at_z(d))
        for d in range(1, nz)
    ]
    for item in q4:
        item.start()

    def add3(k, b):
        v = acc2[b, ours[k], :]
        for d in range(ny - 1):
            v += recv3[d, b].astype(f32)
        slots4[orders[k][2][0], b] = v.astype(bf16)

    p4 = []
    for k in range(len(chunks)):
        for item in p3[k]:
            item.wait()
        each(chunks[k], functools.partial(add3, k))
        pos, count, at_third = orders[k][2]
        spot = slots4.at[pos, part(k)]
        group = [
            remote(spot, spot, sem_s.at[k, 6 + d], sem_r.at[k, 6 + d], at_third(d))
            for d in range(1, count)
        ]
        for item in group:
            item.start()
        p4.append(group)

    def add4(k, b):
        v = (slots4[0, b].astype(f32) + slots4[1, b].astype(f32)) + (
            slots4[2, b].astype(f32) + slots4[3, b].astype(f32)
        )
        half[b, place[k], :] = v.astype(bf16)

    p5 = []
    for k in range(len(chunks)):
        for item in p4[k]:
            item.wait()
        each(chunks[k], functools.partial(add4, k))
        spot = half.at[part(k), place[k], :]
        group = [
            remote(spot, spot, sem_s.at[k, 9 + d], sem_r.at[k, 9 + d], orders[k][1][2](d))
            for d in range(1, orders[k][1][1])
        ]
        for item in group:
            item.start()
        p5.append(group)

    for item in q4:
        item.wait()
    total_ref[...] = ((z_s[0] + z_s[1]) + (z_s[2] + z_s[3])) * scale

    p6 = []
    p7 = []
    for k in range(len(chunks)):
        for item in p5[k]:
            item.wait()
        spot = half.at[part(k), mine[k], :]
        group = [
            remote(spot, spot, sem_s.at[k, 12 + d], sem_r.at[k, 12 + d], orders[k][0][2](d))
            for d in range(1, orders[k][0][1])
        ]
        for item in group:
            item.start()
        p6.append(group)
        p7.append(
            remote(
                half.at[part(k), mine[k], :],
                other.at[part(k), mine[k], :],
                sem_s.at[k, 16],
                sem_r.at[k, 16],
                at_pair(),
            )
        )
        p7[-1].start()
    for k in range(len(chunks)):
        pos, count, _ = orders[k][0]
        for d in range(1, count):
            p6[k][d - 1].wait()
            rows_d = span(lax.rem(pos + count - d, count) * quarter, quarter)
            p7.append(
                remote(
                    half.at[part(k), rows_d, :],
                    other.at[part(k), rows_d, :],
                    sem_s.at[k, 16 + d],
                    sem_r.at[k, 16 + d],
                    at_pair(),
                )
            )
            p7[-1].start()
    for item in p7:
        item.wait()


def unpack_kernel(scale, core_ref, half_ref, other_ref, small_ref, conv_ref, map_ref, hid_ref, bias_ref, in_ref, out_ref):
    f32 = jnp.float32
    blocks, rows, lanes = half_ref.shape
    width = in_ref.shape[1]

    def write(ref, lane0):
        def conv_out(b, carry):
            lane = pl.ds(pl.multiple_of(lane0, lanes), lanes)
            conv_ref[b, :, lane] = ref[b].astype(f32) * scale
            return carry

        lax.fori_loop(0, 9, conv_out, 0)
        for k in range(4):
            lane = pl.ds(pl.multiple_of(k * rows + lane0, lanes), lanes)
            map_ref[:, lane] = ref[9 + k].astype(f32) * scale
            lane = pl.ds(pl.multiple_of(k % 2 * rows + lane0, lanes), lanes)
            hid_ref[k // 2 * rows : (k // 2 + 1) * rows, lane] = ref[13 + k].astype(f32) * scale

    core = core_ref[0]
    write(half_ref, core * lanes)
    write(other_ref, (1 - core) * lanes)
    bias_ref[...] = small_ref[0:1, :]
    in_ref[0:1, :] = small_ref[1:2, 0:width]
    in_ref[1:2, :] = small_ref[1:2, width:]
    in_ref[2:3, :] = small_ref[2:3, 0:width]
    out_ref[...] = small_ref[2:3, width:]


def run_unpack(half, other, small, scale, width):
    f32 = jnp.float32
    _, ch, _ = half.shape
    core = lax.rem(lax.axis_index("lat"), 2).astype(jnp.int32).reshape(1)
    vmem = pl.BlockSpec(memory_space=pltpu.VMEM)
    return pl.pallas_call(
        functools.partial(unpack_kernel, scale),
        out_shape=(
            jax.ShapeDtypeStruct((9, ch, ch), f32),
            jax.ShapeDtypeStruct((ch, 2 * width), f32),
            jax.ShapeDtypeStruct((width, width), f32),
            jax.ShapeDtypeStruct((1, 2 * width), f32),
            jax.ShapeDtypeStruct((3, width), f32),
            jax.ShapeDtypeStruct((1, width), f32),
        ),
        in_specs=[pl.BlockSpec(memory_space=pltpu.SMEM)] + [vmem] * 3,
        out_specs=(vmem,) * 6,
        compiler_params=pltpu.CompilerParams(vmem_limit_bytes=24 << 20),
        name="unpack",
    )(core, half, other, small)


def run_finish(fg, conv_weight, grads, small, tile_shape, scale, width):
    rows, cols, ch = tile_shape
    f32 = jnp.float32
    bf16 = jnp.bfloat16
    blocks, size, _ = grads.shape
    lanes = size // 2
    nx, ny, nz = 4, 4, 4
    dma = pltpu.SemaphoreType.DMA
    vmem = pl.BlockSpec(memory_space=pltpu.VMEM)
    return pl.pallas_call(
        functools.partial(finish_kernel, (nx, ny, nz), CHUNKS, scale),
        out_shape=(
            jax.ShapeDtypeStruct((rows, cols, ch), f32),
            jax.ShapeDtypeStruct((blocks, size, lanes), bf16),
            jax.ShapeDtypeStruct((blocks, size, lanes), bf16),
            jax.ShapeDtypeStruct(small.shape, f32),
        ),
        in_specs=[vmem] * 4,
        out_specs=(vmem,) * 4,
        scratch_shapes=[
            pltpu.VMEM((blocks, size, lanes), bf16),
            pltpu.VMEM((blocks, size, lanes), bf16),
            pltpu.VMEM((blocks, size, lanes), f32),
            pltpu.VMEM((blocks, size, lanes), bf16),
            pltpu.VMEM((nx - 1, blocks, size // nx, lanes), bf16),
            pltpu.VMEM((blocks, size // nx, lanes), f32),
            pltpu.VMEM((blocks, size // nx, lanes), bf16),
            pltpu.VMEM((ny - 1, blocks, size // nx // ny, lanes), bf16),
            pltpu.VMEM((nz, blocks, size // nx // ny, lanes), bf16),
            pltpu.VMEM((2,) + small.shape, f32),
            pltpu.VMEM((nx,) + small.shape, f32),
            pltpu.VMEM((ny,) + small.shape, f32),
            pltpu.VMEM((nz,) + small.shape, f32),
            pltpu.VMEM((6, cols, ch), bf16),
            pltpu.VMEM((2, rows, ch), bf16),
            pltpu.VMEM((2, rows, ch), bf16),
            dma((len(CHUNKS), 20)),
            dma((len(CHUNKS), 20)),
            dma((10,)),
            dma((10,)),
            dma((8,)),
            dma((8,)),
        ],
        compiler_params=pltpu.CompilerParams(
            vmem_limit_bytes=FINISH_MB << 20, collective_id=1, has_side_effects=True
        ),
        name="finish",
    )(fg, conv_weight, grads, small)


def on_device(
    latents,
    conv_weight,
    map_weight,
    map_bias,
    input_weight,
    hidden_weight,
    output_weight,
    hit_owner,
    serve_block,
    query_grid,
    cotangent,
):
    rows, cols, ch = latents.shape
    lat_parts = lax.axis_size("lat")
    lon_parts = lax.axis_size("lon")
    dev_count = lat_parts * lon_parts
    dims = (rows * lat_parts, cols * lon_parts)
    hits = hit_owner.shape[0]
    group = cotangent.shape[0] // hits
    f32 = jnp.float32

    arrived, *halo = run_front(
        query_grid.reshape(3, hits, group),
        cotangent.reshape(hits, group),
        hit_owner,
        latents,
        lat_parts,
        lon_parts,
    )
    arrived = arrived.reshape(dev_count, 4, group)
    block = jnp.maximum(serve_block[0], 0).astype(f32)[:, None]
    sub = arrived[:, 1]
    sub_r = jnp.floor((sub + 0.5) * (1.0 / SUB))
    zero = jnp.zeros_like(sub)
    queries = jnp.stack(
        [
            arrived[:, 0] + BLOCK * block,
            sub_r,
            sub - SUB * sub_r,
            arrived[:, 2],
            arrived[:, 3],
            zero,
            zero,
            zero,
        ]
    ).reshape(8, dev_count * group)

    base = jnp.stack(
        [lax.axis_index("lat") * rows, lax.axis_index("lon") * cols]
    ).astype(f32)
    weights = (conv_weight, map_weight, map_bias, input_weight, hidden_weight, output_weight)
    fg, grads, small = run_main(base, queries, latents, halo, weights, dims)
    scale = float(hits * group * dev_count) ** (-0.5)
    width = input_weight.shape[1]
    latent_grad, half, other, small = run_finish(
        fg, conv_weight, grads, small, latents.shape, scale, width
    )
    conv_grad, map_grad, hidden_grad, bias_grad, input_grad, output_grad = run_unpack(
        half, other, small, scale, width
    )
    return (
        latent_grad,
        conv_grad,
        map_grad,
        bias_grad[0],
        input_grad,
        hidden_grad[None],
        output_grad[0],
    )


def solution(mesh):
    placed = (
        P("lat", "lon", None),
        P(),
        P(),
        P(),
        P(),
        P(),
        P(),
        P(("lat", "lon")),
        P(("lat", "lon"), None),
        P(None, ("lat", "lon")),
        P(("lat", "lon")),
    )
    return jax.shard_map(
        on_device,
        mesh=mesh,
        in_specs=placed,
        out_specs=(P("lat", "lon", None), P(), P(), P(), P(), P(), P()),
        check_vma=False,
    )
```

```python
import functools
import math

import jax
import jax.numpy as jnp
import numpy as np
from jax import lax
from jax.experimental import pallas as pl
from jax.experimental.pallas import tpu as pltpu
from jax.sharding import PartitionSpec as P

BLOCK = 128
LEVELS = 37
SUB = 6
OMEGA = 30.0
INV_TURN = float(1.0 / (2.0 * math.pi))
TURN = float(2.0 * math.pi)
TILE = 512
ROWS = 32
MCH = 512
NCH = 256
GM = 272
SPLIT = 10
MAIN_MB = 36
FINISH_MB = 24
CHUNKS = ((0, 6), (6, 12), (12, 17))


def _fit():
    nodes = np.cos((2 * np.arange(400) + 1) * np.pi / 800)
    r = (nodes + 1) / 4
    found = []
    for odd, target in ((1, np.sin(np.pi * r)), (0, np.cos(np.pi * r))):
        basis = np.stack([r ** (2 * k + odd) for k in range(4)], 1)
        target = np.sqrt(2.0) * target
        weight = np.ones(len(r))
        for _ in range(60):
            root = np.sqrt(weight)
            c = np.linalg.lstsq(basis * root[:, None], target * root, rcond=None)[0]
            weight = weight * np.abs(basis @ c - target)
            weight = weight / weight.sum()
        found.append([float(np.float32(v)) for v in c])
    return found


SIN_C, COS_C = _fit()


def sincos_turns(t):
    r = t - jnp.round(t)
    z = r * r
    s = r * (SIN_C[0] + z * (SIN_C[1] + z * (SIN_C[2] + z * SIN_C[3])))
    c = COS_C[0] + z * (COS_C[1] + z * (COS_C[2] + z * COS_C[3]))
    return s * c, 1.0 - s * s


def dot(a, b):
    return jnp.dot(a, b, preferred_element_type=jnp.float32)


def dot_nt(a, b):
    return lax.dot_general(a, b, (((1,), (1,)), ((), ())), preferred_element_type=jnp.float32)


def dot_tn(a, b):
    return lax.dot_general(a, b, (((0,), (0,)), ((), ())), preferred_element_type=jnp.float32)


def split2(v):
    hi = v.astype(jnp.bfloat16)
    return hi, (v - hi.astype(jnp.float32)).astype(jnp.bfloat16)


def split3(v):
    hi = v.astype(jnp.bfloat16).astype(jnp.float32)
    mid = (v - hi).astype(jnp.bfloat16).astype(jnp.float32)
    return hi, mid, v - hi - mid


def shifted(center, top, bottom, left, right):
    rows, cols, ch = center.shape
    total = (rows + 2) * cols
    mid = jnp.concatenate([top, center.reshape(rows * cols, ch), bottom], axis=0)
    mid32 = mid.astype(jnp.float32)
    col = lax.broadcasted_iota(jnp.int32, (rows + 2, cols, ch), 1)
    low = pltpu.roll(mid32, 1, 0).reshape(rows + 2, cols, ch)
    high = pltpu.roll(mid32, total - 1, 0).reshape(rows + 2, cols, ch)
    low = jnp.where(col == 0, left.astype(jnp.float32)[:, None, :], low)
    high = jnp.where(col == cols - 1, right.astype(jnp.float32)[:, None, :], high)
    return (
        low.reshape(total, ch).astype(jnp.bfloat16),
        mid,
        high.reshape(total, ch).astype(jnp.bfloat16),
    )


def main_kernel(
    dims,
    q_ref,
    center_ref,
    top_ref,
    bottom_ref,
    left_ref,
    right_ref,
    convw_ref,
    mapw_ref,
    mapb_ref,
    inw_ref,
    hid_ref,
    outw_ref,
    fg_ref,
    grads_ref,
    small_ref,
    hidg_ref,
    x3_ref,
    feat_ref,
    tab0_ref,
    tab1_ref,
    hidw_ref,
    g_ref,
    og_ref,
    *pairs,
):
    lat_cells, lon_cells = dims
    rows, cols, ch = center_ref.shape
    cells = rows * cols
    width = inw_ref.shape[1]
    rhs_refs, c0_refs, d_refs = pairs[0:4], pairs[4:8], pairs[8:12]
    ta_ref, tc_ref, te_ref = pairs[12:]
    tile = rhs_refs[0].shape[1]
    tiles = q_ref.shape[1] // tile
    f32 = jnp.float32
    bf16 = jnp.bfloat16

    x3 = shifted(center_ref[...], top_ref[...], bottom_ref[...], left_ref[...], right_ref[...])
    for b in range(3):
        x3_ref[:, b * ch : (b + 1) * ch] = x3[b]
    acc = dot(x3_ref[0:cells, :], convw_ref[0])
    for a in (1, 2):
        acc += dot(x3_ref[a * cols : a * cols + cells, :], convw_ref[a])
    feat_ref[...] = acc.astype(bf16)

    shift = dot(feat_ref[...], mapw_ref[...]) + mapb_ref[...]
    cell = lax.broadcasted_iota(jnp.int32, (cells, width), 0)
    row_f = (cell // cols).astype(f32)
    col_f = (cell % cols).astype(f32)
    lat0 = (lax.axis_index("lat") * rows).astype(f32)
    lon0 = (lax.axis_index("lon") * cols).astype(f32)
    lat_c = ((lat0 + row_f) * SUB + 0.5) * (2.0 / (lat_cells * SUB)) - 1.0
    lon_c = ((lon0 + col_f) * SUB + 0.5) * (2.0 / (lon_cells * SUB)) - 1.0
    lev_c = 1.0 / LEVELS - 1.0
    linear = (
        lat_c * inw_ref[0:1, :] + lon_c * inw_ref[1:2, :] + lev_c * inw_ref[2:3, :]
    )
    turn0 = (OMEGA * linear + shift[:, :width]) * INV_TURN
    turn0 = turn0 - jnp.round(turn0)
    hi, lo = split2(turn0.T)
    tab0_ref[:, 0:cells] = hi
    tab0_ref[:, cells : 2 * cells] = lo
    turn1 = shift[:, width:] * INV_TURN
    turn1 = (turn1 - jnp.round(turn1)) * TURN
    hi, lo = split2(turn1.T)
    tab1_ref[:, width : width + cells] = hi
    tab1_ref[:, width + cells : width + 2 * cells] = lo
    tab1_ref[:, 0:width] = hid_ref[...].astype(f32).T.astype(bf16)
    steps = (
        2.0 * OMEGA * INV_TURN / (lat_cells * SUB),
        2.0 * OMEGA * INV_TURN / (lon_cells * SUB),
        2.0 * OMEGA * INV_TURN / LEVELS,
    )
    parts = [split3(inw_ref[c : c + 1, :] * steps[c]) for c in range(3)]
    ext_row = lax.broadcasted_iota(jnp.int32, (128, width), 0)
    ext = jnp.zeros((128, width), f32)
    for level in range(3):
        for c in range(3):
            ext = jnp.where(ext_row == level * 3 + c, parts[c][level], ext)
    tab0_ref[:, 2 * cells : 2 * cells + 128] = ext.T.astype(bf16)
    hidw_ref[...] = (hid_ref[...].astype(f32) * outw_ref[...]).astype(bf16)

    oh0 = width
    oh1 = width + cells
    ex0 = width + 2 * cells
    for rhs_ref in rhs_refs:
        rhs_ref[ex0:, :] = jnp.zeros((128, tile), bf16)
    g_ref[...] = jnp.zeros_like(g_ref)
    hidg_ref[...] = jnp.zeros_like(hidg_ref)
    og_ref[...] = jnp.zeros_like(og_ref)

    def encode(k, at):
        k = k % 4
        rhs_ref = rhs_refs[k]
        cell_q = q_ref[0:1, at].astype(bf16)
        one = jnp.ones((64, tile), bf16)
        zero = jnp.zeros((64, tile), bf16)
        for m in range(0, cells, 64):
            iota = (lax.broadcasted_iota(jnp.int32, (64, tile), 0) + m).astype(f32).astype(bf16)
            onehot = jnp.where(iota == cell_q, one, zero)
            rhs_ref[oh0 + m : oh0 + m + 64, :] = onehot
            rhs_ref[oh1 + m : oh1 + m + 64, :] = onehot
        r = lax.broadcasted_iota(jnp.int32, (16, tile), 0)
        ints = jnp.where(
            r % 3 == 0, q_ref[1:2, at], jnp.where(r % 3 == 1, q_ref[2:3, at], q_ref[3:4, at])
        )
        rhs_ref[ex0 : ex0 + 16, :] = jnp.where(r < 9, ints, 0.0).astype(bf16)

    def dots(out_ref, a_ref, b_ref, b_rows):
        def piece(m, n):
            def run():
                out_ref[m : m + MCH, n : n + NCH] = dot(
                    a_ref[m : m + MCH, :], b_ref[b_rows, n : n + NCH]
                )

            return run

        return [piece(m, n) for n in range(0, tile, NCH) for m in range(0, width, MCH)]

    def first_dot(k):
        k = k % 4

        return dots(ta_ref, tab0_ref, rhs_refs[k], slice(oh0, ex0 + 128))

    def second_dot(k):
        k = k % 4

        return dots(tc_ref, tab1_ref, rhs_refs[k], slice(0, ex0))

    def back_dot(k):
        k = k % 4

        return dots(te_ref, hidw_ref, d_refs[k], slice(width, 2 * width))

    def first_sine(k):
        k = k % 4

        def piece(m):
            def run():
                s, c = sincos_turns(ta_ref[m : m + ROWS, :])
                rhs_refs[k][m : m + ROWS, :] = s.astype(bf16)
                c0_refs[k][m : m + ROWS, :] = c

            return run

        return [piece(m) for m in range(0, width, ROWS)]

    def second_sine(k, at):
        k = k % 4

        def piece(m):
            def run():
                cot = q_ref[4:5, at]
                s, c = sincos_turns(tc_ref[m : m + ROWS, :] * INV_TURN)
                sw = s * cot
                cc = c * cot
                og = og_ref[m : m + ROWS, :]
                for n in range(0, tile, 128):
                    og = og + sw[:, n : n + 128]
                d_refs[k][width + m : width + m + ROWS, :] = cc.astype(bf16)
                og_ref[m : m + ROWS, :] = og

            return run

        return [piece(m) for m in range(0, width, ROWS)]

    def back_cosine(k):
        k = k % 4

        def piece(m):
            def run():
                d_refs[k][m : m + ROWS, :] = (
                    te_ref[m : m + ROWS, :] * c0_refs[k][m : m + ROWS, :]
                ).astype(bf16)

            return run

        return [piece(m) for m in range(0, width, ROWS)]

    def hidden_sum(k):
        k = k % 4

        def piece(m, n):
            def run():
                hidg_ref[m : m + MCH, n : n + NCH] += dot_nt(
                    rhs_refs[k][m : m + MCH, :], d_refs[k][width + n : width + n + NCH, :]
                )

            return run

        return [piece(m, n) for n in range(0, width, NCH) for m in range(0, width, MCH)]

    def cell_sum(k):
        k = k % 4

        def piece(m, n):
            def run():
                e = min(m + GM, cells + 16)
                g_ref[m:e, n : n + NCH] += dot_nt(
                    rhs_refs[k][oh1 + m : oh1 + e, :], d_refs[k][n : n + NCH, :]
                )

            return run

        return [piece(m, n) for n in range(0, 2 * width, NCH) for m in range(0, cells + 16, GM)]

    def weave(first, second):
        i = j = 0
        while i < len(first) or j < len(second):
            if j >= len(second) or (i < len(first) and i * len(second) <= j * len(first)):
                first[i]()
                i += 1
            else:
                second[j]()
                j += 1

    def at_tile(i):
        return pl.ds(pl.multiple_of(i * tile, tile), tile)

    def stage(u, i, count):
        weave(
            back_dot(u) + (second_dot(u + 1) if count > 1 else []),
            first_sine(u + 2) if count > 2 else [],
        )
        ahead = []
        if count > 3:
            encode(u + 3, at_tile(i + 3))
            ahead = first_dot(u + 3)
        late = second_sine(u + 1, at_tile(i + 1)) if count > 1 else []
        weave(ahead + hidden_sum(u), back_cosine(u) + late[: len(late) * SPLIT // 16])
        weave(cell_sum(u), late[len(late) * SPLIT // 16 :])

    for i in range(3):
        encode(i, at_tile(i))
    weave(first_dot(0), [])
    weave([], first_sine(0))
    weave(first_dot(1) + second_dot(0), [])
    weave([], first_sine(1))
    weave(first_dot(2), second_sine(0, at_tile(0)))

    def step(i, carry):
        for u in range(4):
            stage(u, 4 * i + u, 4)
        return carry

    lax.fori_loop(0, tiles // 4 - 1, step, 0)
    for u in range(4):
        stage(u, tiles - 4 + u, 4 - u)

    hidg_ref[...] = hidg_ref[...] * outw_ref[...]
    g_ref[:, width:] = g_ref[:, width:] * outw_ref[...]
    g = g_ref[0:cells, :]
    hi, lo = split2(g)
    fg = (dot_nt(hi, mapw_ref[...]) + dot_nt(lo, mapw_ref[...])).astype(bf16)
    fg_ref[...] = fg
    feat_t = feat_ref[...].astype(f32).T.astype(bf16)
    grad = dot(feat_t, hi) + dot(feat_t, lo)
    for k in range(4):
        grads_ref[9 + k] = grad[:, k * ch : (k + 1) * ch]
        r, c = k // 2 * ch, k % 2 * ch
        grads_ref[13 + k] = hidg_ref[r : r + ch, c : c + ch]
    for a in range(3):
        grad = dot_tn(x3_ref[a * cols : a * cols + cells, :], fg)
        for b in range(3):
            grads_ref[3 * a + b] = grad[b * ch : (b + 1) * ch, :]
    bias = jnp.sum(g, axis=0, keepdims=True)
    g0 = g[:, :width]
    ig0 = jnp.sum(lat_c * g0, axis=0, keepdims=True) + (2.0 / (lat_cells * SUB)) * g_ref[
        cells : cells + 1, :width
    ]
    ig1 = jnp.sum(lon_c * g0, axis=0, keepdims=True) + (2.0 / (lon_cells * SUB)) * g_ref[
        cells + 1 : cells + 2, :width
    ]
    ig2 = lev_c * bias[:, :width] + (2.0 / LEVELS) * g_ref[cells + 2 : cells + 3, :width]
    og = jnp.sum(og_ref[...].T, axis=0, keepdims=True)
    small_ref[...] = jnp.zeros_like(small_ref)
    small_ref[0:1, :] = bias
    small_ref[1:2, 0:width] = OMEGA * ig0
    small_ref[1:2, width:] = OMEGA * ig1
    small_ref[2:3, 0:width] = OMEGA * ig2
    small_ref[2:3, width:] = og


def run_main(queries, center, halo, weights, dims):
    conv_weight, map_weight, map_bias, input_weight, hidden_weight, output_weight = weights
    rows, cols, ch = center.shape
    cells = rows * cols
    width = input_weight.shape[1]
    f32 = jnp.float32
    bf16 = jnp.bfloat16
    vmem = pl.BlockSpec(memory_space=pltpu.VMEM)
    return pl.pallas_call(
        functools.partial(main_kernel, dims),
        out_shape=(
            jax.ShapeDtypeStruct((cells, ch), bf16),
            jax.ShapeDtypeStruct((17, ch, ch), f32),
            jax.ShapeDtypeStruct((8, 2 * width), f32),
        ),
        in_specs=[vmem] * 12,
        out_specs=(vmem,) * 3,
        scratch_shapes=[
            pltpu.VMEM((width, width), f32),
            pltpu.VMEM(((rows + 2) * cols, 3 * ch), bf16),
            pltpu.VMEM((cells, ch), bf16),
            pltpu.VMEM((width, 2 * cells + 128), bf16),
            pltpu.VMEM((width, width + 2 * cells), bf16),
            pltpu.VMEM((width, width), bf16),
            pltpu.VMEM((cells + 16, 2 * width), f32),
            pltpu.VMEM((width, 128), f32),
        ]
        + [pltpu.VMEM((width + 2 * cells + 128, TILE), bf16)] * 4
        + [pltpu.VMEM((width, TILE), f32)] * 4
        + [pltpu.VMEM((2 * width, TILE), bf16)] * 4
        + [pltpu.VMEM((width, TILE), f32)] * 3,
        compiler_params=pltpu.CompilerParams(vmem_limit_bytes=MAIN_MB << 20),
        name="queries",
    )(
        queries,
        center,
        *halo,
        conv_weight.reshape(3, 3 * ch, ch),
        map_weight,
        map_bias.reshape(1, -1),
        input_weight,
        hidden_weight[0],
        output_weight.reshape(1, -1),
    )


AROUND = ((-1, 0), (1, 0), (0, -1), (0, 1), (-1, -1), (-1, 1), (1, -1), (1, 1))


def remote(src, dst, send, recv, device):
    return pltpu.make_async_remote_copy(
        src_ref=src,
        dst_ref=dst,
        send_sem=send,
        recv_sem=recv,
        device_id=device,
        device_id_type=pl.DeviceIdType.MESH,
    )


def at_rim(da, db):
    lat_n = lax.axis_size("lat")
    lon_n = lax.axis_size("lon")
    lat = lax.rem(lax.axis_index("lat") + da + lat_n, lat_n)
    return (lat, lax.rem(lax.axis_index("lon") + db + lon_n, lon_n))


def meet(peers):
    barrier = pltpu.get_barrier_semaphore()
    for peer in peers:
        pl.semaphore_signal(barrier, inc=1, device_id=peer, device_id_type=pl.DeviceIdType.MESH)

    def wait():
        pl.semaphore_wait(barrier, len(peers))

    return wait


def rim_copies(flat_ref, cols, col_s, row_r, col_r, send, recv):
    cells = flat_ref.shape[0]
    first = flat_ref.at[pl.ds(0, cols)]
    last = flat_ref.at[pl.ds(cells - cols, cols)]
    return [
        remote(last, row_r.at[0], send.at[0], recv.at[0], at_rim(1, 0)),
        remote(first, row_r.at[1], send.at[1], recv.at[1], at_rim(-1, 0)),
        remote(col_s.at[0], col_r.at[0], send.at[2], recv.at[2], at_rim(0, 1)),
        remote(col_s.at[1], col_r.at[1], send.at[3], recv.at[3], at_rim(0, -1)),
        remote(last, row_r.at[2], send.at[4], recv.at[4], at_rim(1, 1)),
        remote(last, row_r.at[3], send.at[5], recv.at[5], at_rim(1, -1)),
        remote(first, row_r.at[4], send.at[6], recv.at[6], at_rim(-1, 1)),
        remote(first, row_r.at[5], send.at[7], recv.at[7], at_rim(-1, -1)),
    ]


def edge_columns(flat, rows, cols, col_s):
    tile = flat.astype(jnp.float32).reshape(rows, cols, flat.shape[1])
    col_s[0] = tile[:, cols - 1, :].astype(flat.dtype)
    col_s[1] = tile[:, 0, :].astype(flat.dtype)


def rim_values(cols, row_r, col_r):
    f32 = jnp.float32
    bf16 = jnp.bfloat16
    lat = lax.axis_index("lat")
    up = jnp.where(lat > 0, 1.0, 0.0).astype(f32)
    down = jnp.where(lat < lax.axis_size("lat") - 1, 1.0, 0.0).astype(f32)
    top = (row_r[0].astype(f32) * up).astype(bf16)
    bottom = (row_r[1].astype(f32) * down).astype(bf16)
    nw = row_r[2].astype(f32)[cols - 1 : cols] * up
    ne = row_r[3].astype(f32)[0:1] * up
    sw = row_r[4].astype(f32)[cols - 1 : cols] * down
    se = row_r[5].astype(f32)[0:1] * down
    left = jnp.concatenate([nw, col_r[0].astype(f32), sw], axis=0)
    right = jnp.concatenate([ne, col_r[1].astype(f32), se], axis=0)
    return top, bottom, left.astype(bf16), right.astype(bf16)


def front_kernel(
    grid_ref,
    cot_ref,
    owner_ref,
    tile_ref,
    out_ref,
    top_ref,
    bottom_ref,
    left_ref,
    right_ref,
    data,
    go,
    mid,
    turned,
    row_r,
    col_s,
    col_r,
    send,
    recv,
    hsem_s,
    hsem_r,
):
    lat = lax.axis_index("lat")
    lon = lax.axis_index("lon")
    lat_n, lon_n, words = out_ref.shape
    hits, group = cot_ref.shape
    cols = top_ref.shape[0]
    rows = tile_ref.shape[0] // cols

    def at_lon(d):
        return (lat, lax.rem(lon + d, lon_n))

    def at_lat(d):
        return (lax.rem(lat + d, lat_n), lon)

    peers = [at_lon(d) for d in range(1, lon_n)] + [at_lat(d) for d in range(1, lat_n)]
    wait = meet(peers + [at_rim(da, db) for da, db in AROUND])

    at = lax.broadcasted_iota(jnp.int32, (lat_n * lon_n, hits), 0)
    device = lax.rem(at, lat_n) * lon_n + lax.div(at, lat_n)
    pick = jnp.where(device == owner_ref[...], 1.0, 0.0).astype(jnp.float32)
    for k in range(3):
        data[:, k * group : (k + 1) * group] = grid_ref[k].astype(jnp.float32)
    data[:, 3 * group :] = cot_ref[...]
    picked = jnp.dot(
        pick, data[...], precision=lax.Precision.HIGHEST, preferred_element_type=jnp.float32
    )
    go[...] = picked.reshape(lon_n, lat_n, words)
    mid[lon] = go[lon]
    edge_columns(tile_ref[...], rows, cols, col_s)
    wait()
    one = []
    for d in range(1, lon_n):
        peer = lax.rem(lon + d, lon_n)
        one.append(remote(go.at[peer], mid.at[lon], send.at[d], recv.at[d], at_lon(d)))
        one[-1].start()
    rim = rim_copies(tile_ref, cols, col_s, row_r, col_r, hsem_s, hsem_r)
    for item in rim:
        item.start()
    for item in one:
        item.wait()
    for k in range(lat_n):
        turned[k] = mid[:, k, :]
    out_ref[lat] = turned[lat]
    two = []
    for d in range(1, lat_n):
        peer = lax.rem(lat + d, lat_n)
        two.append(
            remote(
                turned.at[peer],
                out_ref.at[lat],
                send.at[lon_n + d],
                recv.at[lon_n + d],
                at_lat(d),
            )
        )
        two[-1].start()
    for item in rim:
        item.wait()
    top, bottom, left, right = rim_values(cols, row_r, col_r)
    top_ref[...] = top
    bottom_ref[...] = bottom
    left_ref[...] = left
    right_ref[...] = right
    for item in two:
        item.wait()


def run_front(grid, cot, owner, tile, lat_n, lon_n):
    rows, cols, ch = tile.shape
    hits, group = cot.shape
    words = 4 * group
    f32 = jnp.float32
    bf16 = jnp.bfloat16
    dma = pltpu.SemaphoreType.DMA
    vmem = pl.BlockSpec(memory_space=pltpu.VMEM)
    return pl.pallas_call(
        front_kernel,
        out_shape=(
            jax.ShapeDtypeStruct((lat_n, lon_n, words), f32),
            jax.ShapeDtypeStruct((cols, ch), bf16),
            jax.ShapeDtypeStruct((cols, ch), bf16),
            jax.ShapeDtypeStruct((rows + 2, ch), bf16),
            jax.ShapeDtypeStruct((rows + 2, ch), bf16),
        ),
        in_specs=[vmem] * 4,
        out_specs=(vmem,) * 5,
        scratch_shapes=[
            pltpu.VMEM((hits, words), f32),
            pltpu.VMEM((lon_n, lat_n, words), f32),
            pltpu.VMEM((lon_n, lat_n, words), f32),
            pltpu.VMEM((lat_n, lon_n, words), f32),
            pltpu.VMEM((6, cols, ch), bf16),
            pltpu.VMEM((2, rows, ch), bf16),
            pltpu.VMEM((2, rows, ch), bf16),
            dma((lon_n + lat_n,)),
            dma((lon_n + lat_n,)),
            dma((8,)),
            dma((8,)),
        ],
        compiler_params=pltpu.CompilerParams(
            vmem_limit_bytes=16 << 20, collective_id=2, has_side_effects=True
        ),
        name="front",
    )(grid, cot, owner.reshape(1, hits), tile.reshape(rows * cols, ch))


def finish_kernel(
    sizes,
    chunks,
    scale,
    fg_ref,
    convw_ref,
    wg_ref,
    small_ref,
    latent_ref,
    half,
    other,
    total_ref,
    send1,
    recv1,
    acc1,
    send2,
    recv2,
    acc2,
    send3,
    recv3,
    slots4,
    pair_s,
    x_s,
    y_s,
    z_s,
    row_r,
    col_s,
    col_r,
    sem_s,
    sem_r,
    ssem_s,
    ssem_r,
    hsem_s,
    hsem_r,
):
    nx, ny, nz = sizes
    bf16 = jnp.bfloat16
    f32 = jnp.float32
    lat = lax.axis_index("lat")
    lon = lax.axis_index("lon")
    z, c = lax.div(lat, 2), lax.rem(lat, 2)
    x, y = lax.div(lon, ny), lax.rem(lon, ny)
    blocks, rows, lanes = half.shape
    quarter = rows // nx
    final = quarter // ny

    def at_pair():
        return (lat + 1 - 2 * c, lon)

    def at_x(d):
        return (lat, lax.rem(x + d, nx) * ny + y)

    def at_y(d):
        return (lat, x * ny + lax.rem(y + d, ny))

    def at_z(d):
        return (lax.rem(z + d, nz) * 2 + c, lon)

    axes = ((x, nx, at_x), (y, ny, at_y), (z, nz, at_z))
    orders = [[axes[(k + j) % 3] for j in range(3)] for k in range(len(chunks))]

    peers = [at_pair()]
    peers += [at_x(d) for d in range(1, nx)]
    peers += [at_y(d) for d in range(1, ny)]
    peers += [at_z(d) for d in range(1, nz)]
    peers += [at_rim(da, db) for da, db in AROUND]
    wait = meet(peers)

    tile_rows, cols, ch = latent_ref.shape
    cells = tile_rows * cols
    keep = pl.ds(pl.multiple_of(c * lanes, lanes), lanes)
    give = pl.ds(pl.multiple_of((1 - c) * lanes, lanes), lanes)

    def span(start, size):
        return pl.ds(pl.multiple_of(start, size), size)

    mine = [span(o[0][0] * quarter, quarter) for o in orders]
    ours = [span(o[1][0] * final, final) for o in orders]
    place = [span(o[0][0] * quarter + o[1][0] * final, final) for o in orders]

    def each(chunk, body):
        def one(b, carry):
            body(b)
            return carry

        lax.fori_loop(chunk[0], chunk[1], one, 0)

    def to_send1(b):
        send1[b] = wg_ref[b, :, give].astype(bf16)

    edge_columns(fg_ref[...], tile_rows, cols, col_s)
    pair_s[c] = small_ref[...]
    each(chunks[0], to_send1)
    wait()
    rim = rim_copies(fg_ref, cols, col_s, row_r, col_r, hsem_s, hsem_r)
    for item in rim:
        item.start()
    q1 = remote(pair_s.at[c], pair_s.at[c], ssem_s.at[0], ssem_r.at[0], at_pair())
    q1.start()

    def part(k):
        return pl.ds(chunks[k][0], chunks[k][1] - chunks[k][0])

    p1 = []
    for k in range(len(chunks)):
        if k > 0:
            each(chunks[k], to_send1)
        p1.append(
            remote(
                send1.at[part(k)], recv1.at[part(k)], sem_s.at[k, 0], sem_r.at[k, 0], at_pair()
            )
        )
        p1[-1].start()

    q1.wait()
    x_s[x] = pair_s[0] + pair_s[1]
    q2 = [remote(x_s.at[x], x_s.at[x], ssem_s.at[d], ssem_r.at[d], at_x(d)) for d in range(1, nx)]
    for item in q2:
        item.start()

    def add1(b):
        v = wg_ref[b, :, keep] + recv1[b].astype(f32)
        acc1[b] = v
        send2[b] = v.astype(bf16)

    p2 = []
    for k in range(len(chunks)):
        p1[k].wait()
        each(chunks[k], add1)
        group = []
        pos, count, at_first = orders[k][0]
        for d in range(1, count):
            target = lax.rem(pos + d, count)
            group.append(
                remote(
                    send2.at[part(k), pl.ds(pl.multiple_of(target * quarter, quarter), quarter), :],
                    recv2.at[d - 1, part(k)],
                    sem_s.at[k, d],
                    sem_r.at[k, d],
                    at_first(d),
                )
            )
            group[-1].start()
        p2.append(group)

    for item in q2:
        item.wait()
    y_s[y] = (x_s[0] + x_s[1]) + (x_s[2] + x_s[3])
    q3 = [
        remote(y_s.at[y], y_s.at[y], ssem_s.at[3 + d], ssem_r.at[3 + d], at_y(d))
        for d in range(1, ny)
    ]
    for item in q3:
        item.start()

    for item in rim:
        item.wait()
    top, bottom, left, right = rim_values(cols, row_r, col_r)
    x3 = shifted(fg_ref[...].reshape(tile_rows, cols, ch), top, bottom, left, right)
    acc = None
    for a in (-1, 0, 1):
        start = (1 - a) * cols
        for b in (-1, 0, 1):
            piece = dot_nt(x3[1 - b][start : start + cells], convw_ref[3 * (a + 1) + b + 1])
            acc = piece if acc is None else acc + piece
    latent_ref[...] = acc.reshape(tile_rows, cols, ch)

    def add2(k, b):
        v = acc1[b, mine[k], :]
        for d in range(nx - 1):
            v += recv2[d, b].astype(f32)
        acc2[b] = v
        send3[b] = v.astype(bf16)

    p3 = []
    for k in range(len(chunks)):
        for item in p2[k]:
            item.wait()
        each(chunks[k], functools.partial(add2, k))
        group = []
        pos, count, at_second = orders[k][1]
        for d in range(1, count):
            target = lax.rem(pos + d, count)
            group.append(
                remote(
                    send3.at[part(k), pl.ds(pl.multiple_of(target * final, final), final), :],
                    recv3.at[d - 1, part(k)],
                    sem_s.at[k, 3 + d],
                    sem_r.at[k, 3 + d],
                    at_second(d),
                )
            )
            group[-1].start()
        p3.append(group)

    for item in q3:
        item.wait()
    z_s[z] = (y_s[0] + y_s[1]) + (y_s[2] + y_s[3])
    q4 = [
        remote(z_s.at[z], z_s.at[z], ssem_s.at[6 + d], ssem_r.at[6 + d], at_z(d))
        for d in range(1, nz)
    ]
    for item in q4:
        item.start()

    def add3(k, b):
        v = acc2[b, ours[k], :]
        for d in range(ny - 1):
            v += recv3[d, b].astype(f32)
        slots4[orders[k][2][0], b] = v.astype(bf16)

    p4 = []
    for k in range(len(chunks)):
        for item in p3[k]:
            item.wait()
        each(chunks[k], functools.partial(add3, k))
        pos, count, at_third = orders[k][2]
        spot = slots4.at[pos, part(k)]
        group = [
            remote(spot, spot, sem_s.at[k, 6 + d], sem_r.at[k, 6 + d], at_third(d))
            for d in range(1, count)
        ]
        for item in group:
            item.start()
        p4.append(group)

    def add4(k, b):
        v = (slots4[0, b].astype(f32) + slots4[1, b].astype(f32)) + (
            slots4[2, b].astype(f32) + slots4[3, b].astype(f32)
        )
        half[b, place[k], :] = v.astype(bf16)

    p5 = []
    for k in range(len(chunks)):
        for item in p4[k]:
            item.wait()
        each(chunks[k], functools.partial(add4, k))
        spot = half.at[part(k), place[k], :]
        group = [
            remote(spot, spot, sem_s.at[k, 9 + d], sem_r.at[k, 9 + d], orders[k][1][2](d))
            for d in range(1, orders[k][1][1])
        ]
        for item in group:
            item.start()
        p5.append(group)

    for item in q4:
        item.wait()
    total_ref[...] = ((z_s[0] + z_s[1]) + (z_s[2] + z_s[3])) * scale

    p6 = []
    p7 = []
    for k in range(len(chunks)):
        for item in p5[k]:
            item.wait()
        spot = half.at[part(k), mine[k], :]
        group = [
            remote(spot, spot, sem_s.at[k, 12 + d], sem_r.at[k, 12 + d], orders[k][0][2](d))
            for d in range(1, orders[k][0][1])
        ]
        for item in group:
            item.start()
        p6.append(group)
        p7.append(
            remote(
                half.at[part(k), mine[k], :],
                other.at[part(k), mine[k], :],
                sem_s.at[k, 16],
                sem_r.at[k, 16],
                at_pair(),
            )
        )
        p7[-1].start()
    for k in range(len(chunks)):
        pos, count, _ = orders[k][0]
        for d in range(1, count):
            p6[k][d - 1].wait()
            rows_d = span(lax.rem(pos + count - d, count) * quarter, quarter)
            p7.append(
                remote(
                    half.at[part(k), rows_d, :],
                    other.at[part(k), rows_d, :],
                    sem_s.at[k, 16 + d],
                    sem_r.at[k, 16 + d],
                    at_pair(),
                )
            )
            p7[-1].start()
    for item in p7:
        item.wait()


def unpack_kernel(
    scale, half_ref, other_ref, small_ref, conv_ref, map_ref, hid_ref, bias_ref, in_ref, out_ref
):
    f32 = jnp.float32
    lanes = half_ref.shape[2]
    width = in_ref.shape[1]
    i = pl.program_id(0)
    core = lax.rem(lax.axis_index("lat"), 2)
    keep = pl.ds(pl.multiple_of(core * lanes, lanes), lanes)
    give = pl.ds(pl.multiple_of((1 - core) * lanes, lanes), lanes)
    conv_ref[0, :, keep] = half_ref[i].astype(f32) * scale
    conv_ref[0, :, give] = other_ref[i].astype(f32) * scale

    @pl.when(i < 4)
    def _():
        map_ref[:, keep] = half_ref[9 + i].astype(f32) * scale
        map_ref[:, give] = other_ref[9 + i].astype(f32) * scale
        hid_ref[:, keep] = half_ref[13 + i].astype(f32) * scale
        hid_ref[:, give] = other_ref[13 + i].astype(f32) * scale

    @pl.when(i == 0)
    def _():
        bias_ref[...] = small_ref[0:1, :]
        in_ref[0:1, :] = small_ref[1:2, 0:width]
        in_ref[1:2, :] = small_ref[1:2, width:]
        in_ref[2:3, :] = small_ref[2:3, 0:width]
        out_ref[...] = small_ref[2:3, width:]


def run_unpack(half, other, small, scale, width):
    f32 = jnp.float32
    _, ch, _ = half.shape

    def whole(shape):
        return pl.BlockSpec(shape, lambda i: (0,) * len(shape))

    return pl.pallas_call(
        functools.partial(unpack_kernel, scale),
        grid=(9,),
        out_shape=(
            jax.ShapeDtypeStruct((9, ch, ch), f32),
            jax.ShapeDtypeStruct((ch, 2 * width), f32),
            jax.ShapeDtypeStruct((width, width), f32),
            jax.ShapeDtypeStruct((1, 2 * width), f32),
            jax.ShapeDtypeStruct((3, width), f32),
            jax.ShapeDtypeStruct((1, width), f32),
        ),
        in_specs=[whole(half.shape), whole(other.shape), whole(small.shape)],
        out_specs=(
            pl.BlockSpec((1, ch, ch), lambda i: (i, 0, 0)),
            pl.BlockSpec((ch, ch), lambda i: (0, jnp.minimum(i, 3))),
            pl.BlockSpec((ch, ch), lambda i: (jnp.minimum(i, 3) // 2, jnp.minimum(i, 3) % 2)),
            whole((1, 2 * width)),
            whole((3, width)),
            whole((1, width)),
        ),
        compiler_params=pltpu.CompilerParams(vmem_limit_bytes=24 << 20),
        name="unpack",
    )(half, other, small)


def run_finish(fg, conv_weight, grads, small, tile_shape, scale, width):
    rows, cols, ch = tile_shape
    f32 = jnp.float32
    bf16 = jnp.bfloat16
    blocks, size, _ = grads.shape
    lanes = size // 2
    nx, ny, nz = 4, 4, 4
    dma = pltpu.SemaphoreType.DMA
    vmem = pl.BlockSpec(memory_space=pltpu.VMEM)
    return pl.pallas_call(
        functools.partial(finish_kernel, (nx, ny, nz), CHUNKS, scale),
        out_shape=(
            jax.ShapeDtypeStruct((rows, cols, ch), f32),
            jax.ShapeDtypeStruct((blocks, size, lanes), bf16),
            jax.ShapeDtypeStruct((blocks, size, lanes), bf16),
            jax.ShapeDtypeStruct(small.shape, f32),
        ),
        in_specs=[vmem] * 4,
        out_specs=(vmem,) * 4,
        scratch_shapes=[
            pltpu.VMEM((blocks, size, lanes), bf16),
            pltpu.VMEM((blocks, size, lanes), bf16),
            pltpu.VMEM((blocks, size, lanes), f32),
            pltpu.VMEM((blocks, size, lanes), bf16),
            pltpu.VMEM((nx - 1, blocks, size // nx, lanes), bf16),
            pltpu.VMEM((blocks, size // nx, lanes), f32),
            pltpu.VMEM((blocks, size // nx, lanes), bf16),
            pltpu.VMEM((ny - 1, blocks, size // nx // ny, lanes), bf16),
            pltpu.VMEM((nz, blocks, size // nx // ny, lanes), bf16),
            pltpu.VMEM((2,) + small.shape, f32),
            pltpu.VMEM((nx,) + small.shape, f32),
            pltpu.VMEM((ny,) + small.shape, f32),
            pltpu.VMEM((nz,) + small.shape, f32),
            pltpu.VMEM((6, cols, ch), bf16),
            pltpu.VMEM((2, rows, ch), bf16),
            pltpu.VMEM((2, rows, ch), bf16),
            dma((len(CHUNKS), 20)),
            dma((len(CHUNKS), 20)),
            dma((10,)),
            dma((10,)),
            dma((8,)),
            dma((8,)),
        ],
        compiler_params=pltpu.CompilerParams(
            vmem_limit_bytes=FINISH_MB << 20, collective_id=1, has_side_effects=True
        ),
        name="finish",
    )(fg, conv_weight, grads, small)


def on_device(
    latents,
    conv_weight,
    map_weight,
    map_bias,
    input_weight,
    hidden_weight,
    output_weight,
    hit_owner,
    serve_block,
    query_grid,
    cotangent,
):
    rows, cols, ch = latents.shape
    lat_parts = lax.axis_size("lat")
    lon_parts = lax.axis_size("lon")
    dev_count = lat_parts * lon_parts
    dims = (rows * lat_parts, cols * lon_parts)
    hits = hit_owner.shape[0]
    group = cotangent.shape[0] // hits
    f32 = jnp.float32

    arrived, *halo = run_front(
        query_grid.reshape(3, hits, group),
        cotangent.reshape(hits, group),
        hit_owner,
        latents,
        lat_parts,
        lon_parts,
    )
    arrived = arrived.reshape(dev_count, 4, group)
    block = jnp.maximum(serve_block[0], 0).astype(f32)[:, None]
    sub = arrived[:, 1]
    sub_r = jnp.floor((sub + 0.5) * (1.0 / SUB))
    zero = jnp.zeros_like(sub)
    queries = jnp.stack(
        [
            arrived[:, 0] + BLOCK * block,
            sub_r,
            sub - SUB * sub_r,
            arrived[:, 2],
            arrived[:, 3],
            zero,
            zero,
            zero,
        ]
    ).reshape(8, dev_count * group)

    weights = (conv_weight, map_weight, map_bias, input_weight, hidden_weight, output_weight)
    fg, grads, small = run_main(queries, latents, halo, weights, dims)
    scale = float(hits * group * dev_count) ** (-0.5)
    width = input_weight.shape[1]
    latent_grad, half, other, small = run_finish(
        fg, conv_weight, grads, small, latents.shape, scale, width
    )
    conv_grad, map_grad, hidden_grad, bias_grad, input_grad, output_grad = run_unpack(
        half, other, small, scale, width
    )
    return (
        latent_grad,
        conv_grad,
        map_grad,
        bias_grad[0],
        input_grad,
        hidden_grad[None],
        output_grad[0],
    )


def solution(mesh):
    placed = (
        P("lat", "lon", None),
        P(),
        P(),
        P(),
        P(),
        P(),
        P(),
        P(("lat", "lon")),
        P(("lat", "lon"), None),
        P(None, ("lat", "lon")),
        P(("lat", "lon")),
    )
    return jax.shard_map(
        on_device,
        mesh=mesh,
        in_specs=placed,
        out_specs=(P("lat", "lon", None), P(), P(), P(), P(), P(), P()),
        check_vma=False,
    )
```

```python
import functools
import math

import jax
import jax.numpy as jnp
import numpy as np
from jax import lax
from jax.experimental import pallas as pl
from jax.experimental.pallas import tpu as pltpu
from jax.sharding import PartitionSpec as P

BLOCK = 128
LEVELS = 37
SUB = 6
OMEGA = 30.0
INV_TURN = float(1.0 / (2.0 * math.pi))
TURN = float(2.0 * math.pi)
TILE = 512
ROWS = 32
MCH = 512
NCH = 256
GM = 272
SPLIT = 10
MAIN_MB = 36
FINISH_MB = 24
CHUNKS = ((0, 6), (6, 12), (12, 17))


def _fit():
    nodes = np.cos((2 * np.arange(400) + 1) * np.pi / 800)
    r = (nodes + 1) / 4
    found = []
    for odd, target in ((1, np.sin(np.pi * r)), (0, np.cos(np.pi * r))):
        basis = np.stack([r ** (2 * k + odd) for k in range(4)], 1)
        target = np.sqrt(2.0) * target
        weight = np.ones(len(r))
        for _ in range(60):
            root = np.sqrt(weight)
            c = np.linalg.lstsq(basis * root[:, None], target * root, rcond=None)[0]
            weight = weight * np.abs(basis @ c - target)
            weight = weight / weight.sum()
        found.append([float(np.float32(v)) for v in c])
    return found


SIN_C, COS_C = _fit()


def sincos_turns(t):
    r = t - jnp.round(t)
    z = r * r
    s = r * (SIN_C[0] + z * (SIN_C[1] + z * (SIN_C[2] + z * SIN_C[3])))
    c = COS_C[0] + z * (COS_C[1] + z * (COS_C[2] + z * COS_C[3]))
    return s * c, 1.0 - s * s


def dot(a, b):
    return jnp.dot(a, b, preferred_element_type=jnp.float32)


def dot_nt(a, b):
    return lax.dot_general(a, b, (((1,), (1,)), ((), ())), preferred_element_type=jnp.float32)


def dot_tn(a, b):
    return lax.dot_general(a, b, (((0,), (0,)), ((), ())), preferred_element_type=jnp.float32)


def split2(v):
    hi = v.astype(jnp.bfloat16)
    return hi, (v - hi.astype(jnp.float32)).astype(jnp.bfloat16)


def split3(v):
    hi = v.astype(jnp.bfloat16).astype(jnp.float32)
    mid = (v - hi).astype(jnp.bfloat16).astype(jnp.float32)
    return hi, mid, v - hi - mid


def shifted(center, top, bottom, left, right):
    rows, cols, ch = center.shape
    total = (rows + 2) * cols
    mid = jnp.concatenate([top, center.reshape(rows * cols, ch), bottom], axis=0)
    mid32 = mid.astype(jnp.float32)
    col = lax.broadcasted_iota(jnp.int32, (rows + 2, cols, ch), 1)
    low = pltpu.roll(mid32, 1, 0).reshape(rows + 2, cols, ch)
    high = pltpu.roll(mid32, total - 1, 0).reshape(rows + 2, cols, ch)
    low = jnp.where(col == 0, left.astype(jnp.float32)[:, None, :], low)
    high = jnp.where(col == cols - 1, right.astype(jnp.float32)[:, None, :], high)
    return (
        low.reshape(total, ch).astype(jnp.bfloat16),
        mid,
        high.reshape(total, ch).astype(jnp.bfloat16),
    )


def main_kernel(
    dims,
    q_ref,
    center_ref,
    top_ref,
    bottom_ref,
    left_ref,
    right_ref,
    convw_ref,
    mapw_ref,
    mapb_ref,
    inw_ref,
    hid_ref,
    outw_ref,
    fg_ref,
    grads_ref,
    small_ref,
    hidg_ref,
    x3_ref,
    feat_ref,
    tab0_ref,
    tab1_ref,
    hidw_ref,
    g_ref,
    og_ref,
    *pairs,
):
    lat_cells, lon_cells = dims
    rows, cols, ch = center_ref.shape
    cells = rows * cols
    width = inw_ref.shape[1]
    rhs_refs, c0_refs, d_refs = pairs[0:4], pairs[4:8], pairs[8:12]
    ta_ref, tc_ref, te_ref = pairs[12:]
    tile = rhs_refs[0].shape[1]
    tiles = q_ref.shape[1] // tile
    f32 = jnp.float32
    bf16 = jnp.bfloat16

    x3 = shifted(center_ref[...], top_ref[...], bottom_ref[...], left_ref[...], right_ref[...])
    for b in range(3):
        x3_ref[:, b * ch : (b + 1) * ch] = x3[b]
    acc = dot(x3_ref[0:cells, :], convw_ref[0])
    for a in (1, 2):
        acc += dot(x3_ref[a * cols : a * cols + cells, :], convw_ref[a])
    feat_ref[...] = acc.astype(bf16)

    shift = dot(feat_ref[...], mapw_ref[...]) + mapb_ref[...]
    cell = lax.broadcasted_iota(jnp.int32, (cells, width), 0)
    row_f = (cell // cols).astype(f32)
    col_f = (cell % cols).astype(f32)
    lat0 = (lax.axis_index("lat") * rows).astype(f32)
    lon0 = (lax.axis_index("lon") * cols).astype(f32)
    lat_c = ((lat0 + row_f) * SUB + 0.5) * (2.0 / (lat_cells * SUB)) - 1.0
    lon_c = ((lon0 + col_f) * SUB + 0.5) * (2.0 / (lon_cells * SUB)) - 1.0
    lev_c = 1.0 / LEVELS - 1.0
    linear = (
        lat_c * inw_ref[0:1, :] + lon_c * inw_ref[1:2, :] + lev_c * inw_ref[2:3, :]
    )
    turn0 = (OMEGA * linear + shift[:, :width]) * INV_TURN
    turn0 = turn0 - jnp.round(turn0)
    hi, lo = split2(turn0.T)
    tab0_ref[:, 0:cells] = hi
    tab0_ref[:, cells : 2 * cells] = lo
    turn1 = shift[:, width:] * INV_TURN
    turn1 = (turn1 - jnp.round(turn1)) * TURN
    hi, lo = split2(turn1.T)
    tab1_ref[:, width : width + cells] = hi
    tab1_ref[:, width + cells : width + 2 * cells] = lo
    tab1_ref[:, 0:width] = hid_ref[...].astype(f32).T.astype(bf16)
    steps = (
        2.0 * OMEGA * INV_TURN / (lat_cells * SUB),
        2.0 * OMEGA * INV_TURN / (lon_cells * SUB),
        2.0 * OMEGA * INV_TURN / LEVELS,
    )
    parts = [split3(inw_ref[c : c + 1, :] * steps[c]) for c in range(3)]
    ext_row = lax.broadcasted_iota(jnp.int32, (128, width), 0)
    ext = jnp.zeros((128, width), f32)
    for level in range(3):
        for c in range(3):
            ext = jnp.where(ext_row == level * 3 + c, parts[c][level], ext)
    tab0_ref[:, 2 * cells : 2 * cells + 128] = ext.T.astype(bf16)
    hidw_ref[...] = (hid_ref[...].astype(f32) * outw_ref[...]).astype(bf16)

    oh0 = width
    oh1 = width + cells
    ex0 = width + 2 * cells
    for rhs_ref in rhs_refs:
        rhs_ref[ex0:, :] = jnp.zeros((128, tile), bf16)
    g_ref[...] = jnp.zeros_like(g_ref)
    hidg_ref[...] = jnp.zeros_like(hidg_ref)
    og_ref[...] = jnp.zeros_like(og_ref)

    def encode(k, at):
        k = k % 4
        rhs_ref = rhs_refs[k]
        cell_q = q_ref[0:1, at].astype(bf16)
        one = jnp.ones((64, tile), bf16)
        zero = jnp.zeros((64, tile), bf16)
        for m in range(0, cells, 64):
            iota = (lax.broadcasted_iota(jnp.int32, (64, tile), 0) + m).astype(f32).astype(bf16)
            onehot = jnp.where(iota == cell_q, one, zero)
            rhs_ref[oh0 + m : oh0 + m + 64, :] = onehot
            rhs_ref[oh1 + m : oh1 + m + 64, :] = onehot
        r = lax.broadcasted_iota(jnp.int32, (16, tile), 0)
        ints = jnp.where(
            r % 3 == 0, q_ref[1:2, at], jnp.where(r % 3 == 1, q_ref[2:3, at], q_ref[3:4, at])
        )
        rhs_ref[ex0 : ex0 + 16, :] = jnp.where(r < 9, ints, 0.0).astype(bf16)

    def dots(out_ref, a_ref, b_ref, b_rows):
        def piece(m, n):
            def run():
                out_ref[m : m + MCH, n : n + NCH] = dot(
                    a_ref[m : m + MCH, :], b_ref[b_rows, n : n + NCH]
                )

            return run

        return [piece(m, n) for n in range(0, tile, NCH) for m in range(0, width, MCH)]

    def first_dot(k):
        k = k % 4

        return dots(ta_ref, tab0_ref, rhs_refs[k], slice(oh0, ex0 + 128))

    def second_dot(k):
        k = k % 4

        return dots(tc_ref, tab1_ref, rhs_refs[k], slice(0, ex0))

    def back_dot(k):
        k = k % 4

        return dots(te_ref, hidw_ref, d_refs[k], slice(width, 2 * width))

    def first_sine(k):
        k = k % 4

        def piece(m):
            def run():
                s, c = sincos_turns(ta_ref[m : m + ROWS, :])
                rhs_refs[k][m : m + ROWS, :] = s.astype(bf16)
                c0_refs[k][m : m + ROWS, :] = c

            return run

        return [piece(m) for m in range(0, width, ROWS)]

    def second_sine(k, at):
        k = k % 4

        def piece(m):
            def run():
                cot = q_ref[4:5, at]
                s, c = sincos_turns(tc_ref[m : m + ROWS, :] * INV_TURN)
                sw = s * cot
                cc = c * cot
                og = og_ref[m : m + ROWS, :]
                for n in range(0, tile, 128):
                    og = og + sw[:, n : n + 128]
                d_refs[k][width + m : width + m + ROWS, :] = cc.astype(bf16)
                og_ref[m : m + ROWS, :] = og

            return run

        return [piece(m) for m in range(0, width, ROWS)]

    def back_cosine(k):
        k = k % 4

        def piece(m):
            def run():
                d_refs[k][m : m + ROWS, :] = (
                    te_ref[m : m + ROWS, :] * c0_refs[k][m : m + ROWS, :]
                ).astype(bf16)

            return run

        return [piece(m) for m in range(0, width, ROWS)]

    def hidden_sum(k):
        k = k % 4

        def piece(m, n):
            def run():
                hidg_ref[m : m + MCH, n : n + NCH] += dot_nt(
                    rhs_refs[k][m : m + MCH, :], d_refs[k][width + n : width + n + NCH, :]
                )

            return run

        return [piece(m, n) for n in range(0, width, NCH) for m in range(0, width, MCH)]

    def cell_sum(k):
        k = k % 4

        def piece(m, n):
            def run():
                e = min(m + GM, cells + 16)
                g_ref[m:e, n : n + NCH] += dot_nt(
                    rhs_refs[k][oh1 + m : oh1 + e, :], d_refs[k][n : n + NCH, :]
                )

            return run

        return [piece(m, n) for n in range(0, 2 * width, NCH) for m in range(0, cells + 16, GM)]

    def weave(first, second):
        i = j = 0
        while i < len(first) or j < len(second):
            if j >= len(second) or (i < len(first) and i * len(second) <= j * len(first)):
                first[i]()
                i += 1
            else:
                second[j]()
                j += 1

    def at_tile(i):
        return pl.ds(pl.multiple_of(i * tile, tile), tile)

    def stage(u, i, count):
        weave(
            back_dot(u) + (second_dot(u + 1) if count > 1 else []),
            first_sine(u + 2) if count > 2 else [],
        )
        ahead = []
        if count > 3:
            encode(u + 3, at_tile(i + 3))
            ahead = first_dot(u + 3)
        late = second_sine(u + 1, at_tile(i + 1)) if count > 1 else []
        weave(ahead + hidden_sum(u), back_cosine(u) + late[: len(late) * SPLIT // 16])
        weave(cell_sum(u), late[len(late) * SPLIT // 16 :])

    for i in range(3):
        encode(i, at_tile(i))
    weave(first_dot(0), [])
    weave([], first_sine(0))
    weave(first_dot(1) + second_dot(0), [])
    weave([], first_sine(1))
    weave(first_dot(2), second_sine(0, at_tile(0)))

    def step(i, carry):
        for u in range(4):
            stage(u, 4 * i + u, 4)
        return carry

    lax.fori_loop(0, tiles // 4 - 1, step, 0)
    for u in range(4):
        stage(u, tiles - 4 + u, 4 - u)

    hidg_ref[...] = hidg_ref[...] * outw_ref[...]
    g_ref[:, width:] = g_ref[:, width:] * outw_ref[...]
    g = g_ref[0:cells, :]
    hi, lo = split2(g)
    fg = (dot_nt(hi, mapw_ref[...]) + dot_nt(lo, mapw_ref[...])).astype(bf16)
    fg_ref[...] = fg
    feat_t = feat_ref[...].astype(f32).T.astype(bf16)
    grad = dot(feat_t, hi) + dot(feat_t, lo)
    for k in range(4):
        grads_ref[9 + k] = grad[:, k * ch : (k + 1) * ch]
        r, c = k // 2 * ch, k % 2 * ch
        grads_ref[13 + k] = hidg_ref[r : r + ch, c : c + ch]
    for a in range(3):
        grad = dot_tn(x3_ref[a * cols : a * cols + cells, :], fg)
        for b in range(3):
            grads_ref[3 * a + b] = grad[b * ch : (b + 1) * ch, :]
    bias = jnp.sum(g, axis=0, keepdims=True)
    g0 = g[:, :width]
    ig0 = jnp.sum(lat_c * g0, axis=0, keepdims=True) + (2.0 / (lat_cells * SUB)) * g_ref[
        cells : cells + 1, :width
    ]
    ig1 = jnp.sum(lon_c * g0, axis=0, keepdims=True) + (2.0 / (lon_cells * SUB)) * g_ref[
        cells + 1 : cells + 2, :width
    ]
    ig2 = lev_c * bias[:, :width] + (2.0 / LEVELS) * g_ref[cells + 2 : cells + 3, :width]
    og = jnp.sum(og_ref[...].T, axis=0, keepdims=True)
    small_ref[...] = jnp.zeros_like(small_ref)
    small_ref[0:1, :] = bias
    small_ref[1:2, 0:width] = OMEGA * ig0
    small_ref[1:2, width:] = OMEGA * ig1
    small_ref[2:3, 0:width] = OMEGA * ig2
    small_ref[2:3, width:] = og


def run_main(queries, center, halo, weights, dims):
    conv_weight, map_weight, map_bias, input_weight, hidden_weight, output_weight = weights
    rows, cols, ch = center.shape
    cells = rows * cols
    width = input_weight.shape[1]
    f32 = jnp.float32
    bf16 = jnp.bfloat16
    vmem = pl.BlockSpec(memory_space=pltpu.VMEM)
    return pl.pallas_call(
        functools.partial(main_kernel, dims),
        out_shape=(
            jax.ShapeDtypeStruct((cells, ch), bf16),
            jax.ShapeDtypeStruct((17, ch, ch), f32),
            jax.ShapeDtypeStruct((8, 2 * width), f32),
        ),
        in_specs=[vmem] * 12,
        out_specs=(vmem,) * 3,
        scratch_shapes=[
            pltpu.VMEM((width, width), f32),
            pltpu.VMEM(((rows + 2) * cols, 3 * ch), bf16),
            pltpu.VMEM((cells, ch), bf16),
            pltpu.VMEM((width, 2 * cells + 128), bf16),
            pltpu.VMEM((width, width + 2 * cells), bf16),
            pltpu.VMEM((width, width), bf16),
            pltpu.VMEM((cells + 16, 2 * width), f32),
            pltpu.VMEM((width, 128), f32),
        ]
        + [pltpu.VMEM((width + 2 * cells + 128, TILE), bf16)] * 4
        + [pltpu.VMEM((width, TILE), f32)] * 4
        + [pltpu.VMEM((2 * width, TILE), bf16)] * 4
        + [pltpu.VMEM((width, TILE), f32)] * 3,
        compiler_params=pltpu.CompilerParams(vmem_limit_bytes=MAIN_MB << 20),
        name="queries",
    )(
        queries,
        center,
        *halo,
        conv_weight.reshape(3, 3 * ch, ch),
        map_weight,
        map_bias.reshape(1, -1),
        input_weight,
        hidden_weight[0],
        output_weight.reshape(1, -1),
    )


AROUND = ((-1, 0), (1, 0), (0, -1), (0, 1), (-1, -1), (-1, 1), (1, -1), (1, 1))


def remote(src, dst, send, recv, device):
    return pltpu.make_async_remote_copy(
        src_ref=src,
        dst_ref=dst,
        send_sem=send,
        recv_sem=recv,
        device_id=device,
        device_id_type=pl.DeviceIdType.MESH,
    )


def at_rim(da, db):
    lat_n = lax.axis_size("lat")
    lon_n = lax.axis_size("lon")
    lat = lax.rem(lax.axis_index("lat") + da + lat_n, lat_n)
    return (lat, lax.rem(lax.axis_index("lon") + db + lon_n, lon_n))


def meet(peers):
    barrier = pltpu.get_barrier_semaphore()
    for peer in peers:
        pl.semaphore_signal(barrier, inc=1, device_id=peer, device_id_type=pl.DeviceIdType.MESH)

    def wait():
        pl.semaphore_wait(barrier, len(peers))

    return wait


def rim_copies(flat_ref, cols, col_s, row_r, col_r, send, recv):
    cells = flat_ref.shape[0]
    first = flat_ref.at[pl.ds(0, cols)]
    last = flat_ref.at[pl.ds(cells - cols, cols)]
    return [
        remote(last, row_r.at[0], send.at[0], recv.at[0], at_rim(1, 0)),
        remote(first, row_r.at[1], send.at[1], recv.at[1], at_rim(-1, 0)),
        remote(col_s.at[0], col_r.at[0], send.at[2], recv.at[2], at_rim(0, 1)),
        remote(col_s.at[1], col_r.at[1], send.at[3], recv.at[3], at_rim(0, -1)),
        remote(last, row_r.at[2], send.at[4], recv.at[4], at_rim(1, 1)),
        remote(last, row_r.at[3], send.at[5], recv.at[5], at_rim(1, -1)),
        remote(first, row_r.at[4], send.at[6], recv.at[6], at_rim(-1, 1)),
        remote(first, row_r.at[5], send.at[7], recv.at[7], at_rim(-1, -1)),
    ]


def edge_columns(flat, rows, cols, col_s):
    tile = flat.astype(jnp.float32).reshape(rows, cols, flat.shape[1])
    col_s[0] = tile[:, cols - 1, :].astype(flat.dtype)
    col_s[1] = tile[:, 0, :].astype(flat.dtype)


def rim_values(cols, row_r, col_r):
    f32 = jnp.float32
    bf16 = jnp.bfloat16
    lat = lax.axis_index("lat")
    up = jnp.where(lat > 0, 1.0, 0.0).astype(f32)
    down = jnp.where(lat < lax.axis_size("lat") - 1, 1.0, 0.0).astype(f32)
    top = (row_r[0].astype(f32) * up).astype(bf16)
    bottom = (row_r[1].astype(f32) * down).astype(bf16)
    nw = row_r[2].astype(f32)[cols - 1 : cols] * up
    ne = row_r[3].astype(f32)[0:1] * up
    sw = row_r[4].astype(f32)[cols - 1 : cols] * down
    se = row_r[5].astype(f32)[0:1] * down
    left = jnp.concatenate([nw, col_r[0].astype(f32), sw], axis=0)
    right = jnp.concatenate([ne, col_r[1].astype(f32), se], axis=0)
    return top, bottom, left.astype(bf16), right.astype(bf16)


def front_kernel(
    grid_ref,
    cot_ref,
    owner_ref,
    tile_ref,
    out_ref,
    top_ref,
    bottom_ref,
    left_ref,
    right_ref,
    data,
    go,
    mid,
    turned,
    row_r,
    col_s,
    col_r,
    send,
    recv,
    hsem_s,
    hsem_r,
):
    lat = lax.axis_index("lat")
    lon = lax.axis_index("lon")
    lat_n, lon_n, words = out_ref.shape
    hits, group = cot_ref.shape
    cols = top_ref.shape[0]
    rows = tile_ref.shape[0] // cols

    def at_lon(d):
        return (lat, lax.rem(lon + d, lon_n))

    def at_lat(d):
        return (lax.rem(lat + d, lat_n), lon)

    peers = [at_lon(d) for d in range(1, lon_n)] + [at_lat(d) for d in range(1, lat_n)]
    wait = meet(peers + [at_rim(da, db) for da, db in AROUND])

    at = lax.broadcasted_iota(jnp.int32, (lat_n * lon_n, hits), 0)
    device = lax.rem(at, lat_n) * lon_n + lax.div(at, lat_n)
    pick = jnp.where(device == owner_ref[...], 1.0, 0.0).astype(jnp.float32)
    for k in range(3):
        data[:, k * group : (k + 1) * group] = grid_ref[k].astype(jnp.float32)
    data[:, 3 * group :] = cot_ref[...]
    picked = jnp.dot(
        pick, data[...], precision=lax.Precision.HIGHEST, preferred_element_type=jnp.float32
    )
    go[...] = picked.reshape(lon_n, lat_n, words)
    mid[lon] = go[lon]
    edge_columns(tile_ref[...], rows, cols, col_s)
    wait()
    one = []
    for d in range(1, lon_n):
        peer = lax.rem(lon + d, lon_n)
        one.append(remote(go.at[peer], mid.at[lon], send.at[d], recv.at[d], at_lon(d)))
        one[-1].start()
    rim = rim_copies(tile_ref, cols, col_s, row_r, col_r, hsem_s, hsem_r)
    for item in rim:
        item.start()
    for item in one:
        item.wait()
    for k in range(lat_n):
        turned[k] = mid[:, k, :]
    out_ref[lat] = turned[lat]
    two = []
    for d in range(1, lat_n):
        peer = lax.rem(lat + d, lat_n)
        two.append(
            remote(
                turned.at[peer],
                out_ref.at[lat],
                send.at[lon_n + d],
                recv.at[lon_n + d],
                at_lat(d),
            )
        )
        two[-1].start()
    for item in rim:
        item.wait()
    top, bottom, left, right = rim_values(cols, row_r, col_r)
    top_ref[...] = top
    bottom_ref[...] = bottom
    left_ref[...] = left
    right_ref[...] = right
    for item in two:
        item.wait()


def run_front(grid, cot, owner, tile, lat_n, lon_n):
    rows, cols, ch = tile.shape
    hits, group = cot.shape
    words = 4 * group
    f32 = jnp.float32
    bf16 = jnp.bfloat16
    dma = pltpu.SemaphoreType.DMA
    vmem = pl.BlockSpec(memory_space=pltpu.VMEM)
    return pl.pallas_call(
        front_kernel,
        out_shape=(
            jax.ShapeDtypeStruct((lat_n, lon_n, words), f32),
            jax.ShapeDtypeStruct((cols, ch), bf16),
            jax.ShapeDtypeStruct((cols, ch), bf16),
            jax.ShapeDtypeStruct((rows + 2, ch), bf16),
            jax.ShapeDtypeStruct((rows + 2, ch), bf16),
        ),
        in_specs=[vmem] * 4,
        out_specs=(vmem,) * 5,
        scratch_shapes=[
            pltpu.VMEM((hits, words), f32),
            pltpu.VMEM((lon_n, lat_n, words), f32),
            pltpu.VMEM((lon_n, lat_n, words), f32),
            pltpu.VMEM((lat_n, lon_n, words), f32),
            pltpu.VMEM((6, cols, ch), bf16),
            pltpu.VMEM((2, rows, ch), bf16),
            pltpu.VMEM((2, rows, ch), bf16),
            dma((lon_n + lat_n,)),
            dma((lon_n + lat_n,)),
            dma((8,)),
            dma((8,)),
        ],
        compiler_params=pltpu.CompilerParams(
            vmem_limit_bytes=16 << 20, collective_id=2, has_side_effects=True
        ),
        name="front",
    )(grid, cot, owner.reshape(1, hits), tile.reshape(rows * cols, ch))


def finish_kernel(
    sizes,
    chunks,
    scale,
    fg_ref,
    convw_ref,
    wg_ref,
    small_ref,
    latent_ref,
    half,
    other,
    total_ref,
    send1,
    recv1,
    acc1,
    send2,
    recv2,
    acc2,
    send3,
    recv3,
    slots4,
    pair_s,
    x_s,
    y_s,
    z_s,
    row_r,
    col_s,
    col_r,
    sem_s,
    sem_r,
    ssem_s,
    ssem_r,
    hsem_s,
    hsem_r,
):
    nx, ny, nz = sizes
    bf16 = jnp.bfloat16
    f32 = jnp.float32
    lat = lax.axis_index("lat")
    lon = lax.axis_index("lon")
    z, c = lax.div(lat, 2), lax.rem(lat, 2)
    x, y = lax.div(lon, ny), lax.rem(lon, ny)
    blocks, rows, lanes = half.shape
    quarter = rows // nx
    final = quarter // ny

    def at_pair():
        return (lat + 1 - 2 * c, lon)

    def at_x(d):
        return (lat, lax.rem(x + d, nx) * ny + y)

    def at_y(d):
        return (lat, x * ny + lax.rem(y + d, ny))

    def at_z(d):
        return (lax.rem(z + d, nz) * 2 + c, lon)

    axes = ((x, nx, at_x), (y, ny, at_y), (z, nz, at_z))
    orders = [[axes[(k + j) % 3] for j in range(3)] for k in range(len(chunks))]

    peers = [at_pair()]
    peers += [at_x(d) for d in range(1, nx)]
    peers += [at_y(d) for d in range(1, ny)]
    peers += [at_z(d) for d in range(1, nz)]
    peers += [at_rim(da, db) for da, db in AROUND]
    wait = meet(peers)

    tile_rows, cols, ch = latent_ref.shape
    cells = tile_rows * cols
    keep = pl.ds(pl.multiple_of(c * lanes, lanes), lanes)
    give = pl.ds(pl.multiple_of((1 - c) * lanes, lanes), lanes)

    def span(start, size):
        return pl.ds(pl.multiple_of(start, size), size)

    mine = [span(o[0][0] * quarter, quarter) for o in orders]
    ours = [span(o[1][0] * final, final) for o in orders]
    place = [span(o[0][0] * quarter + o[1][0] * final, final) for o in orders]

    def each(chunk, body):
        def one(b, carry):
            body(b)
            return carry

        lax.fori_loop(chunk[0], chunk[1], one, 0)

    def to_send1(b):
        send1[b] = wg_ref[b, :, give].astype(bf16)

    edge_columns(fg_ref[...], tile_rows, cols, col_s)
    pair_s[c] = small_ref[...]
    each(chunks[0], to_send1)
    wait()
    rim = rim_copies(fg_ref, cols, col_s, row_r, col_r, hsem_s, hsem_r)
    for item in rim:
        item.start()
    q1 = remote(pair_s.at[c], pair_s.at[c], ssem_s.at[0], ssem_r.at[0], at_pair())
    q1.start()

    def part(k):
        return pl.ds(chunks[k][0], chunks[k][1] - chunks[k][0])

    p1 = []
    for k in range(len(chunks)):
        if k > 0:
            each(chunks[k], to_send1)
        p1.append(
            remote(
                send1.at[part(k)], recv1.at[part(k)], sem_s.at[k, 0], sem_r.at[k, 0], at_pair()
            )
        )
        p1[-1].start()

    q1.wait()
    x_s[x] = pair_s[0] + pair_s[1]
    q2 = [remote(x_s.at[x], x_s.at[x], ssem_s.at[d], ssem_r.at[d], at_x(d)) for d in range(1, nx)]
    for item in q2:
        item.start()

    def add1(b):
        v = wg_ref[b, :, keep] + recv1[b].astype(f32)
        acc1[b] = v
        send2[b] = v.astype(bf16)

    p2 = []
    for k in range(len(chunks)):
        p1[k].wait()
        each(chunks[k], add1)
        group = []
        pos, count, at_first = orders[k][0]
        for d in range(1, count):
            target = lax.rem(pos + d, count)
            group.append(
                remote(
                    send2.at[part(k), pl.ds(pl.multiple_of(target * quarter, quarter), quarter), :],
                    recv2.at[d - 1, part(k)],
                    sem_s.at[k, d],
                    sem_r.at[k, d],
                    at_first(d),
                )
            )
            group[-1].start()
        p2.append(group)

    for item in q2:
        item.wait()
    y_s[y] = (x_s[0] + x_s[1]) + (x_s[2] + x_s[3])
    q3 = [
        remote(y_s.at[y], y_s.at[y], ssem_s.at[3 + d], ssem_r.at[3 + d], at_y(d))
        for d in range(1, ny)
    ]
    for item in q3:
        item.start()

    for item in rim:
        item.wait()
    top, bottom, left, right = rim_values(cols, row_r, col_r)
    x3 = shifted(fg_ref[...].reshape(tile_rows, cols, ch), top, bottom, left, right)
    acc = None
    for a in (-1, 0, 1):
        start = (1 - a) * cols
        for b in (-1, 0, 1):
            piece = dot_nt(x3[1 - b][start : start + cells], convw_ref[3 * (a + 1) + b + 1])
            acc = piece if acc is None else acc + piece
    latent_ref[...] = acc.reshape(tile_rows, cols, ch)

    def add2(k, b):
        v = acc1[b, mine[k], :]
        for d in range(nx - 1):
            v += recv2[d, b].astype(f32)
        acc2[b] = v
        send3[b] = v.astype(bf16)

    p3 = []
    for k in range(len(chunks)):
        for item in p2[k]:
            item.wait()
        each(chunks[k], functools.partial(add2, k))
        group = []
        pos, count, at_second = orders[k][1]
        for d in range(1, count):
            target = lax.rem(pos + d, count)
            group.append(
                remote(
                    send3.at[part(k), pl.ds(pl.multiple_of(target * final, final), final), :],
                    recv3.at[d - 1, part(k)],
                    sem_s.at[k, 3 + d],
                    sem_r.at[k, 3 + d],
                    at_second(d),
                )
            )
            group[-1].start()
        p3.append(group)

    for item in q3:
        item.wait()
    z_s[z] = (y_s[0] + y_s[1]) + (y_s[2] + y_s[3])
    q4 = [
        remote(z_s.at[z], z_s.at[z], ssem_s.at[6 + d], ssem_r.at[6 + d], at_z(d))
        for d in range(1, nz)
    ]
    for item in q4:
        item.start()

    def add3(k, b):
        v = acc2[b, ours[k], :]
        for d in range(ny - 1):
            v += recv3[d, b].astype(f32)
        slots4[orders[k][2][0], b] = v.astype(bf16)

    p4 = []
    for k in range(len(chunks)):
        for item in p3[k]:
            item.wait()
        each(chunks[k], functools.partial(add3, k))
        pos, count, at_third = orders[k][2]
        spot = slots4.at[pos, part(k)]
        group = [
            remote(spot, spot, sem_s.at[k, 6 + d], sem_r.at[k, 6 + d], at_third(d))
            for d in range(1, count)
        ]
        for item in group:
            item.start()
        p4.append(group)

    def add4(k, b):
        v = (slots4[0, b].astype(f32) + slots4[1, b].astype(f32)) + (
            slots4[2, b].astype(f32) + slots4[3, b].astype(f32)
        )
        half[b, place[k], :] = v.astype(bf16)

    p5 = []
    for k in range(len(chunks)):
        for item in p4[k]:
            item.wait()
        each(chunks[k], functools.partial(add4, k))
        spot = half.at[part(k), place[k], :]
        group = [
            remote(spot, spot, sem_s.at[k, 9 + d], sem_r.at[k, 9 + d], orders[k][1][2](d))
            for d in range(1, orders[k][1][1])
        ]
        for item in group:
            item.start()
        p5.append(group)

    for item in q4:
        item.wait()
    total_ref[...] = ((z_s[0] + z_s[1]) + (z_s[2] + z_s[3])) * scale

    p6 = []
    p7 = []
    for k in range(len(chunks)):
        for item in p5[k]:
            item.wait()
        spot = half.at[part(k), mine[k], :]
        group = [
            remote(spot, spot, sem_s.at[k, 12 + d], sem_r.at[k, 12 + d], orders[k][0][2](d))
            for d in range(1, orders[k][0][1])
        ]
        for item in group:
            item.start()
        p6.append(group)
        p7.append(
            remote(
                half.at[part(k), mine[k], :],
                other.at[part(k), mine[k], :],
                sem_s.at[k, 16],
                sem_r.at[k, 16],
                at_pair(),
            )
        )
        p7[-1].start()
    for k in range(len(chunks)):
        pos, count, _ = orders[k][0]
        for d in range(1, count):
            p6[k][d - 1].wait()
            rows_d = span(lax.rem(pos + count - d, count) * quarter, quarter)
            p7.append(
                remote(
                    half.at[part(k), rows_d, :],
                    other.at[part(k), rows_d, :],
                    sem_s.at[k, 16 + d],
                    sem_r.at[k, 16 + d],
                    at_pair(),
                )
            )
            p7[-1].start()
    for item in p7:
        item.wait()


def unpack_kernel(scale, half_ref, other_ref, small_ref, conv_ref, map_ref, hid_ref, bias_ref, in_ref, out_ref):
    f32 = jnp.float32
    blocks, rows, lanes = half_ref.shape
    width = in_ref.shape[1]

    def write(ref, lane0):
        def conv_out(b, carry):
            lane = pl.ds(pl.multiple_of(lane0, lanes), lanes)
            conv_ref[b, :, lane] = ref[b].astype(f32) * scale
            return carry

        lax.fori_loop(0, 9, conv_out, 0)
        for k in range(4):
            lane = pl.ds(pl.multiple_of(k * rows + lane0, lanes), lanes)
            map_ref[:, lane] = ref[9 + k].astype(f32) * scale
            lane = pl.ds(pl.multiple_of(k % 2 * rows + lane0, lanes), lanes)
            hid_ref[k // 2 * rows : (k // 2 + 1) * rows, lane] = ref[13 + k].astype(f32) * scale

    core = lax.rem(lax.axis_index("lat"), 2)
    write(half_ref, core * lanes)
    write(other_ref, (1 - core) * lanes)
    bias_ref[...] = small_ref[0:1, :]
    in_ref[0:1, :] = small_ref[1:2, 0:width]
    in_ref[1:2, :] = small_ref[1:2, width:]
    in_ref[2:3, :] = small_ref[2:3, 0:width]
    out_ref[...] = small_ref[2:3, width:]


def run_unpack(half, other, small, scale, width):
    f32 = jnp.float32
    _, ch, _ = half.shape
    vmem = pl.BlockSpec(memory_space=pltpu.VMEM)
    return pl.pallas_call(
        functools.partial(unpack_kernel, scale),
        out_shape=(
            jax.ShapeDtypeStruct((9, ch, ch), f32),
            jax.ShapeDtypeStruct((ch, 2 * width), f32),
            jax.ShapeDtypeStruct((width, width), f32),
            jax.ShapeDtypeStruct((1, 2 * width), f32),
            jax.ShapeDtypeStruct((3, width), f32),
            jax.ShapeDtypeStruct((1, width), f32),
        ),
        in_specs=[vmem] * 3,
        out_specs=(vmem,) * 6,
        compiler_params=pltpu.CompilerParams(vmem_limit_bytes=24 << 20),
        name="unpack",
    )(half, other, small)


def run_finish(fg, conv_weight, grads, small, tile_shape, scale, width):
    rows, cols, ch = tile_shape
    f32 = jnp.float32
    bf16 = jnp.bfloat16
    blocks, size, _ = grads.shape
    lanes = size // 2
    nx, ny, nz = 4, 4, 4
    dma = pltpu.SemaphoreType.DMA
    vmem = pl.BlockSpec(memory_space=pltpu.VMEM)
    return pl.pallas_call(
        functools.partial(finish_kernel, (nx, ny, nz), CHUNKS, scale),
        out_shape=(
            jax.ShapeDtypeStruct((rows, cols, ch), f32),
            jax.ShapeDtypeStruct((blocks, size, lanes), bf16),
            jax.ShapeDtypeStruct((blocks, size, lanes), bf16),
            jax.ShapeDtypeStruct(small.shape, f32),
        ),
        in_specs=[vmem] * 4,
        out_specs=(vmem,) * 4,
        scratch_shapes=[
            pltpu.VMEM((blocks, size, lanes), bf16),
            pltpu.VMEM((blocks, size, lanes), bf16),
            pltpu.VMEM((blocks, size, lanes), f32),
            pltpu.VMEM((blocks, size, lanes), bf16),
            pltpu.VMEM((nx - 1, blocks, size // nx, lanes), bf16),
            pltpu.VMEM((blocks, size // nx, lanes), f32),
            pltpu.VMEM((blocks, size // nx, lanes), bf16),
            pltpu.VMEM((ny - 1, blocks, size // nx // ny, lanes), bf16),
            pltpu.VMEM((nz, blocks, size // nx // ny, lanes), bf16),
            pltpu.VMEM((2,) + small.shape, f32),
            pltpu.VMEM((nx,) + small.shape, f32),
            pltpu.VMEM((ny,) + small.shape, f32),
            pltpu.VMEM((nz,) + small.shape, f32),
            pltpu.VMEM((6, cols, ch), bf16),
            pltpu.VMEM((2, rows, ch), bf16),
            pltpu.VMEM((2, rows, ch), bf16),
            dma((len(CHUNKS), 20)),
            dma((len(CHUNKS), 20)),
            dma((10,)),
            dma((10,)),
            dma((8,)),
            dma((8,)),
        ],
        compiler_params=pltpu.CompilerParams(
            vmem_limit_bytes=FINISH_MB << 20, collective_id=1, has_side_effects=True
        ),
        name="finish",
    )(fg, conv_weight, grads, small)


def on_device(
    latents,
    conv_weight,
    map_weight,
    map_bias,
    input_weight,
    hidden_weight,
    output_weight,
    hit_owner,
    serve_block,
    query_grid,
    cotangent,
):
    rows, cols, ch = latents.shape
    lat_parts = lax.axis_size("lat")
    lon_parts = lax.axis_size("lon")
    dev_count = lat_parts * lon_parts
    dims = (rows * lat_parts, cols * lon_parts)
    hits = hit_owner.shape[0]
    group = cotangent.shape[0] // hits
    f32 = jnp.float32

    arrived, *halo = run_front(
        query_grid.reshape(3, hits, group),
        cotangent.reshape(hits, group),
        hit_owner,
        latents,
        lat_parts,
        lon_parts,
    )
    arrived = arrived.reshape(dev_count, 4, group)
    block = jnp.maximum(serve_block[0], 0).astype(f32)[:, None]
    sub = arrived[:, 1]
    sub_r = jnp.floor((sub + 0.5) * (1.0 / SUB))
    zero = jnp.zeros_like(sub)
    queries = jnp.stack(
        [
            arrived[:, 0] + BLOCK * block,
            sub_r,
            sub - SUB * sub_r,
            arrived[:, 2],
            arrived[:, 3],
            zero,
            zero,
            zero,
        ]
    ).reshape(8, dev_count * group)

    weights = (conv_weight, map_weight, map_bias, input_weight, hidden_weight, output_weight)
    fg, grads, small = run_main(queries, latents, halo, weights, dims)
    scale = float(hits * group * dev_count) ** (-0.5)
    width = input_weight.shape[1]
    latent_grad, half, other, small = run_finish(
        fg, conv_weight, grads, small, latents.shape, scale, width
    )
    conv_grad, map_grad, hidden_grad, bias_grad, input_grad, output_grad = run_unpack(
        half, other, small, scale, width
    )
    return (
        latent_grad,
        conv_grad,
        map_grad,
        bias_grad[0],
        input_grad,
        hidden_grad[None],
        output_grad[0],
    )


def solution(mesh):
    placed = (
        P("lat", "lon", None),
        P(),
        P(),
        P(),
        P(),
        P(),
        P(),
        P(("lat", "lon")),
        P(("lat", "lon"), None),
        P(None, ("lat", "lon")),
        P(("lat", "lon")),
    )
    return jax.shard_map(
        on_device,
        mesh=mesh,
        in_specs=placed,
        out_specs=(P("lat", "lon", None), P(), P(), P(), P(), P(), P()),
        check_vma=False,
    )
```
